32 devices in a mesh: gx: 4 (over x, core), gy: 8 (over z, y).
Axes of the slice: x: 2, y: 2, z: 4, core: 2. Of those that a mesh axis runs over, the one named last changes fastest.
Arguments:
- displacement: float32 [6, 262144], P(None, ('gx', 'gy')), may hold values from -4 to 4
- velocity: float32 [6, 262144], P(None, ('gx', 'gy')), may hold values from -6 to 6
- ref_pos: float32 [3, 262144], P(None, ('gx', 'gy')), may hold values from -6 to 6
- normals: float32 [3, 262144], P(None, ('gx', 'gy')), may hold values from -4 to 4
- inv_mass: float32 [6, 262144], P(None, ('gx', 'gy')), may hold values from 0.5 to 2
- connectivity: int32 [4, 262144], P(None, ('gx', 'gy')), may hold values from 0 to 8191, as said below
- stiffness: bfloat16 [24, 24, 262144], P(None, None, ('gx', 'gy'))
- yield_force: float32 [262144], P(('gx', 'gy')), may hold values from 2 to 20
- shared_nodes: int32 [4, 4096], P(None, ('gx', 'gy')), may hold values from 0 to 8191, as said below
- block_slot: int32 [2048], P(('gx', 'gy')), may hold values from 0 to 63, as said below
- edge_slots: int32 [256], P(('gx', 'gy')), may hold values from 0 to 63, as said below
- tile_pairs: int32 [2, 4096], P(None, ('gx', 'gy')), may hold values from 0 to 95, as said below
- tile_count: int32 [32], P(('gx', 'gy')), may hold values from 0 to 128, as said below
- win_start: int32 [4096, 128], P(('gx', 'gy')), may hold values from 0 to 127
- win_len: int32 [4096, 128], P(('gx', 'gy')), may hold values from 1 to 128
Outputs:
- displacement_out: float32 [6, 262144], P(None, ('gx', 'gy'))
- velocity_out: float32 [6, 262144], P(None, ('gx', 'gy'))
The draws below stay inside these ranges and needn't reach their ends.
Inputs may be any that keep to these rules, and one draw needn't show every extreme that they name: `connectivity`: element e of a partition (e counted within the partition) has its corners among the partition's nodes 128 * (e // 128) to 128 * (e // 128) + 127. `shared_nodes`: the four rows of a partition list distinct local nodes, 128 a row, 512 distinct in all. `block_slot`: entries of one partition are distinct; box = entry // 2 is the receiving box. Every partition fills all 2 places of some boxes, and some boxes receive 2 blocks from every partition. `edge_slots`: places of a box's received blocks. `tile_pairs`: row 0 is a received place; row 1 is a received place or 64 + k for entry k of the neighbours' edge blocks. A box uses its first tile_count tiles; some box uses all 128 in every draw.
All inputs are finite; a program needn't handle non-finite values.
Results may differ from the reference program's by a relative error of at most 0.0003.
Values sent between devices are 32-bit elements; how exact they have to be, the bound alone decides.
No kernel may reach another device: no remote copies, remote signals or barrier semaphores. Data moves between devices by JAX's collectives and lax.ppermute only.
A program may use at most 128 MiB of HBM per device.

```python
import math
import jax
import jax.numpy as jnp
from jax import lax

BLK = 128
SBLK_DEV = 64
CAP = 2
EDGE = 8
SHARE = 128
STEPS = 2
NODE_DEV = 8192
NODES = 262144
ELEMS = 262144
TILES_DEV = 128
TILES = 4096
N_GX = 4
N_GY = 8


def routing_plan(key):
    devices = N_GX * N_GY
    slot_total = devices * CAP
    hot_number = max(1, SBLK_DEV // (4 * CAP))
    base_key = jax.random.fold_in(key, 7001)
    boxes_order = jax.random.permutation(jax.random.fold_in(base_key, 1), devices)
    hot_flag = jnp.zeros((devices,), jnp.int32).at[boxes_order[:hot_number]].set(1)
    slot_hot = jnp.repeat(hot_flag, CAP)
    source_keys = jax.random.split(jax.random.fold_in(base_key, 2), devices)

    def pick_slots(one_key):
        key_score, key_order = jax.random.split(one_key)
        slot_score = jax.random.randint(key_score, (slot_total,), 0, 1 << 20) + slot_hot * (1 << 21)
        slot_score = slot_score * slot_total + jnp.arange(slot_total, dtype=jnp.int32)
        chosen = jnp.argsort(-slot_score)[:SBLK_DEV]
        return jax.random.permutation(key_order, chosen).astype(jnp.int32)
    return jax.vmap(pick_slots)(source_keys)


def contact_plan(key):
    devices = N_GX * N_GY
    slot_total = devices * CAP
    routed = routing_plan(key)
    box_of = routed // CAP
    within = routed % CAP
    source = jnp.arange(devices, dtype=jnp.int32)[:, None]
    occupied = jnp.zeros((devices, slot_total), jnp.int32).at[box_of, source * CAP + within].set(1)
    live_count = jnp.sum(occupied, axis=1)
    plan_key = jax.random.fold_in(key, 7002)
    noise = jax.random.randint(jax.random.fold_in(plan_key, 1), (devices, slot_total), 0, 1 << 10)
    order_score = (occupied * (1 << 20) + noise) * slot_total + jnp.arange(slot_total, dtype=jnp.int32)[None, :]
    live_order = jnp.argsort(-order_score, axis=1).astype(jnp.int32)
    safe_count = jnp.maximum(live_count, 1)
    tile_index = jnp.arange(TILES_DEV, dtype=jnp.int32)
    slave_pos = tile_index[None, :] // 2 % safe_count[:, None]
    slaves = jnp.take_along_axis(live_order, slave_pos, axis=1)
    own_pick = jax.random.randint(jax.random.fold_in(plan_key, 2), (devices, TILES_DEV), 0, 1 << 20) % safe_count[:, None]
    own_master = jnp.take_along_axis(live_order, own_pick, axis=1)
    edge_master = slot_total + jax.random.randint(jax.random.fold_in(plan_key, 3), (devices, TILES_DEV), 0, 4 * EDGE)
    masters = jnp.where(tile_index[None, :] % 2 == 0, own_master, edge_master)
    counts = jnp.minimum(2 * live_count, TILES_DEV)
    edge_pos = jnp.arange(EDGE, dtype=jnp.int32)[None, :] % safe_count[:, None]
    edges = jnp.take_along_axis(live_order, edge_pos, axis=1)
    return (slaves.astype(jnp.int32), masters.astype(jnp.int32), counts.astype(jnp.int32), edges.astype(jnp.int32))


def draw_connectivity(key, part):
    local = jax.random.randint(jax.random.fold_in(key, 7005), (4, ELEMS), 0, BLK)
    local = local.at[0, 0].set(0)
    local = local.at[0, ELEMS - 1].set(BLK - 1)
    element = jnp.arange(ELEMS, dtype=jnp.int32) % NODE_DEV
    return (element // BLK * BLK)[None, :] + local.astype(jnp.int32)


def draw_block_slot(key, part):
    return routing_plan(key).reshape(-1)


def draw_tile_pairs(key, part):
    slaves, masters, counts, edges = contact_plan(key)
    stacked = jnp.stack([slaves, masters], axis=1)
    return jnp.transpose(stacked, (1, 0, 2)).reshape(2, -1)


def draw_tile_count(key, part):
    slaves, masters, counts, edges = contact_plan(key)
    return counts


def draw_edge_slots(key, part):
    slaves, masters, counts, edges = contact_plan(key)
    return edges.reshape(-1)


def draw_shared_nodes(key, part):
    devices = N_GX * N_GY
    node_keys = jax.random.split(jax.random.fold_in(key, 7003), devices)

    def pick_nodes(one_key):
        return jax.random.permutation(one_key, NODE_DEV)[:4 * SHARE].reshape(4, SHARE)
    lists = jax.vmap(pick_nodes)(node_keys)
    return jnp.transpose(lists, (1, 0, 2)).reshape(4, -1).astype(jnp.int32)


def draw_stiffness(key, part):
    noise = jax.random.normal(jax.random.fold_in(key, 7004), (24, 24, ELEMS), jnp.float32) * 0.25
    diagonal = 1.5 * jnp.eye(24, dtype=jnp.float32)[:, :, None]
    return (noise + diagonal).astype(jnp.bfloat16)


def plant(array, own_key, low, largest):
    place = [jax.random.randint(jax.random.fold_in(own_key, axis), (), 0, length) for axis, length in enumerate(array.shape)]
    widest = array.shape.index(max(array.shape))
    beside = place[:widest] + [(place[widest] + 1) % array.shape[widest]] + place[widest + 1:]
    return array.at[tuple(place)].set(low).at[tuple(beside)].set(largest)


def shard_levels(own_key, extent, shards, smallest, largest):
    def one(axis_at, blocks):
        draws = jax.random.uniform(jax.random.fold_in(jax.random.fold_in(own_key, 6), axis_at), (blocks,), jnp.float32, smallest / len(shards), largest / len(shards))
        return jnp.repeat(jnp.exp(draws), extent[axis_at] // blocks).reshape((-1,) + (1,) * (len(extent) - axis_at - 1))

    level = one(*shards[0])
    for cut in shards[1:]:
        level = level * one(*cut)
    return level


def gaussian(key, dims, scale, most, cuts=(), held_as=jnp.bfloat16):
    gain = shard_levels(key, dims, cuts, -0.22, 0.18) if cuts else 1.0
    array = jax.random.normal(key, dims, jnp.float32) * scale * gain
    return jnp.minimum(jnp.maximum(array, -most), most).astype(held_as)


def setup_inputs(seed: int = 0) -> dict:
    key_list = jax.random.split(jax.random.key(seed), 16)
    displacement = gaussian(key_list[0], (6, NODES), 0.5, 4.0, ((1, 32),), jnp.float32)
    velocity = gaussian(key_list[1], (6, NODES), 1.0, 6.0, ((1, 32),), jnp.float32)
    ref_pos = gaussian(key_list[2], (3, NODES), 1.0, 6.0, ((1, 32),), jnp.float32)
    normals = gaussian(key_list[3], (3, NODES), 0.6, 4.0, ((1, 32),), jnp.float32)
    inv_mass = jnp.clip(jnp.exp(math.log(2.0) - 1.3862944 * jax.random.uniform(key_list[4], (6, NODES), jnp.float32) ** shard_levels(key_list[4], (6, NODES), ((1, 32),), -0.2, 0.2)), 0.5, 2.0)
    connectivity = draw_connectivity(jax.random.fold_in(key_list[15], 71), 0)
    stiffness = draw_stiffness(jax.random.fold_in(key_list[15], 71), 0)
    yield_force = jnp.clip(jnp.exp(math.log(20.0) - 2.3025851 * jax.random.uniform(key_list[7], (ELEMS,), jnp.float32) ** shard_levels(key_list[7], (ELEMS,), ((0, 32),), -0.2, 0.2)), 2.0, 20.0)
    shared_nodes = draw_shared_nodes(jax.random.fold_in(key_list[15], 71), 0)
    block_slot = draw_block_slot(jax.random.fold_in(key_list[15], 71), 0)
    edge_slots = draw_edge_slots(jax.random.fold_in(key_list[15], 71), 0)
    tile_pairs = draw_tile_pairs(jax.random.fold_in(key_list[15], 71), 0)
    tile_count = draw_tile_count(jax.random.fold_in(key_list[15], 71), 0)
    win_start = plant(jax.random.randint(key_list[13], (TILES, BLK), 0, BLK), jax.random.fold_in(key_list[13], 1), 0, BLK - 1).astype(jnp.int32)
    win_len = plant(jax.random.randint(key_list[14], (TILES, BLK), 1, BLK + 1), jax.random.fold_in(key_list[14], 1), 1, BLK).astype(jnp.int32)
    return dict(displacement=displacement, velocity=velocity, ref_pos=ref_pos, normals=normals, inv_mass=inv_mass, connectivity=connectivity, stiffness=stiffness, yield_force=yield_force, shared_nodes=shared_nodes, block_slot=block_slot, edge_slots=edge_slots, tile_pairs=tile_pairs, tile_count=tile_count, win_start=win_start, win_len=win_len)


TIME_STEP = 0.5
PENALTY = 32.0
THICKNESS = 0.2

def element_forces(displacement, connectivity, stiffness, yield_force):
    node_count = displacement.shape[1]
    gathered = displacement[:, connectivity]
    elem_dofs = gathered.reshape(24, -1)
    trial = lax.optimization_barrier(jnp.sum(stiffness.astype(jnp.float32) * elem_dofs[None, :, :], axis=1))
    squared = lax.optimization_barrier(jnp.sum(trial * trial, axis=0))
    factor = 1.0 / jnp.sqrt(1.0 + squared / (yield_force * yield_force))
    element_force = (trial * factor[None, :]).reshape(6, 4, -1)
    internal = jnp.zeros((6, node_count), jnp.float32)
    for corner in range(4):
        internal = internal.at[:, connectivity[corner]].add(element_force[:, corner])
    return internal

def tile_forces(own_blocks, extended, slaves, masters, starts, lengths, active):
    width = own_blocks.shape[2]
    slave_pos = own_blocks[0:3][:, slaves]
    master_pos = extended[0:3][:, masters]
    master_nrm = extended[3:6][:, masters]
    offset = lax.optimization_barrier(jnp.sum(master_pos * master_nrm, axis=0))
    gap_matrix = jnp.einsum('cti,ctj->tij', slave_pos, master_nrm, precision=lax.Precision.HIGHEST) - offset[:, None, :]
    column = jnp.arange(width, dtype=jnp.int32)
    inside = (column[None, None, :] - starts[:, :, None]) % width < lengths[:, :, None]
    inside = jnp.logical_and(inside, active[:, None, None])
    pressure = jnp.where(inside, jnp.maximum(THICKNESS - gap_matrix, 0.0), 0.0)
    return PENALTY / width * jnp.einsum('tij,ctj->cti', pressure, master_nrm, precision=lax.Precision.HIGHEST)

def fetch(blocks, owner, box_index, rows):
    source = rows // CAP
    slot_place = rows % CAP
    block_index = owner[source, box_index * CAP + slot_place]
    present = block_index >= 0
    global_index = source * SBLK_DEV + jnp.maximum(block_index, 0)
    block_data = jnp.where(present[None, :, None], blocks[:, global_index], 0.0)
    return (block_data, global_index, present)

def side_values(force_dev, lists_dev):
    return force_dev[:, lists_dev]

def place_sides(force_dev, lists_dev, incoming_dev):
    for side in range(4):
        force_dev = force_dev.at[:, lists_dev[side]].add(incoming_dev[:, side])
    return force_dev

def reference(displacement, velocity, ref_pos, normals, inv_mass, connectivity, stiffness, yield_force, shared_nodes, block_slot, edge_slots, tile_pairs, tile_count, win_start, win_len):
    devices = N_GX * N_GY
    slot_total = devices * CAP
    node_dev = SBLK_DEV * BLK
    device_ids = jnp.arange(devices, dtype=jnp.int32)
    owner = jnp.full((devices, slot_total), -1, jnp.int32)
    owner = owner.at[device_ids[:, None], block_slot.reshape(devices, SBLK_DEV)].set(jnp.arange(SBLK_DEV, dtype=jnp.int32)[None, :])
    all_rows = jnp.arange(slot_total, dtype=jnp.int32)
    for time_step in range(STEPS):

        def per_device(index):
            start = index * node_dev
            disp_dev = lax.dynamic_slice_in_dim(displacement, start, node_dev, 1)
            conn_dev = lax.dynamic_slice_in_dim(connectivity, start, node_dev, 1)
            stiff_dev = lax.dynamic_slice_in_dim(stiffness, start, node_dev, 2)
            yield_dev = lax.dynamic_slice_in_dim(yield_force, start, node_dev, 0)
            return element_forces(disp_dev, conn_dev, stiff_dev, yield_dev)
        internal = lax.map(per_device, device_ids)
        internal = jnp.transpose(internal, (1, 0, 2)).reshape(6, -1)
        positions = ref_pos + displacement[0:3]
        blocks = jnp.concatenate([positions, normals], axis=0).reshape(6, devices * SBLK_DEV, BLK)

        def per_box(running, box_index):
            box_row = box_index // N_GY
            box_col = box_index % N_GY
            own_blocks, own_index, own_present = fetch(blocks, owner, box_index, all_rows)
            pieces = [own_blocks]
            for row_step, col_step in ((-1, 0), (1, 0), (0, -1), (0, 1)):
                near_row = box_row + row_step
                near_col = box_col + col_step
                exists = (near_row >= 0) & (near_row < N_GX) & (near_col >= 0) & (near_col < N_GY)
                near_box = jnp.clip(near_row, 0, N_GX - 1) * N_GY + jnp.clip(near_col, 0, N_GY - 1)
                edge_list = lax.dynamic_slice_in_dim(edge_slots, near_box * EDGE, EDGE, 0)
                edge_data, unused_index, unused_present = fetch(blocks, owner, near_box, edge_list)
                pieces.append(jnp.where(exists, edge_data, 0.0))
            extended = jnp.concatenate(pieces, axis=1)
            tile_rows = lax.dynamic_slice_in_dim(tile_pairs, box_index * TILES_DEV, TILES_DEV, 1)
            starts = lax.dynamic_slice_in_dim(win_start, box_index * TILES_DEV, TILES_DEV, 0)
            lengths = lax.dynamic_slice_in_dim(win_len, box_index * TILES_DEV, TILES_DEV, 0)
            active = jnp.arange(TILES_DEV, dtype=jnp.int32) < tile_count[box_index]
            forces = tile_forces(own_blocks, extended, tile_rows[0], tile_rows[1], starts, lengths, active)
            box_force = jnp.zeros((3, slot_total, BLK), jnp.float32).at[:, tile_rows[0]].add(forces)
            box_force = jnp.where(own_present[None, :, None], box_force, 0.0)
            running = running.at[:, own_index].add(box_force)
            return (running, None)
        contact, unused = lax.scan(per_box, jnp.zeros((3, devices * SBLK_DEV, BLK), jnp.float32), device_ids)
        contact_nodes = contact.reshape(3, -1)
        nodal_force = jnp.concatenate([contact_nodes, jnp.zeros_like(contact_nodes)], axis=0) - internal
        force_grid = nodal_force.reshape(6, devices, node_dev)
        lists = shared_nodes.reshape(4, devices, SHARE)
        sides = jax.vmap(side_values, in_axes=(1, 1), out_axes=1)(force_grid, lists)
        grid = sides.reshape(6, N_GX, N_GY, 4, SHARE)
        from_west = jnp.pad(grid[:, :-1, :, 1], ((0, 0), (1, 0), (0, 0), (0, 0)))
        from_east = jnp.pad(grid[:, 1:, :, 0], ((0, 0), (0, 1), (0, 0), (0, 0)))
        from_south = jnp.pad(grid[:, :, :-1, 3], ((0, 0), (0, 0), (1, 0), (0, 0)))
        from_north = jnp.pad(grid[:, :, 1:, 2], ((0, 0), (0, 0), (0, 1), (0, 0)))
        incoming = jnp.stack([from_west, from_east, from_south, from_north], axis=3).reshape(6, devices, 4, SHARE)
        assembled = jax.vmap(place_sides, in_axes=(1, 1, 1), out_axes=1)(force_grid, lists, incoming).reshape(6, -1)
        velocity = velocity + TIME_STEP * inv_mass * assembled
        displacement = displacement + TIME_STEP * velocity
    return (displacement, velocity)
```

```python
import jax
import jax.numpy as jnp
from jax import lax
from jax.experimental import pallas as pl
from jax.experimental.pallas import tpu as pltpu
from jax.sharding import PartitionSpec as P

BLK = 128
CAP = 2
STEPS = 2
ROWS = 8
HALF = 4
EBLK = 8

TIME_STEP = 0.5
PENALTY = 32.0
THICKNESS = 0.2

AXES = ("gx", "gy")
F32 = jnp.float32
BF16 = jnp.bfloat16
VMEM = pltpu.VMEM
SMEM = pltpu.SMEM


def vspec():
    return pl.BlockSpec(memory_space=VMEM)


def sspec():
    return pl.BlockSpec(memory_space=SMEM)


def lane_gather(data, index):
    return jnp.take_along_axis(data, index, axis=1, mode="promise_in_bounds")


def split(x):
    high = x.astype(BF16).astype(F32)
    return high, x - high


def prep_kernel(slot_ref, disp_ref, pos_ref, nrm_ref, out_ref):
    places = out_ref.shape[0]
    blocks = slot_ref.shape[0]
    if places != blocks:
        out_ref[...] = jnp.zeros(out_ref.shape, F32)
    pad = jnp.zeros((ROWS - 6, BLK), F32)
    for k in range(blocks):
        lanes = slice(k * BLK, (k + 1) * BLK)
        position = pos_ref[:, lanes] + disp_ref[0:3, lanes]
        out_ref[slot_ref[k]] = jnp.concatenate([position, nrm_ref[:, lanes], pad], axis=0)


def prep(block_slot, displacement, ref_pos, normals, places):
    return pl.pallas_call(
        prep_kernel,
        out_shape=jax.ShapeDtypeStruct((places, ROWS, BLK), F32),
        in_specs=[sspec(), vspec(), vspec(), vspec()],
        out_specs=vspec(),
        name="prep",
    )(block_slot, displacement, ref_pos, normals)


def fold_rows(tiles, row):
    low4 = row < 4
    low2 = (row & 2) == 0
    low1 = (row & 1) == 0
    four = []
    for i in range(4):
        a, b = tiles[i], tiles[i + 4]
        four.append(jnp.where(low4, a, b) + pltpu.roll(jnp.where(low4, b, a), 4, 0))
    two = []
    for i in range(2):
        a, b = four[i], four[i + 2]
        two.append(jnp.where(low2, a + pltpu.roll(a, 6, 0), b + pltpu.roll(b, 2, 0)))
    a, b = two
    return jnp.where(low1, a + pltpu.roll(a, 7, 0), b + pltpu.roll(b, 1, 0))


def element_kernel(disp_ref, conn_ref, stiff_ref, yield_ref, out_ref):
    row = lax.broadcasted_iota(jnp.int32, (ROWS, BLK), 0)
    row48 = lax.broadcasted_iota(jnp.int32, (48, BLK), 0)
    node = lax.broadcasted_iota(jnp.int32, (BLK, BLK), 0)
    for k in range(out_ref.shape[0]):
        lanes = slice(k * BLK, (k + 1) * BLK)
        local = conn_ref[:, lanes] & (BLK - 1)
        index = jnp.concatenate([local, local], axis=0)
        dofs = []
        for t in range(3):
            first = jnp.broadcast_to(disp_ref[2 * t : 2 * t + 1, lanes], (4, BLK))
            second = jnp.broadcast_to(disp_ref[2 * t + 1 : 2 * t + 2, lanes], (4, BLK))
            dofs.append(lane_gather(jnp.concatenate([first, second], axis=0), index))
        trial = []
        for g in range(3):
            tiles = []
            for i in range(8 * g, 8 * g + 8):
                line = stiff_ref[i, :, lanes].astype(F32)
                tiles.append(line[0:8] * dofs[0] + line[8:16] * dofs[1] + line[16:24] * dofs[2])
            trial.append(fold_rows(tiles, row))
        squared = trial[0] * trial[0] + trial[1] * trial[1] + trial[2] * trial[2]
        squared = squared + pltpu.roll(squared, 4, 0)
        squared = squared + pltpu.roll(squared, 2, 0)
        squared = squared + pltpu.roll(squared, 1, 0)
        level = yield_ref[0, k : k + 1, :]
        factor = lax.rsqrt(1.0 + squared / (level * level))
        forces = jnp.concatenate([t * factor for t in trial], axis=0)
        high, low = split(forces)
        stacked = jnp.concatenate([high, low], axis=0)
        total = jnp.zeros((48, BLK), F32)
        for a in range(4):
            corner = jnp.where((row48 & 3) == a, stacked, 0.0).astype(BF16)
            picker = jnp.where(node == local[a : a + 1, :], 1.0, 0.0).astype(BF16)
            total = total + lax.dot_general(
                corner, picker, (((1,), (1,)), ((), ())), preferred_element_type=F32
            )
        total = total[0:24] + total[24:48]
        pieces = []
        for t in range(3):
            x = total[8 * t : 8 * t + 8]
            x = x + pltpu.roll(x, 7, 0)
            x = x + pltpu.roll(x, 6, 0)
            pieces += [x[0:1], x[4:5]]
        out_ref[k] = jnp.concatenate(pieces + [jnp.zeros((2, BLK), F32)], axis=0)


def element_forces(displacement, connectivity, stiffness, yield_force):
    nodes = displacement.shape[1]
    blocks = nodes // BLK
    wide = EBLK * BLK
    return pl.pallas_call(
        element_kernel,
        out_shape=jax.ShapeDtypeStruct((blocks, ROWS, BLK), F32),
        grid=(blocks // EBLK,),
        in_specs=[
            pl.BlockSpec((6, wide), lambda i: (0, i)),
            pl.BlockSpec((4, wide), lambda i: (0, i)),
            pl.BlockSpec((24, 24, wide), lambda i: (0, 0, i)),
            pl.BlockSpec((1, EBLK, BLK), lambda i: (i, 0, 0)),
        ],
        out_specs=pl.BlockSpec((EBLK, ROWS, BLK), lambda i: (i, 0, 0)),
        cost_estimate=pl.CostEstimate(
            flops=2 * 576 * nodes, transcendentals=nodes, bytes_accessed=2 * 576 * nodes
        ),
        name="element",
    )(displacement, connectivity, stiffness, yield_force.reshape(-1, EBLK, BLK))


def contact_kernel(
    count_ref, pairs_ref, valid_ref, *refs, places, edges, fresh
):
    if fresh:
        recv_ref = refs[0]
        edge_refs = refs[1:5]
        rest = refs[5:]
    else:
        recv_ref, pos_ref = refs[0:2]
        edge_refs = refs[2:6]
        edge_pos_refs = refs[6:10]
        rest = refs[10:]
    start_ref, length_ref, out_ref, slave_tab, master_tab, force_tab, total_ref = rest
    zero1 = jnp.zeros((1, BLK), F32)
    ones = jnp.ones((3, BLK), F32)
    zero10 = jnp.zeros((10, BLK), F32)

    def master_entry(where, position, normal):
        n_high, n_low = split(normal)
        product = position * normal
        offset = THICKNESS + (product[0:1] + product[1:2] + product[2:3])
        o_high, o_rest = split(offset)
        o_mid, o_low = split(o_rest)
        negative = jnp.concatenate([-n_high, -n_low], axis=0)
        master_tab[where] = jnp.concatenate(
            [negative, negative, o_high, o_mid, o_low, zero1], axis=0
        ).astype(BF16)
        force_tab[where] = jnp.concatenate([n_high, n_low, zero10], axis=0).astype(BF16)

    def own_entry(p, carry):
        tile = recv_ref[p]
        position = tile[0:3] if fresh else pos_ref[p][0:3]
        p_high, p_low = split(position)
        slave_tab[p] = jnp.concatenate(
            [p_high, p_high, p_low, p_low, ones, zero1], axis=0
        ).astype(BF16)
        master_entry(p, position, tile[3:6])
        total_ref[p] = jnp.zeros((16, BLK), F32)
        return carry

    lax.fori_loop(0, places, own_entry, 0, unroll=4)
    for side in range(4):
        valid = valid_ref[side] > 0
        for e in range(edges):
            tile = jnp.where(valid, edge_refs[side][e], 0.0)
            if fresh:
                position = tile[0:3]
            else:
                position = jnp.where(valid, edge_pos_refs[side][e], 0.0)[0:3]
            master_entry(places + side * edges + e, position, tile[3:6])

    facet = lax.broadcasted_iota(jnp.int32, (BLK, BLK), 0)
    count = count_ref[0]

    def one_tile(t, live):
        slave = pairs_ref[0, t]
        master = pairs_ref[1, t]
        depth = lax.dot_general(
            master_tab[master],
            slave_tab[slave],
            (((0,), (0,)), ((), ())),
            preferred_element_type=F32,
        )
        start = start_ref[pl.ds(t, 1), :]
        length = jnp.where(live, length_ref[pl.ds(t, 1), :], 0)
        inside = ((facet - start) & (BLK - 1)) < length
        pressure = jnp.where(inside, jnp.maximum(depth, 0.0), 0.0)
        high = pressure.astype(BF16)
        low = (pressure - high.astype(F32)).astype(BF16)
        rows = force_tab[master]
        force = jnp.dot(rows, high, preferred_element_type=F32) + jnp.dot(
            rows, low, preferred_element_type=F32
        )
        total_ref[slave] = total_ref[slave] + force

    unroll = 4

    def body(r, carry):
        for d in range(unroll):
            t = r * unroll + d
            one_tile(t, t < count)
        return carry

    lax.fori_loop(0, (count + unroll - 1) // unroll, body, 0)

    def finish(p, carry):
        tile = total_ref[p]
        out_ref[p] = (PENALTY / BLK) * jnp.concatenate([tile[0:3] + tile[3:6], zero1], axis=0)
        return carry

    lax.fori_loop(0, places, finish, 0, unroll=8)


def contact(count, pairs, valid, received, positions, edges, edge_positions, start, length):
    places = received.shape[0]
    edge_count = edges[0].shape[0]
    extended = places + 4 * edge_count
    fresh = positions is None
    arrays = [received] + ([] if fresh else [positions]) + list(edges)
    arrays += [] if fresh else list(edge_positions)
    arrays += [start, length]
    tiles = start.shape[0]

    def kernel(*refs):
        contact_kernel(*refs, places=places, edges=edge_count, fresh=fresh)

    return pl.pallas_call(
        kernel,
        out_shape=jax.ShapeDtypeStruct((places, HALF, BLK), F32),
        in_specs=[sspec()] * 3 + [vspec()] * len(arrays),
        out_specs=vspec(),
        scratch_shapes=[
            VMEM((places, 16, BLK), BF16),
            VMEM((extended, 16, BLK), BF16),
            VMEM((extended, 16, BLK), BF16),
            VMEM((places, 16, BLK), F32),
        ],
        cost_estimate=pl.CostEstimate(
            flops=tiles * BLK * BLK * 64, transcendentals=0, bytes_accessed=tiles * BLK * 8
        ),
        name="contact",
    )(count, pairs, valid, *arrays)


def inverse_kernel(valid_ref, list_ref, out_ref):
    blocks = out_ref.shape[0]
    block_id = lax.broadcasted_iota(jnp.int32, (blocks, BLK), 0)
    lane_id = lax.broadcasted_iota(jnp.int32, (BLK, BLK), 0)
    rank = (lax.broadcasted_iota(jnp.int32, (BLK, BLK), 1) + 1).astype(F32)
    code = jnp.full((blocks, BLK), -1, jnp.int32)
    for side in range(4):
        nodes = list_ref[side : side + 1, :]
        valid = valid_ref[side] > 0
        in_block = jnp.where(
            jnp.logical_and(block_id == nodes // BLK, valid), 1.0, 0.0
        ).astype(BF16)
        at_lane = jnp.where(lane_id == (nodes & (BLK - 1)), rank, 0.0).astype(BF16)
        found = lax.dot_general(
            in_block, at_lane, (((1,), (1,)), ((), ())), preferred_element_type=F32
        ).astype(jnp.int32)
        code = jnp.where(found > 0, found - 1 + side * BLK, code)
    out_ref[...] = code


def inverse(valid, lists, blocks):
    return pl.pallas_call(
        inverse_kernel,
        out_shape=jax.ShapeDtypeStruct((blocks, BLK), jnp.int32),
        in_specs=[sspec(), vspec()],
        out_specs=vspec(),
        name="inverse",
    )(valid, lists)


def force_kernel(slot_ref, back_ref, internal_ref, list_ref, force_ref, *side_refs):
    blocks = slot_ref.shape[0]
    pad = jnp.zeros((ROWS - HALF, BLK), F32)
    lanes = []
    owners = []
    for side in range(4):
        nodes = jnp.broadcast_to(list_ref[side : side + 1, :], (ROWS, BLK))
        lanes.append(nodes & (BLK - 1))
        owners.append(nodes // BLK)
    sums = [jnp.zeros((ROWS, BLK), F32) for _ in range(4)]
    for k in range(blocks):
        tile = jnp.concatenate([back_ref[slot_ref[k]], pad], axis=0) - internal_ref[k]
        force_ref[k] = tile
        for side in range(4):
            sums[side] = jnp.where(
                owners[side] == k, lane_gather(tile, lanes[side]), sums[side]
            )
    for side in range(4):
        side_refs[side][...] = sums[side]


def nodal_force(block_slot, returned, internal, lists):
    blocks = internal.shape[0]
    return pl.pallas_call(
        force_kernel,
        out_shape=[jax.ShapeDtypeStruct((blocks, ROWS, BLK), F32)]
        + [jax.ShapeDtypeStruct((ROWS, BLK), F32)] * 4,
        in_specs=[sspec(), vspec(), vspec(), vspec()],
        out_specs=[vspec()] * 5,
        name="force",
    )(block_slot, returned, internal, lists)


def update_kernel(
    slot_ref,
    force_ref,
    near0_ref,
    near1_ref,
    near2_ref,
    near3_ref,
    code_ref,
    mass_ref,
    vel_ref,
    disp_ref,
    pos_ref,
    vel_out,
    disp_out,
    *send_refs,
):
    blocks = force_ref.shape[0]
    near = [r[...] for r in (near0_ref, near1_ref, near2_ref, near3_ref)]
    if send_refs and send_refs[0].shape[0] != blocks:
        send_refs[0][...] = jnp.zeros(send_refs[0].shape, F32)
    zero1 = jnp.zeros((1, BLK), F32)
    for k in range(blocks):
        lanes = slice(k * BLK, (k + 1) * BLK)
        code = jnp.broadcast_to(code_ref[k : k + 1, :], (ROWS, BLK))
        index = code & (BLK - 1)
        extra = jnp.zeros((ROWS, BLK), F32)
        for side in range(4):
            inside = jnp.logical_and(code >= side * BLK, code < (side + 1) * BLK)
            extra = jnp.where(inside, lane_gather(near[side], index), extra)
        assembled = (force_ref[k] + extra)[0:6]
        vel = vel_ref[:, lanes] + TIME_STEP * mass_ref[:, lanes] * assembled
        disp = disp_ref[:, lanes] + TIME_STEP * vel
        vel_out[:, lanes] = vel
        disp_out[:, lanes] = disp
        if send_refs:
            send_refs[0][slot_ref[k]] = jnp.concatenate(
                [pos_ref[:, lanes] + disp[0:3], zero1], axis=0
            )


def update(block_slot, force, near, code, inv_mass, velocity, displacement, ref_pos, places):
    nodes = displacement.shape[1]
    out = [jax.ShapeDtypeStruct((6, nodes), F32)] * 2
    if places:
        out = out + [jax.ShapeDtypeStruct((places, HALF, BLK), F32)]
    return pl.pallas_call(
        update_kernel,
        out_shape=out,
        in_specs=[sspec()] + [vspec()] * 10,
        out_specs=[vspec()] * len(out),
        name="update",
    )(block_slot, force, *near, code, inv_mass, velocity, displacement, ref_pos)


def pair_lists(size):
    first = [(i, i ^ 1) for i in range(size)]
    second = [(i, (i + 1) % size if i % 2 else (i - 1) % size) for i in range(size)]
    return first, second


def swap(values, sizes):
    out = []
    for at, axis in enumerate(AXES):
        for stage, pairs in enumerate(pair_lists(sizes[at])):
            out.append(lax.ppermute(values[2 * at + stage], axis, pairs))
    return out


def body(
    displacement,
    velocity,
    ref_pos,
    normals,
    inv_mass,
    connectivity,
    stiffness,
    yield_force,
    shared_nodes,
    block_slot,
    edge_slots,
    tile_pairs,
    tile_count,
    win_start,
    win_len,
):
    sizes = [lax.axis_size(axis) for axis in AXES]
    if any(size % 2 for size in sizes):
        raise ValueError("odd axis")
    places = sizes[0] * sizes[1] * CAP
    blocks = displacement.shape[1] // BLK
    edge_count = edge_slots.shape[0]
    at = [lax.axis_index(axis) for axis in AXES]
    even = [1 - i % 2 for i in at]
    valid = []
    for i, size in zip(at, sizes):
        valid += [jnp.int32(1), jnp.where((i == 0) | (i == size - 1), 0, 1).astype(jnp.int32)]
    valid = jnp.stack(valid)
    lists = []
    for axis in range(2):
        low, high = shared_nodes[2 * axis], shared_nodes[2 * axis + 1]
        is_even = even[axis] == 1
        lists += [jnp.where(is_even, high, low), jnp.where(is_even, low, high)]
    lists = jnp.stack(lists)
    far = tile_pairs[1] - places
    side = far // edge_count
    flip = jnp.where(side < 2, even[0], even[1])
    masters = jnp.where(
        far < 0, tile_pairs[1], places + (side ^ flip) * edge_count + far % edge_count
    )
    pairs = jnp.stack([tile_pairs[0], masters])
    code = inverse(valid, lists, blocks)

    def exchange(blocks_out):
        return lax.all_to_all(blocks_out, AXES, split_axis=0, concat_axis=0, tiled=True)

    outgoing = prep(block_slot, displacement, ref_pos, normals, places)
    first = None
    for step in range(STEPS):
        received = exchange(outgoing)
        internal = element_forces(displacement, connectivity, stiffness, yield_force)
        rows = received[edge_slots]
        near = swap([rows] * 4, sizes)
        if step == 0:
            first = (received, near)
            box_force = contact(
                tile_count, pairs, valid, received, None, near, None, win_start, win_len
            )
        else:
            box_force = contact(
                tile_count, pairs, valid, first[0], received, first[1], near, win_start, win_len
            )
        returned = exchange(box_force)
        force, *sides = nodal_force(block_slot, returned, internal, lists)
        incoming = swap(sides, sizes)
        last = step == STEPS - 1
        out = update(
            block_slot,
            force,
            incoming,
            code,
            inv_mass,
            velocity,
            displacement,
            ref_pos,
            0 if last else places,
        )
        velocity, displacement = out[0:2]
        if not last:
            outgoing = out[2]
    return (displacement, velocity)


def solution(mesh):
    split_last = P(None, AXES)
    placed = (
        split_last,
        split_last,
        split_last,
        split_last,
        split_last,
        split_last,
        P(None, None, AXES),
        P(AXES),
        split_last,
        P(AXES),
        P(AXES),
        split_last,
        P(AXES),
        P(AXES, None),
        P(AXES, None),
    )
    return jax.shard_map(
        body,
        mesh=mesh,
        in_specs=placed,
        out_specs=(split_last, split_last),
        check_vma=False,
    )
```

```python
import jax
import jax.numpy as jnp
from jax import lax
from jax.experimental import pallas as pl
from jax.experimental.pallas import tpu as pltpu
from jax.sharding import PartitionSpec as P

BLK = 128
CAP = 2
STEPS = 2
ROWS = 8
HALF = 4
EBLK = 8
GROUP = 16

TIME_STEP = 0.5
PENALTY = 32.0
THICKNESS = 0.2

AXES = ("gx", "gy")
F32 = jnp.float32
BF16 = jnp.bfloat16
VMEM = pltpu.VMEM
SMEM = pltpu.SMEM


def vspec():
    return pl.BlockSpec(memory_space=VMEM)


def sspec():
    return pl.BlockSpec(memory_space=SMEM)


def lane_gather(data, index):
    return jnp.take_along_axis(data, index, axis=1, mode="promise_in_bounds")


def split(x):
    high = x.astype(BF16).astype(F32)
    return high, x - high


def prep_kernel(slot_ref, disp_ref, pos_ref, nrm_ref, out_ref):
    places = out_ref.shape[0]
    blocks = slot_ref.shape[0]
    if places != blocks:
        out_ref[...] = jnp.zeros(out_ref.shape, F32)
    pad = jnp.zeros((ROWS - 6, BLK), F32)
    for k in range(blocks):
        lanes = slice(k * BLK, (k + 1) * BLK)
        position = pos_ref[:, lanes] + disp_ref[0:3, lanes]
        out_ref[slot_ref[k]] = jnp.concatenate([position, nrm_ref[:, lanes], pad], axis=0)


def prep(block_slot, displacement, ref_pos, normals, places):
    return pl.pallas_call(
        prep_kernel,
        out_shape=jax.ShapeDtypeStruct((places, ROWS, BLK), F32),
        in_specs=[sspec(), vspec(), vspec(), vspec()],
        out_specs=vspec(),
        name="prep",
    )(block_slot, displacement, ref_pos, normals)


def fold_rows(tiles, row):
    low4 = row < 4
    low2 = (row & 2) == 0
    low1 = (row & 1) == 0
    four = []
    for i in range(4):
        a, b = tiles[i], tiles[i + 4]
        four.append(jnp.where(low4, a, b) + pltpu.roll(jnp.where(low4, b, a), 4, 0))
    two = []
    for i in range(2):
        a, b = four[i], four[i + 2]
        two.append(jnp.where(low2, a + pltpu.roll(a, 6, 0), b + pltpu.roll(b, 2, 0)))
    a, b = two
    return jnp.where(low1, a + pltpu.roll(a, 7, 0), b + pltpu.roll(b, 1, 0))


def element_kernel(disp_ref, conn_ref, stiff_ref, yield_ref, out_ref):
    row = lax.broadcasted_iota(jnp.int32, (ROWS, BLK), 0)
    row48 = lax.broadcasted_iota(jnp.int32, (48, BLK), 0)
    node = lax.broadcasted_iota(jnp.int32, (BLK, BLK), 0).astype(jnp.int16)
    unit = jnp.ones((), BF16)
    zero = jnp.zeros((), BF16)
    row48 = row48.astype(jnp.int16) & 3
    for k in range(out_ref.shape[0]):
        lanes = slice(k * BLK, (k + 1) * BLK)
        local = conn_ref[:, lanes] & (BLK - 1)
        index = jnp.concatenate([local, local], axis=0)
        dofs = []
        for t in range(3):
            first = jnp.broadcast_to(disp_ref[2 * t : 2 * t + 1, lanes], (4, BLK))
            second = jnp.broadcast_to(disp_ref[2 * t + 1 : 2 * t + 2, lanes], (4, BLK))
            dofs.append(lane_gather(jnp.concatenate([first, second], axis=0), index))
        trial = []
        for g in range(3):
            tiles = []
            for i in range(8 * g, 8 * g + 8):
                line = stiff_ref[i, :, lanes].astype(F32)
                tiles.append(line[0:8] * dofs[0] + line[8:16] * dofs[1] + line[16:24] * dofs[2])
            trial.append(fold_rows(tiles, row))
        squared = trial[0] * trial[0] + trial[1] * trial[1] + trial[2] * trial[2]
        squared = squared + pltpu.roll(squared, 4, 0)
        squared = squared + pltpu.roll(squared, 2, 0)
        squared = squared + pltpu.roll(squared, 1, 0)
        level = yield_ref[0, k : k + 1, :]
        factor = lax.rsqrt(1.0 + squared / (level * level))
        forces = jnp.concatenate([t * factor for t in trial], axis=0)
        high, low = split(forces)
        stacked = jnp.concatenate([high, low], axis=0).astype(BF16)
        small = local.astype(jnp.int16)
        total = jnp.zeros((48, BLK), F32)
        for a in range(4):
            corner = jnp.where(row48 == a, stacked, zero)
            picker = jnp.where(node == small[a : a + 1, :], unit, zero)
            total = total + lax.dot_general(
                corner, picker, (((1,), (1,)), ((), ())), preferred_element_type=F32
            )
        total = total[0:24] + total[24:48]
        pieces = []
        for t in range(3):
            x = total[8 * t : 8 * t + 8]
            x = x + pltpu.roll(x, 7, 0)
            x = x + pltpu.roll(x, 6, 0)
            pieces += [x[0:1], x[4:5]]
        out_ref[k] = jnp.concatenate(pieces + [jnp.zeros((2, BLK), F32)], axis=0)


def element_forces(displacement, connectivity, stiffness, yield_force, part=0, parts=1):
    nodes = displacement.shape[1]
    blocks = nodes // BLK // parts
    wide = EBLK * BLK
    steps = blocks // EBLK
    first = part * steps
    return pl.pallas_call(
        element_kernel,
        out_shape=jax.ShapeDtypeStruct((blocks, ROWS, BLK), F32),
        grid=(steps,),
        in_specs=[
            pl.BlockSpec((6, wide), lambda i: (0, i + first)),
            pl.BlockSpec((4, wide), lambda i: (0, i + first)),
            pl.BlockSpec((24, 24, wide), lambda i: (0, 0, i + first)),
            pl.BlockSpec((1, EBLK, BLK), lambda i: (i + first, 0, 0)),
        ],
        out_specs=pl.BlockSpec((EBLK, ROWS, BLK), lambda i: (i, 0, 0)),
        cost_estimate=pl.CostEstimate(
            flops=2 * 576 * nodes, transcendentals=nodes, bytes_accessed=2 * 576 * nodes
        ),
        name="element",
    )(displacement, connectivity, stiffness, yield_force.reshape(-1, EBLK, BLK))


def plan_kernel(count_ref, pairs_ref, even_ref, plan_ref, *, places, edges):
    for row, value in enumerate((0, 0, 0, 0, 0, places)):
        plan_ref[row, 0] = value

    def sort(t, numbers):
        own, far = numbers
        slave = pairs_ref[0, t]
        master = pairs_ref[1, t]
        is_own = master < places
        entry = jnp.maximum(master - places, 0)
        side = entry // edges
        flip = jnp.where(side < 2, even_ref[0], even_ref[1])
        moved = places + (side ^ flip) * edges + entry % edges

        @pl.when(is_own)
        def _():
            plan_ref[0, own] = t
            plan_ref[1, own] = slave
            plan_ref[2, own] = master

        @pl.when(jnp.logical_not(is_own))
        def _():
            plan_ref[3, far] = t
            plan_ref[4, far] = slave
            plan_ref[5, far] = moved

        return own + is_own.astype(jnp.int32), far + 1 - is_own.astype(jnp.int32)

    own, far = lax.fori_loop(0, count_ref[0], sort, (jnp.int32(0), jnp.int32(0)))
    plan_ref[6, 0] = own
    plan_ref[7, 0] = far


def plan_tiles(tile_count, tile_pairs, even, places, edges):
    def kernel(*refs):
        plan_kernel(*refs, places=places, edges=edges)

    return pl.pallas_call(
        kernel,
        out_shape=jax.ShapeDtypeStruct((8, tile_pairs.shape[1]), jnp.int32),
        in_specs=[sspec()] * 3,
        out_specs=sspec(),
        name="plan",
    )(tile_count, tile_pairs, even)


def master_entry(where, position, normal, master_tab, force_tab):
    zero1 = jnp.zeros((1, BLK), F32)
    zero2 = jnp.zeros((2, BLK), F32)
    n_high, n_low = split(normal)
    product = position * normal
    offset = THICKNESS + (product[0:1] + product[1:2] + product[2:3])
    o_high, o_rest = split(offset)
    o_mid, o_low = split(o_rest)
    negative = jnp.concatenate([-n_high, -n_low], axis=0)
    master_tab[where] = jnp.concatenate(
        [negative, negative, o_high, o_mid, o_low, zero1], axis=0
    ).astype(BF16)
    lines = [n_high, n_low, zero2]
    force_tab[where] = jnp.concatenate(lines + lines, axis=0).astype(BF16)


def run_tiles(
    plan_ref, row, number, base, start_ref, length_ref, slave_tab, master_tab, force_tab,
    total_ref, depth_ref,
):
    facet = lax.broadcasted_iota(jnp.int32, (BLK, 2 * BLK), 0).astype(jnp.int16)
    upper = lax.broadcasted_iota(jnp.int32, (16, BLK), 0) < 8
    blank = jnp.zeros((16, BLK), BF16)
    small = jnp.int16
    last = jnp.maximum(number - 1, 0)

    def at(group, d):
        i = group * GROUP + d
        return jnp.clip(i, 0, last), jnp.logical_and(i >= 0, i < number)

    def body(r, carry):
        forces = []
        for d in range(0, GROUP, 2):
            starts, lengths, rows = [], [], []
            for e in range(2):
                i, live = at(r - 1, d + e)
                t = plan_ref[row, i]
                starts.append(start_ref[pl.ds(t, 1), :])
                lengths.append(jnp.where(live, length_ref[pl.ds(t, 1), :], 0))
                rows.append(force_tab[plan_ref[row + 2, i] - base])
            start = jnp.concatenate(starts, axis=1).astype(small)
            length = jnp.concatenate(lengths, axis=1).astype(small)
            inside = ((facet - start) & (BLK - 1)) < length
            pressure = jnp.maximum(depth_ref[d // 2], 0.0)
            high = pressure.astype(BF16)
            low = (pressure - high.astype(F32)).astype(BF16)
            high = jnp.where(inside, high, jnp.zeros((), BF16))
            low = jnp.where(inside, low, jnp.zeros((), BF16))
            both = jnp.where(upper, rows[0], rows[1])
            forces.append(
                jnp.dot(
                    jnp.concatenate([both, both], axis=1),
                    jnp.concatenate([high, low], axis=0),
                    preferred_element_type=F32,
                )
            )
        for d in range(0, GROUP, 2):
            facets, nodes = [], []
            for e in range(2):
                i, _ = at(r, d + e)
                facets.append(master_tab[plan_ref[row + 2, i] - base])
                nodes.append(slave_tab[plan_ref[row + 1, i]])
            left = jnp.concatenate([nodes[0], blank], axis=0)
            right = jnp.concatenate([blank, nodes[1]], axis=0)
            depth_ref[d // 2] = lax.dot_general(
                jnp.concatenate(facets, axis=0),
                jnp.concatenate([left, right], axis=1),
                (((0,), (0,)), ((), ())),
                preferred_element_type=F32,
            )
        for d in range(GROUP):
            i, _ = at(r - 1, d)
            e = d % 2
            slave = plan_ref[row + 1, i]
            part = forces[d // 2][8 * e : 8 * e + 8, e * BLK : (e + 1) * BLK]
            total_ref[slave] = total_ref[slave] + part
        return carry

    lax.fori_loop(0, (number + GROUP - 1) // GROUP + 1, body, 0)


def own_kernel(plan_ref, recv_ref, *refs, fresh):
    pos_ref = recv_ref if fresh else refs[0]
    refs = refs if fresh else refs[1:]
    start_ref, length_ref, total_ref, slave_tab, master_tab, force_tab, depth_ref = refs
    ones = jnp.ones((3, BLK), F32)
    zero1 = jnp.zeros((1, BLK), F32)
    places = recv_ref.shape[0]

    def entry(p, carry):
        position = pos_ref[p][0:3]
        p_high, p_low = split(position)
        slave_tab[p] = jnp.concatenate(
            [p_high, p_high, p_low, p_low, ones, zero1], axis=0
        ).astype(BF16)
        master_entry(p, position, recv_ref[p][3:6], master_tab, force_tab)
        total_ref[p] = jnp.zeros((ROWS, BLK), F32)
        return carry

    lax.fori_loop(0, places, entry, 0, unroll=8)
    run_tiles(
        plan_ref, 0, plan_ref[6, 0], 0, start_ref, length_ref, slave_tab, master_tab, force_tab,
        total_ref, depth_ref,
    )


def far_kernel(plan_ref, valid_ref, *refs, edges, fresh):
    edge_refs = refs[0:4]
    pos_refs = edge_refs if fresh else refs[4:8]
    refs = refs[4:] if fresh else refs[8:]
    start_ref, length_ref, own_ref, slave_tab, out_ref = refs[0:5]
    master_tab, force_tab, total_ref, depth_ref = refs[5:9]
    places = own_ref.shape[0]
    zero1 = jnp.zeros((1, BLK), F32)
    total_ref[...] = own_ref[...]
    for side in range(4):
        valid = valid_ref[side] > 0
        for e in range(edges):
            normal = jnp.where(valid, edge_refs[side][e], 0.0)[3:6]
            position = jnp.where(valid, pos_refs[side][e], 0.0)[0:3]
            master_entry(side * edges + e, position, normal, master_tab, force_tab)
    run_tiles(
        plan_ref, 3, plan_ref[7, 0], places, start_ref, length_ref, slave_tab, master_tab,
        force_tab, total_ref, depth_ref,
    )

    def finish(p, carry):
        tile = total_ref[p]
        out_ref[p] = (PENALTY / BLK) * jnp.concatenate([tile[0:3] + tile[3:6], zero1], axis=0)
        return carry

    lax.fori_loop(0, places, finish, 0, unroll=8)


def tile_cost(tiles):
    return pl.CostEstimate(
        flops=tiles * BLK * BLK * 64, transcendentals=0, bytes_accessed=tiles * BLK * 8
    )


def own_contact(plan, received, positions, start, length):
    places = received.shape[0]
    fresh = positions is None
    arrays = [received] + ([] if fresh else [positions]) + [start, length]

    def kernel(*refs):
        own_kernel(*refs, fresh=fresh)

    return pl.pallas_call(
        kernel,
        out_shape=[
            jax.ShapeDtypeStruct((places, ROWS, BLK), F32),
            jax.ShapeDtypeStruct((places, 16, BLK), BF16),
        ],
        in_specs=[sspec()] + [vspec()] * len(arrays),
        out_specs=[vspec()] * 2,
        scratch_shapes=[
            VMEM((places, 16, BLK), BF16),
            VMEM((places, 16, BLK), BF16),
            VMEM((GROUP // 2, BLK, 2 * BLK), F32),
        ],
        cost_estimate=tile_cost(start.shape[0] // 2),
        name="own_contact",
    )(plan, *arrays)


def far_contact(plan, valid, edges, edge_positions, start, length, total, slave_tab):
    places = total.shape[0]
    fresh = edge_positions is None
    edge_count = edges[0].shape[0]
    arrays = list(edges) + ([] if fresh else list(edge_positions))
    arrays += [start, length, total, slave_tab]

    def kernel(*refs):
        far_kernel(*refs, edges=edge_count, fresh=fresh)

    return pl.pallas_call(
        kernel,
        out_shape=jax.ShapeDtypeStruct((places, HALF, BLK), F32),
        in_specs=[sspec()] * 2 + [vspec()] * len(arrays),
        out_specs=vspec(),
        scratch_shapes=[
            VMEM((4 * edge_count, 16, BLK), BF16),
            VMEM((4 * edge_count, 16, BLK), BF16),
            VMEM((places, ROWS, BLK), F32),
            VMEM((GROUP // 2, BLK, 2 * BLK), F32),
        ],
        cost_estimate=tile_cost(start.shape[0] // 2),
        name="far_contact",
    )(plan, valid, *arrays)


def inverse_kernel(valid_ref, list_ref, out_ref):
    blocks = out_ref.shape[0]
    block_id = lax.broadcasted_iota(jnp.int32, (blocks, BLK), 0)
    lane_id = lax.broadcasted_iota(jnp.int32, (BLK, BLK), 0)
    rank = (lax.broadcasted_iota(jnp.int32, (BLK, BLK), 1) + 1).astype(F32)
    code = jnp.full((blocks, BLK), -1, jnp.int32)
    for side in range(4):
        nodes = list_ref[side : side + 1, :]
        valid = valid_ref[side] > 0
        in_block = jnp.where(
            jnp.logical_and(block_id == nodes // BLK, valid), 1.0, 0.0
        ).astype(BF16)
        at_lane = jnp.where(lane_id == (nodes & (BLK - 1)), rank, 0.0).astype(BF16)
        found = lax.dot_general(
            in_block, at_lane, (((1,), (1,)), ((), ())), preferred_element_type=F32
        ).astype(jnp.int32)
        code = jnp.where(found > 0, found - 1 + side * BLK, code)
    out_ref[...] = code


def inverse(valid, lists, blocks):
    return pl.pallas_call(
        inverse_kernel,
        out_shape=jax.ShapeDtypeStruct((blocks, BLK), jnp.int32),
        in_specs=[sspec(), vspec()],
        out_specs=vspec(),
        name="inverse",
    )(valid, lists)


def force_kernel(slot_ref, back_ref, first_ref, second_ref, list_ref, force_ref, *side_refs):
    half = first_ref.shape[0]
    blocks = slot_ref.shape[0]
    pad = jnp.zeros((ROWS - HALF, BLK), F32)
    lanes = []
    owners = []
    for side in range(4):
        nodes = jnp.broadcast_to(list_ref[side : side + 1, :], (ROWS, BLK))
        lanes.append(nodes & (BLK - 1))
        owners.append(nodes // BLK)
    sums = [jnp.zeros((ROWS, BLK), F32) for _ in range(4)]
    for k in range(blocks):
        internal = first_ref[k] if k < half else second_ref[k - half]
        tile = jnp.concatenate([back_ref[slot_ref[k]], pad], axis=0) - internal
        force_ref[k] = tile
        for side in range(4):
            sums[side] = jnp.where(
                owners[side] == k, lane_gather(tile, lanes[side]), sums[side]
            )
    for side in range(4):
        side_refs[side][...] = sums[side]


def nodal_force(block_slot, returned, internal, lists):
    blocks = 2 * internal[0].shape[0]
    return pl.pallas_call(
        force_kernel,
        out_shape=[jax.ShapeDtypeStruct((blocks, ROWS, BLK), F32)]
        + [jax.ShapeDtypeStruct((ROWS, BLK), F32)] * 4,
        in_specs=[sspec()] + [vspec()] * 4,
        out_specs=[vspec()] * 5,
        name="force",
    )(block_slot, returned, *internal, lists)


def update_kernel(
    slot_ref,
    force_ref,
    near0_ref,
    near1_ref,
    near2_ref,
    near3_ref,
    code_ref,
    mass_ref,
    vel_ref,
    disp_ref,
    pos_ref,
    vel_out,
    disp_out,
    *send_refs,
):
    blocks = force_ref.shape[0]
    near = [r[...] for r in (near0_ref, near1_ref, near2_ref, near3_ref)]
    if send_refs and send_refs[0].shape[0] != blocks:
        send_refs[0][...] = jnp.zeros(send_refs[0].shape, F32)
    zero1 = jnp.zeros((1, BLK), F32)
    for k in range(blocks):
        lanes = slice(k * BLK, (k + 1) * BLK)
        code = jnp.broadcast_to(code_ref[k : k + 1, :], (ROWS, BLK))
        index = code & (BLK - 1)
        extra = jnp.zeros((ROWS, BLK), F32)
        for side in range(4):
            inside = jnp.logical_and(code >= side * BLK, code < (side + 1) * BLK)
            extra = jnp.where(inside, lane_gather(near[side], index), extra)
        assembled = (force_ref[k] + extra)[0:6]
        vel = vel_ref[:, lanes] + TIME_STEP * mass_ref[:, lanes] * assembled
        disp = disp_ref[:, lanes] + TIME_STEP * vel
        vel_out[:, lanes] = vel
        disp_out[:, lanes] = disp
        if send_refs:
            send_refs[0][slot_ref[k]] = jnp.concatenate(
                [pos_ref[:, lanes] + disp[0:3], zero1], axis=0
            )


def update(block_slot, force, near, code, inv_mass, velocity, displacement, ref_pos, places):
    nodes = displacement.shape[1]
    out = [jax.ShapeDtypeStruct((6, nodes), F32)] * 2
    if places:
        out = out + [jax.ShapeDtypeStruct((places, HALF, BLK), F32)]
    return pl.pallas_call(
        update_kernel,
        out_shape=out,
        in_specs=[sspec()] + [vspec()] * 10,
        out_specs=[vspec()] * len(out),
        name="update",
    )(block_slot, force, *near, code, inv_mass, velocity, displacement, ref_pos)


def pair_lists(size):
    first = [(i, i ^ 1) for i in range(size)]
    second = [(i, (i + 1) % size if i % 2 else (i - 1) % size) for i in range(size)]
    return first, second


def swap(values, sizes):
    out = []
    for at, axis in enumerate(AXES):
        for stage, pairs in enumerate(pair_lists(sizes[at])):
            out.append(lax.ppermute(values[2 * at + stage], axis, pairs))
    return out


def body(
    displacement,
    velocity,
    ref_pos,
    normals,
    inv_mass,
    connectivity,
    stiffness,
    yield_force,
    shared_nodes,
    block_slot,
    edge_slots,
    tile_pairs,
    tile_count,
    win_start,
    win_len,
):
    sizes = [lax.axis_size(axis) for axis in AXES]
    if any(size % 2 for size in sizes):
        raise ValueError("odd axis")
    places = sizes[0] * sizes[1] * CAP
    blocks = displacement.shape[1] // BLK
    edge_count = edge_slots.shape[0]
    at = [lax.axis_index(axis) for axis in AXES]
    even = jnp.stack([1 - i % 2 for i in at]).astype(jnp.int32)
    valid = []
    for i, size in zip(at, sizes):
        valid += [jnp.int32(1), jnp.where((i == 0) | (i == size - 1), 0, 1).astype(jnp.int32)]
    valid = jnp.stack(valid)
    plan = plan_tiles(tile_count, tile_pairs, even, places, edge_count)
    lists = []
    for axis in range(2):
        low, high = shared_nodes[2 * axis], shared_nodes[2 * axis + 1]
        is_even = even[axis] == 1
        lists += [jnp.where(is_even, high, low), jnp.where(is_even, low, high)]
    lists = jnp.stack(lists)
    code = inverse(valid, lists, blocks)

    def exchange(blocks_out):
        return lax.all_to_all(blocks_out, AXES, split_axis=0, concat_axis=0, tiled=True)

    def half(disp, part):
        return element_forces(disp, connectivity, stiffness, yield_force, part, 2)

    outgoing = prep(block_slot, displacement, ref_pos, normals, places)
    first = None
    for step in range(STEPS):
        fresh = step == 0
        received = exchange(outgoing)
        internal0 = half(displacement, 0)
        received, internal0, plan, code = lax.optimization_barrier(
            (received, internal0, plan, code)
        )
        near = swap([received[edge_slots]] * 4, sizes)
        if fresh:
            first = (received, near)
        total, slave_tab = own_contact(
            plan, first[0], None if fresh else received, win_start, win_len
        )
        box_force = far_contact(
            plan, valid, first[1], None if fresh else near, win_start, win_len, total, slave_tab
        )
        box_force, later = lax.optimization_barrier((box_force, displacement))
        returned = exchange(box_force)
        internal1 = half(later, 1)
        force, *sides = nodal_force(block_slot, returned, (internal0, internal1), lists)
        incoming = swap(sides, sizes)
        last = step == STEPS - 1
        out = update(
            block_slot,
            force,
            incoming,
            code,
            inv_mass,
            velocity,
            displacement,
            ref_pos,
            0 if last else places,
        )
        velocity, displacement = out[0:2]
        if not last:
            outgoing = out[2]
    return (displacement, velocity)


def solution(mesh):
    split_last = P(None, AXES)
    placed = (
        split_last,
        split_last,
        split_last,
        split_last,
        split_last,
        split_last,
        P(None, None, AXES),
        P(AXES),
        split_last,
        P(AXES),
        P(AXES),
        split_last,
        P(AXES),
        P(AXES, None),
        P(AXES, None),
    )
    return jax.shard_map(
        body,
        mesh=mesh,
        in_specs=placed,
        out_specs=(split_last, split_last),
        check_vma=False,
    )
```

```python
import jax
import jax.numpy as jnp
from jax import lax
from jax.experimental import pallas as pl
from jax.experimental.pallas import tpu as pltpu
from jax.sharding import PartitionSpec as P

BLK = 128
CAP = 2
STEPS = 2
ROWS = 8
HALF = 4
EBLK = 8
GROUP = 16

TIME_STEP = 0.5
PENALTY = 32.0
THICKNESS = 0.2

AXES = ("gx", "gy")
F32 = jnp.float32
BF16 = jnp.bfloat16
VMEM = pltpu.VMEM
SMEM = pltpu.SMEM


def vspec():
    return pl.BlockSpec(memory_space=VMEM)


def sspec():
    return pl.BlockSpec(memory_space=SMEM)


def limit(mebibytes):
    return pltpu.CompilerParams(vmem_limit_bytes=mebibytes << 20)


def lane_gather(data, index):
    return jnp.take_along_axis(data, index, axis=1, mode="promise_in_bounds")


def split(x):
    high = x.astype(BF16).astype(F32)
    return high, x - high


def prep_kernel(slot_ref, disp_ref, pos_ref, nrm_ref, out_ref):
    places = out_ref.shape[0]
    blocks = slot_ref.shape[0]
    if places != blocks:
        out_ref[...] = jnp.zeros(out_ref.shape, F32)
    pad = jnp.zeros((ROWS - 6, BLK), F32)
    for k in range(blocks):
        lanes = slice(k * BLK, (k + 1) * BLK)
        position = pos_ref[:, lanes] + disp_ref[0:3, lanes]
        out_ref[slot_ref[k]] = jnp.concatenate([position, nrm_ref[:, lanes], pad], axis=0)


def prep(block_slot, displacement, ref_pos, normals, places):
    return pl.pallas_call(
        prep_kernel,
        out_shape=jax.ShapeDtypeStruct((places, ROWS, BLK), F32),
        in_specs=[sspec(), vspec(), vspec(), vspec()],
        out_specs=vspec(),
        compiler_params=limit(4),
        name="prep",
    )(block_slot, displacement, ref_pos, normals)


def fold_rows(tiles, row):
    low4 = row < 4
    low2 = (row & 2) == 0
    low1 = (row & 1) == 0
    four = []
    for i in range(4):
        a, b = tiles[i], tiles[i + 4]
        four.append(jnp.where(low4, a, b) + pltpu.roll(jnp.where(low4, b, a), 4, 0))
    two = []
    for i in range(2):
        a, b = four[i], four[i + 2]
        two.append(jnp.where(low2, a + pltpu.roll(a, 6, 0), b + pltpu.roll(b, 2, 0)))
    a, b = two
    return jnp.where(low1, a + pltpu.roll(a, 7, 0), b + pltpu.roll(b, 1, 0))


def element_kernel(disp_ref, conn_ref, stiff_ref, yield_ref, out_ref):
    row = lax.broadcasted_iota(jnp.int32, (ROWS, BLK), 0)
    row48 = lax.broadcasted_iota(jnp.int32, (48, BLK), 0)
    node = lax.broadcasted_iota(jnp.int32, (BLK, BLK), 0).astype(jnp.int16)
    unit = jnp.ones((), BF16)
    zero = jnp.zeros((), BF16)
    row48 = row48.astype(jnp.int16) & 3
    for k in range(out_ref.shape[0]):
        lanes = slice(k * BLK, (k + 1) * BLK)
        local = conn_ref[:, lanes] & (BLK - 1)
        index = jnp.concatenate([local, local], axis=0)
        dofs = []
        for t in range(3):
            first = jnp.broadcast_to(disp_ref[2 * t : 2 * t + 1, lanes], (4, BLK))
            second = jnp.broadcast_to(disp_ref[2 * t + 1 : 2 * t + 2, lanes], (4, BLK))
            dofs.append(lane_gather(jnp.concatenate([first, second], axis=0), index))
        trial = []
        for g in range(3):
            tiles = []
            for i in range(8 * g, 8 * g + 8):
                line = stiff_ref[i, :, lanes].astype(F32)
                tiles.append(line[0:8] * dofs[0] + line[8:16] * dofs[1] + line[16:24] * dofs[2])
            trial.append(fold_rows(tiles, row))
        squared = trial[0] * trial[0] + trial[1] * trial[1] + trial[2] * trial[2]
        squared = squared + pltpu.roll(squared, 4, 0)
        squared = squared + pltpu.roll(squared, 2, 0)
        squared = squared + pltpu.roll(squared, 1, 0)
        level = yield_ref[0, k : k + 1, :]
        factor = lax.rsqrt(1.0 + squared / (level * level))
        forces = jnp.concatenate([t * factor for t in trial], axis=0)
        high, low = split(forces)
        stacked = jnp.concatenate([high, low], axis=0).astype(BF16)
        small = local.astype(jnp.int16)
        total = jnp.zeros((48, BLK), F32)
        for a in range(4):
            corner = jnp.where(row48 == a, stacked, zero)
            picker = jnp.where(node == small[a : a + 1, :], unit, zero)
            total = total + lax.dot_general(
                corner, picker, (((1,), (1,)), ((), ())), preferred_element_type=F32
            )
        total = total[0:24] + total[24:48]
        pieces = []
        for t in range(3):
            x = total[8 * t : 8 * t + 8]
            x = x + pltpu.roll(x, 7, 0)
            x = x + pltpu.roll(x, 6, 0)
            pieces += [x[0:1], x[4:5]]
        out_ref[k] = jnp.concatenate(pieces + [jnp.zeros((2, BLK), F32)], axis=0)


def element_forces(displacement, connectivity, stiffness, yield_force, part=0, parts=1):
    nodes = displacement.shape[1]
    blocks = nodes // BLK // parts
    wide = EBLK * BLK
    steps = blocks // EBLK
    first = part * steps
    return pl.pallas_call(
        element_kernel,
        out_shape=jax.ShapeDtypeStruct((blocks, ROWS, BLK), F32),
        grid=(steps,),
        in_specs=[
            pl.BlockSpec((6, wide), lambda i: (0, i + first)),
            pl.BlockSpec((4, wide), lambda i: (0, i + first)),
            pl.BlockSpec((24, 24, wide), lambda i: (0, 0, i + first)),
            pl.BlockSpec((1, EBLK, BLK), lambda i: (i + first, 0, 0)),
        ],
        out_specs=pl.BlockSpec((EBLK, ROWS, BLK), lambda i: (i, 0, 0)),
        cost_estimate=pl.CostEstimate(
            flops=2 * 576 * nodes, transcendentals=nodes, bytes_accessed=2 * 576 * nodes
        ),
        compiler_params=limit(10),
        name="element",
    )(
        displacement,
        connectivity,
        pltpu.with_memory_space_constraint(stiffness, pltpu.HBM),
        yield_force.reshape(-1, EBLK, BLK),
    )


def plan_kernel(count_ref, pairs_ref, meta_ref, plan_ref, *, places, edges):
    tiles = pairs_ref.shape[1]
    for first, master in ((0, 0), (tiles, places)):
        plan_ref[0, first] = 0
        plan_ref[1, first] = 0
        plan_ref[2, first] = master
    log = edges.bit_length() - 1
    power = edges == 1 << log

    def sort(t, own):
        slave = pairs_ref[0, t]
        master = pairs_ref[1, t]
        is_own = master < places
        entry = master - places
        side = entry >> log if power else entry // edges
        flip = jnp.where(side < 2, meta_ref[0], meta_ref[1])
        moved = entry + edges * ((side ^ flip) - side)
        where = jnp.where(is_own, own, tiles + t - own)
        plan_ref[0, where] = t
        plan_ref[1, where] = slave
        plan_ref[2, where] = jnp.where(is_own, master, places + moved)
        return own + is_own.astype(jnp.int32)

    own = lax.fori_loop(0, count_ref[0], sort, jnp.int32(0))
    plan_ref[3, 0] = own
    plan_ref[3, 1] = count_ref[0] - own


def plan_tiles(tile_count, tile_pairs, meta, places, edges):
    def kernel(*refs):
        plan_kernel(*refs, places=places, edges=edges)

    return pl.pallas_call(
        kernel,
        out_shape=jax.ShapeDtypeStruct((4, 2 * tile_pairs.shape[1]), jnp.int32),
        in_specs=[sspec()] * 3,
        out_specs=sspec(),
        compiler_params=limit(1),
        name="plan",
    )(tile_count, tile_pairs, meta)


def master_entry(where, position, normal, master_tab, force_tab):
    zero1 = jnp.zeros((1, BLK), F32)
    zero2 = jnp.zeros((2, BLK), F32)
    n_high, n_low = split(normal)
    product = position * normal
    offset = THICKNESS + (product[0:1] + product[1:2] + product[2:3])
    o_high, o_rest = split(offset)
    o_mid, o_low = split(o_rest)
    negative = jnp.concatenate([-n_high, -n_low], axis=0)
    master_tab[where] = jnp.concatenate(
        [negative, negative, o_high, o_mid, o_low, zero1], axis=0
    ).astype(BF16)
    lines = [n_high, n_low, zero2]
    force_tab[where] = jnp.concatenate(lines + lines, axis=0).astype(BF16)


def run_tiles(
    plan_ref, first, number, base, start_ref, length_ref, slave_tab, master_tab, force_tab,
    total_ref, depth_ref,
):
    facet = lax.broadcasted_iota(jnp.int32, (BLK, 2 * BLK), 0).astype(jnp.int16)
    upper = lax.broadcasted_iota(jnp.int32, (16, BLK), 0) < 8
    blank = jnp.zeros((16, BLK), BF16)
    small = jnp.int16
    last = jnp.maximum(number - 1, 0)

    def at(group, d):
        i = group * GROUP + d
        return first + jnp.clip(i, 0, last), jnp.logical_and(i >= 0, i < number)

    def body(r, carry):
        forces = []
        for d in range(0, GROUP, 2):
            starts, lengths, rows = [], [], []
            for e in range(2):
                i, live = at(r - 1, d + e)
                t = plan_ref[0, i]
                starts.append(start_ref[pl.ds(t, 1), :])
                lengths.append(jnp.where(live, length_ref[pl.ds(t, 1), :], 0))
                rows.append(force_tab[plan_ref[2, i] - base])
            start = jnp.concatenate(starts, axis=1).astype(small)
            length = jnp.concatenate(lengths, axis=1).astype(small)
            inside = ((facet - start) & (BLK - 1)) < length
            pressure = jnp.maximum(depth_ref[d // 2], 0.0)
            high = pressure.astype(BF16)
            low = (pressure - high.astype(F32)).astype(BF16)
            high = jnp.where(inside, high, jnp.zeros((), BF16))
            low = jnp.where(inside, low, jnp.zeros((), BF16))
            both = jnp.where(upper, rows[0], rows[1])
            forces.append(
                jnp.dot(
                    jnp.concatenate([both, both], axis=1),
                    jnp.concatenate([high, low], axis=0),
                    preferred_element_type=F32,
                )
            )
        for d in range(0, GROUP, 2):
            facets, nodes = [], []
            for e in range(2):
                i, _ = at(r, d + e)
                facets.append(master_tab[plan_ref[2, i] - base])
                nodes.append(slave_tab[plan_ref[1, i]])
            left = jnp.concatenate([nodes[0], blank], axis=0)
            right = jnp.concatenate([blank, nodes[1]], axis=0)
            depth_ref[d // 2] = lax.dot_general(
                jnp.concatenate(facets, axis=0),
                jnp.concatenate([left, right], axis=1),
                (((0,), (0,)), ((), ())),
                preferred_element_type=F32,
            )
        for d in range(GROUP):
            i, _ = at(r - 1, d)
            e = d % 2
            slave = plan_ref[1, i]
            part = forces[d // 2][8 * e : 8 * e + 8, e * BLK : (e + 1) * BLK]
            total_ref[slave] = total_ref[slave] + part
        return carry

    lax.fori_loop(0, (number + GROUP - 1) // GROUP + 1, body, 0)


def own_kernel(plan_ref, recv_ref, *refs, fresh):
    pos_ref = recv_ref if fresh else refs[0]
    refs = refs if fresh else refs[1:]
    start_ref, length_ref, total_ref, slave_tab, master_tab, force_tab, depth_ref = refs
    ones = jnp.ones((3, BLK), F32)
    zero1 = jnp.zeros((1, BLK), F32)
    places = recv_ref.shape[0]

    def entry(p, carry):
        position = pos_ref[p][0:3]
        p_high, p_low = split(position)
        slave_tab[p] = jnp.concatenate(
            [p_high, p_high, p_low, p_low, ones, zero1], axis=0
        ).astype(BF16)
        master_entry(p, position, recv_ref[p][3:6], master_tab, force_tab)
        total_ref[p] = jnp.zeros((ROWS, BLK), F32)
        return carry

    lax.fori_loop(0, places, entry, 0, unroll=8)
    run_tiles(
        plan_ref, 0, plan_ref[3, 0], 0, start_ref, length_ref, slave_tab, master_tab, force_tab,
        total_ref, depth_ref,
    )


def far_kernel(plan_ref, meta_ref, *refs, edges, fresh):
    edge_refs = refs[0:4]
    pos_refs = edge_refs if fresh else refs[4:8]
    refs = refs[4:] if fresh else refs[8:]
    start_ref, length_ref, own_ref, slave_tab, out_ref = refs[0:5]
    master_tab, force_tab, total_ref, depth_ref = refs[5:9]
    places = own_ref.shape[0]
    zero1 = jnp.zeros((1, BLK), F32)
    total_ref[...] = own_ref[...]
    for side in range(4):
        valid = meta_ref[2 + side] > 0
        for e in range(edges):
            normal = jnp.where(valid, edge_refs[side][e], 0.0)[3:6]
            position = jnp.where(valid, pos_refs[side][e], 0.0)[0:3]
            master_entry(side * edges + e, position, normal, master_tab, force_tab)
    run_tiles(
        plan_ref, plan_ref.shape[1] // 2, plan_ref[3, 1], places, start_ref, length_ref, slave_tab, master_tab,
        force_tab, total_ref, depth_ref,
    )

    def finish(p, carry):
        tile = total_ref[p]
        out_ref[p] = (PENALTY / BLK) * jnp.concatenate([tile[0:3] + tile[3:6], zero1], axis=0)
        return carry

    lax.fori_loop(0, places, finish, 0, unroll=8)


def tile_cost(tiles):
    return pl.CostEstimate(
        flops=tiles * BLK * BLK * 64, transcendentals=0, bytes_accessed=tiles * BLK * 8
    )


def own_contact(plan, received, positions, start, length):
    places = received.shape[0]
    fresh = positions is None
    arrays = [received] + ([] if fresh else [positions]) + [start, length]

    def kernel(*refs):
        own_kernel(*refs, fresh=fresh)

    return pl.pallas_call(
        kernel,
        out_shape=[
            jax.ShapeDtypeStruct((places, ROWS, BLK), F32),
            jax.ShapeDtypeStruct((places, 16, BLK), BF16),
        ],
        in_specs=[sspec()] + [vspec()] * len(arrays),
        out_specs=[vspec()] * 2,
        scratch_shapes=[
            VMEM((places, 16, BLK), BF16),
            VMEM((places, 16, BLK), BF16),
            VMEM((GROUP // 2, BLK, 2 * BLK), F32),
        ],
        cost_estimate=tile_cost(start.shape[0] // 2),
        compiler_params=limit(8),
        name="own_contact",
    )(plan, *arrays)


def far_contact(plan, meta, edges, edge_positions, start, length, total, slave_tab):
    places = total.shape[0]
    fresh = edge_positions is None
    edge_count = edges[0].shape[0]
    arrays = list(edges) + ([] if fresh else list(edge_positions))
    arrays += [start, length, total, slave_tab]

    def kernel(*refs):
        far_kernel(*refs, edges=edge_count, fresh=fresh)

    return pl.pallas_call(
        kernel,
        out_shape=jax.ShapeDtypeStruct((places, HALF, BLK), F32),
        in_specs=[sspec()] * 2 + [vspec()] * len(arrays),
        out_specs=vspec(),
        scratch_shapes=[
            VMEM((4 * edge_count, 16, BLK), BF16),
            VMEM((4 * edge_count, 16, BLK), BF16),
            VMEM((places, ROWS, BLK), F32),
            VMEM((GROUP // 2, BLK, 2 * BLK), F32),
        ],
        cost_estimate=tile_cost(start.shape[0] // 2),
        compiler_params=limit(8),
        name="far_contact",
    )(plan, meta, *arrays)


def side_list(list_ref, meta_ref, side):
    axis = side // 2
    low = list_ref[2 * axis : 2 * axis + 1, :]
    high = list_ref[2 * axis + 1 : 2 * axis + 2, :]
    return jnp.where(meta_ref[axis] != side % 2, high, low)


def inverse_kernel(meta_ref, list_ref, out_ref):
    blocks = out_ref.shape[0]
    block_id = lax.broadcasted_iota(jnp.int32, (blocks, BLK), 0)
    lane_id = lax.broadcasted_iota(jnp.int32, (BLK, BLK), 0)
    rank = (lax.broadcasted_iota(jnp.int32, (BLK, BLK), 1) + 1).astype(F32)
    code = jnp.full((blocks, BLK), -1, jnp.int32)
    for side in range(4):
        nodes = side_list(list_ref, meta_ref, side)
        valid = meta_ref[2 + side] > 0
        in_block = jnp.where(
            jnp.logical_and(block_id == nodes // BLK, valid), 1.0, 0.0
        ).astype(BF16)
        at_lane = jnp.where(lane_id == (nodes & (BLK - 1)), rank, 0.0).astype(BF16)
        found = lax.dot_general(
            in_block, at_lane, (((1,), (1,)), ((), ())), preferred_element_type=F32
        ).astype(jnp.int32)
        code = jnp.where(found > 0, found - 1 + side * BLK, code)
    out_ref[...] = code


def inverse(meta, lists, blocks):
    return pl.pallas_call(
        inverse_kernel,
        out_shape=jax.ShapeDtypeStruct((blocks, BLK), jnp.int32),
        in_specs=[sspec(), vspec()],
        out_specs=vspec(),
        compiler_params=limit(2),
        name="inverse",
    )(meta, lists)


def force_kernel(slot_ref, meta_ref, back_ref, first_ref, second_ref, list_ref, force_ref, *side_refs):
    half = first_ref.shape[0]
    blocks = slot_ref.shape[0]
    pad = jnp.zeros((ROWS - HALF, BLK), F32)
    lanes = []
    owners = []
    for side in range(4):
        nodes = jnp.broadcast_to(side_list(list_ref, meta_ref, side), (ROWS, BLK))
        lanes.append(nodes & (BLK - 1))
        owners.append(nodes // BLK)
    sums = [jnp.zeros((ROWS, BLK), F32) for _ in range(4)]
    for k in range(blocks):
        internal = first_ref[k] if k < half else second_ref[k - half]
        tile = jnp.concatenate([back_ref[slot_ref[k]], pad], axis=0) - internal
        force_ref[k] = tile
        for side in range(4):
            sums[side] = jnp.where(
                owners[side] == k, lane_gather(tile, lanes[side]), sums[side]
            )
    for side in range(4):
        side_refs[side][...] = sums[side]


def nodal_force(block_slot, meta, returned, internal, lists):
    blocks = 2 * internal[0].shape[0]
    return pl.pallas_call(
        force_kernel,
        out_shape=[jax.ShapeDtypeStruct((blocks, ROWS, BLK), F32)]
        + [jax.ShapeDtypeStruct((ROWS, BLK), F32)] * 4,
        in_specs=[sspec()] * 2 + [vspec()] * 4,
        out_specs=[vspec()] * 5,
        compiler_params=limit(4),
        name="force",
    )(block_slot, meta, returned, *internal, lists)


def update_kernel(
    slot_ref,
    force_ref,
    near0_ref,
    near1_ref,
    near2_ref,
    near3_ref,
    code_ref,
    mass_ref,
    vel_ref,
    disp_ref,
    pos_ref,
    vel_out,
    disp_out,
    *send_refs,
):
    blocks = force_ref.shape[0]
    near = [r[...] for r in (near0_ref, near1_ref, near2_ref, near3_ref)]
    if send_refs and send_refs[0].shape[0] != blocks:
        send_refs[0][...] = jnp.zeros(send_refs[0].shape, F32)
    zero1 = jnp.zeros((1, BLK), F32)
    for k in range(blocks):
        lanes = slice(k * BLK, (k + 1) * BLK)
        code = jnp.broadcast_to(code_ref[k : k + 1, :], (ROWS, BLK))
        index = code & (BLK - 1)
        extra = jnp.zeros((ROWS, BLK), F32)
        for side in range(4):
            inside = jnp.logical_and(code >= side * BLK, code < (side + 1) * BLK)
            extra = jnp.where(inside, lane_gather(near[side], index), extra)
        assembled = (force_ref[k] + extra)[0:6]
        vel = vel_ref[:, lanes] + TIME_STEP * mass_ref[:, lanes] * assembled
        disp = disp_ref[:, lanes] + TIME_STEP * vel
        vel_out[:, lanes] = vel
        disp_out[:, lanes] = disp
        if send_refs:
            send_refs[0][slot_ref[k]] = jnp.concatenate(
                [pos_ref[:, lanes] + disp[0:3], zero1], axis=0
            )


def update(block_slot, force, near, code, inv_mass, velocity, displacement, ref_pos, places):
    nodes = displacement.shape[1]
    out = [jax.ShapeDtypeStruct((6, nodes), F32)] * 2
    if places:
        out = out + [jax.ShapeDtypeStruct((places, HALF, BLK), F32)]
    return pl.pallas_call(
        update_kernel,
        out_shape=out,
        in_specs=[sspec()] + [vspec()] * 10,
        out_specs=[vspec()] * len(out),
        compiler_params=limit(6),
        name="update",
    )(block_slot, force, *near, code, inv_mass, velocity, displacement, ref_pos)


def pair_lists(sizes):
    rows, columns = sizes
    near = [[(i, i ^ 1) for i in range(size)] for size in sizes]
    other = [(i, (i + 1) % rows if i % 2 else (i - 1) % rows) for i in range(rows)]
    flat = []
    for i in range(rows):
        for j in range(columns):
            k = j + 1 if j % 2 else j - 1
            inside = 0 <= k < columns
            flat.append((i * columns + j, i * columns + k if inside else (i ^ 1) * columns + j))
    return [("gx", near[0]), ("gx", other), ("gy", near[1]), (AXES, flat)]


def swap(values, sizes):
    moved = [
        lax.ppermute(value, axis, pairs)
        for value, (axis, pairs) in reversed(list(zip(values, pair_lists(sizes))))
    ]
    return moved[::-1]


def body(
    displacement,
    velocity,
    ref_pos,
    normals,
    inv_mass,
    connectivity,
    stiffness,
    yield_force,
    shared_nodes,
    block_slot,
    edge_slots,
    tile_pairs,
    tile_count,
    win_start,
    win_len,
):
    sizes = [lax.axis_size(axis) for axis in AXES]
    if any(size % 2 for size in sizes):
        raise ValueError("odd axis")
    places = sizes[0] * sizes[1] * CAP
    blocks = displacement.shape[1] // BLK
    edge_count = edge_slots.shape[0]
    at = [lax.axis_index(axis) for axis in AXES]
    odd = [i % 2 for i in at]
    inner = [((i > 0) & (i < size - 1)).astype(jnp.int32) for i, size in zip(at, sizes)]
    slot = jnp.arange(8, dtype=jnp.int32)
    meta = jnp.ones((8,), jnp.int32)
    for i, value in ((0, 1 - odd[0]), (1, 1 - odd[1]), (3, inner[0]), (5, inner[1])):
        meta = jnp.where(slot == i, value, meta)
    plan = plan_tiles(tile_count, tile_pairs, meta, places, edge_count)
    code = None

    def exchange(blocks_out):
        return lax.all_to_all(blocks_out, AXES, split_axis=0, concat_axis=0, tiled=True)

    def half(disp, part):
        return element_forces(disp, connectivity, stiffness, yield_force, part, 2)

    outgoing = prep(block_slot, displacement, ref_pos, normals, places)
    first = None
    for step in range(STEPS):
        fresh = step == 0
        received = exchange(outgoing)
        internal0 = half(displacement, 0)
        received, internal0, plan = lax.optimization_barrier((received, internal0, plan))
        near = swap([received[edge_slots]] * 4, sizes)
        if fresh:
            first = (received, near)
        total, slave_tab = own_contact(
            plan, first[0], None if fresh else received, win_start, win_len
        )
        box_force = far_contact(
            plan, meta, first[1], None if fresh else near, win_start, win_len, total, slave_tab
        )
        box_force, later = lax.optimization_barrier((box_force, displacement))
        returned = exchange(box_force)
        internal1 = half(later, 1)
        force, *sides = nodal_force(
            block_slot, meta, returned, (internal0, internal1), shared_nodes
        )
        if code is None:
            sides, lists = lax.optimization_barrier((sides, shared_nodes))
            code = inverse(meta, lists, blocks)
        incoming = swap(sides, sizes)
        last = step == STEPS - 1
        out = update(
            block_slot,
            force,
            incoming,
            code,
            inv_mass,
            velocity,
            displacement,
            ref_pos,
            0 if last else places,
        )
        velocity, displacement = out[0:2]
        if not last:
            outgoing = out[2]
    return (displacement, velocity)


def solution(mesh):
    split_last = P(None, AXES)
    placed = (
        split_last,
        split_last,
        split_last,
        split_last,
        split_last,
        split_last,
        P(None, None, AXES),
        P(AXES),
        split_last,
        P(AXES),
        P(AXES),
        split_last,
        P(AXES),
        P(AXES, None),
        P(AXES, None),
    )
    return jax.shard_map(
        body,
        mesh=mesh,
        in_specs=placed,
        out_specs=(split_last, split_last),
        check_vma=False,
    )
```

```python
import jax
import jax.numpy as jnp
from jax import lax
from jax.experimental import pallas as pl
from jax.experimental.pallas import tpu as pltpu
from jax.sharding import PartitionSpec as P

BLK = 128
CAP = 2
STEPS = 2
ROWS = 8
HALF = 4
EBLK = 8
GROUP = 16

TIME_STEP = 0.5
PENALTY = 32.0
THICKNESS = 0.2

AXES = ("gx", "gy")
F32 = jnp.float32
BF16 = jnp.bfloat16
VMEM = pltpu.VMEM
SMEM = pltpu.SMEM


def vspec():
    return pl.BlockSpec(memory_space=VMEM)


def sspec():
    return pl.BlockSpec(memory_space=SMEM)


def limit(mebibytes):
    return pltpu.CompilerParams(vmem_limit_bytes=mebibytes << 20)


def held(x):
    return pltpu.with_memory_space_constraint(x, pltpu.VMEM)


def left(x):
    return pltpu.with_memory_space_constraint(x, pltpu.HBM)


def lane_gather(data, index):
    return jnp.take_along_axis(data, index, axis=1, mode="promise_in_bounds")


def split(x):
    high = x.astype(BF16).astype(F32)
    return high, x - high


def prep_kernel(slot_ref, disp_ref, pos_ref, nrm_ref, out_ref):
    places = out_ref.shape[0]
    blocks = slot_ref.shape[0]
    if places != blocks:
        out_ref[...] = jnp.zeros(out_ref.shape, F32)
    pad = jnp.zeros((ROWS - 6, BLK), F32)
    for k in range(blocks):
        lanes = slice(k * BLK, (k + 1) * BLK)
        position = pos_ref[:, lanes] + disp_ref[0:3, lanes]
        out_ref[slot_ref[k]] = jnp.concatenate([position, nrm_ref[:, lanes], pad], axis=0)


def prep(block_slot, displacement, ref_pos, normals, places):
    return pl.pallas_call(
        prep_kernel,
        out_shape=jax.ShapeDtypeStruct((places, ROWS, BLK), F32),
        in_specs=[sspec(), vspec(), vspec(), vspec()],
        out_specs=vspec(),
        compiler_params=limit(4),
        name="prep",
    )(block_slot, left(displacement), left(ref_pos), left(normals))


def fold_rows(tiles, row):
    low4 = row < 4
    low2 = (row & 2) == 0
    low1 = (row & 1) == 0
    four = []
    for i in range(4):
        a, b = tiles[i], tiles[i + 4]
        four.append(jnp.where(low4, a, b) + pltpu.roll(jnp.where(low4, b, a), 4, 0))
    two = []
    for i in range(2):
        a, b = four[i], four[i + 2]
        two.append(jnp.where(low2, a + pltpu.roll(a, 6, 0), b + pltpu.roll(b, 2, 0)))
    a, b = two
    return jnp.where(low1, a + pltpu.roll(a, 7, 0), b + pltpu.roll(b, 1, 0))


def element_kernel(
    disp_ref, conn_ref, hbm_ref, yield_ref, out_ref, stiff_ref, sems, *, origin
):
    wide = EBLK * BLK
    turns = out_ref.shape[0] // EBLK

    def load(r):
        return pltpu.make_async_copy(
            hbm_ref.at[:, :, pl.ds(origin * BLK + r * wide, wide)], stiff_ref.at[r], sems.at[r]
        )

    for r in range(turns):
        load(r).start()
    row = lax.broadcasted_iota(jnp.int32, (ROWS, BLK), 0)
    row48 = lax.broadcasted_iota(jnp.int32, (48, BLK), 0)
    node = lax.broadcasted_iota(jnp.int32, (BLK, BLK), 0).astype(jnp.int16)
    unit = jnp.ones((), BF16)
    zero = jnp.zeros((), BF16)
    row48 = row48.astype(jnp.int16) & 3
    def one_block(r, d):
        k = r * EBLK + d
        lanes = pl.ds(pl.multiple_of((origin + k) * BLK, BLK), BLK)
        local = conn_ref[:, lanes] & (BLK - 1)
        index = jnp.concatenate([local, local], axis=0)
        dofs = []
        for t in range(3):
            first = jnp.broadcast_to(disp_ref[2 * t : 2 * t + 1, lanes], (4, BLK))
            second = jnp.broadcast_to(disp_ref[2 * t + 1 : 2 * t + 2, lanes], (4, BLK))
            dofs.append(lane_gather(jnp.concatenate([first, second], axis=0), index))
        trial = []
        for g in range(3):
            tiles = []
            for i in range(8 * g, 8 * g + 8):
                line = stiff_ref[r, i, :, d * BLK : (d + 1) * BLK].astype(F32)
                tiles.append(line[0:8] * dofs[0] + line[8:16] * dofs[1] + line[16:24] * dofs[2])
            trial.append(fold_rows(tiles, row))
        squared = trial[0] * trial[0] + trial[1] * trial[1] + trial[2] * trial[2]
        squared = squared + pltpu.roll(squared, 4, 0)
        squared = squared + pltpu.roll(squared, 2, 0)
        squared = squared + pltpu.roll(squared, 1, 0)
        level = yield_ref[pl.ds(origin + k, 1), :]
        factor = lax.rsqrt(1.0 + squared / (level * level))
        forces = jnp.concatenate([t * factor for t in trial], axis=0)
        high, low = split(forces)
        stacked = jnp.concatenate([high, low], axis=0).astype(BF16)
        small = local.astype(jnp.int16)
        total = jnp.zeros((48, BLK), F32)
        for a in range(4):
            corner = jnp.where(row48 == a, stacked, zero)
            picker = jnp.where(node == small[a : a + 1, :], unit, zero)
            total = total + lax.dot_general(
                corner, picker, (((1,), (1,)), ((), ())), preferred_element_type=F32
            )
        total = total[0:24] + total[24:48]
        pieces = []
        for t in range(3):
            x = total[8 * t : 8 * t + 8]
            x = x + pltpu.roll(x, 7, 0)
            x = x + pltpu.roll(x, 6, 0)
            pieces += [x[0:1], x[4:5]]
        out_ref[k] = jnp.concatenate(pieces + [jnp.zeros((2, BLK), F32)], axis=0)

    def body(r, carry):
        load(r).wait()
        for d in range(EBLK):
            one_block(r, d)
        return carry

    lax.fori_loop(0, turns, body, 0)


def element_forces(displacement, connectivity, stiffness, yield_force, part=0, parts=1):
    nodes = displacement.shape[1]
    blocks = nodes // BLK // parts

    def kernel(*refs):
        element_kernel(*refs, origin=part * blocks)

    return pl.pallas_call(
        kernel,
        out_shape=jax.ShapeDtypeStruct((blocks, ROWS, BLK), F32),
        in_specs=[vspec()] * 2 + [pl.BlockSpec(memory_space=pltpu.HBM)] + [vspec()],
        out_specs=vspec(),
        scratch_shapes=[
            VMEM((blocks // EBLK, 24, 24, EBLK * BLK), BF16),
            pltpu.SemaphoreType.DMA((blocks // EBLK,)),
        ],
        cost_estimate=pl.CostEstimate(
            flops=2 * 576 * nodes, transcendentals=nodes, bytes_accessed=2 * 576 * nodes
        ),
        compiler_params=limit(12),
        name="element",
    )(displacement, connectivity, left(stiffness), yield_force.reshape(-1, BLK))


def plan_kernel(count_ref, pairs_ref, meta_ref, plan_ref, *, places, edges):
    tiles = pairs_ref.shape[1]
    for first, master in ((0, 0), (tiles, places)):
        plan_ref[0, first] = 0
        plan_ref[1, first] = 0
        plan_ref[2, first] = master
    log = edges.bit_length() - 1
    power = edges == 1 << log

    def sort(t, own):
        slave = pairs_ref[0, t]
        master = pairs_ref[1, t]
        is_own = master < places
        entry = master - places
        side = entry >> log if power else entry // edges
        flip = jnp.where(side < 2, meta_ref[0], meta_ref[1])
        moved = entry + edges * ((side ^ flip) - side)
        where = jnp.where(is_own, own, tiles + t - own)
        plan_ref[0, where] = t
        plan_ref[1, where] = slave
        plan_ref[2, where] = jnp.where(is_own, master, places + moved)
        return own + is_own.astype(jnp.int32)

    def several(r, own):
        for d in range(8):
            own = sort(8 * r + d, own)
        return own

    own = lax.fori_loop(0, count_ref[0] // 8, several, jnp.int32(0))
    own = lax.fori_loop(count_ref[0] // 8 * 8, count_ref[0], sort, own)
    plan_ref[3, 0] = own
    plan_ref[3, 1] = count_ref[0] - own


def plan_tiles(tile_count, tile_pairs, meta, places, edges):
    def kernel(*refs):
        plan_kernel(*refs, places=places, edges=edges)

    return pl.pallas_call(
        kernel,
        out_shape=jax.ShapeDtypeStruct((4, 2 * tile_pairs.shape[1]), jnp.int32),
        in_specs=[sspec()] * 3,
        out_specs=sspec(),
        compiler_params=limit(1),
        name="plan",
    )(tile_count, tile_pairs, meta)


def master_entry(where, position, normal, master_tab, force_tab):
    zero1 = jnp.zeros((1, BLK), F32)
    zero2 = jnp.zeros((2, BLK), F32)
    n_high, n_low = split(normal)
    product = position * normal
    offset = THICKNESS + (product[0:1] + product[1:2] + product[2:3])
    o_high, o_rest = split(offset)
    o_mid, o_low = split(o_rest)
    negative = jnp.concatenate([-n_high, -n_low], axis=0)
    master_tab[where] = jnp.concatenate(
        [negative, negative, o_high, o_mid, o_low, zero1], axis=0
    ).astype(BF16)
    lines = [n_high, n_low, zero2]
    force_tab[where] = jnp.concatenate(lines + lines, axis=0).astype(BF16)


def run_tiles(
    plan_ref, first, number, base, start_ref, length_ref, slave_tab, master_tab, force_tab,
    total_ref, depth_ref,
):
    facet = lax.broadcasted_iota(jnp.int32, (BLK, 2 * BLK), 0).astype(jnp.int16)
    upper = lax.broadcasted_iota(jnp.int32, (16, BLK), 0) < 8
    blank = jnp.zeros((16, BLK), BF16)
    small = jnp.int16
    last = jnp.maximum(number - 1, 0)

    def at(group, d):
        i = group * GROUP + d
        return first + jnp.minimum(i, last), i < number

    def depths(group):
        for d in range(0, GROUP, 2):
            facets, nodes = [], []
            for e in range(2):
                i, _ = at(group, d + e)
                facets.append(master_tab[plan_ref[2, i] - base])
                nodes.append(slave_tab[plan_ref[1, i]])
            left = jnp.concatenate([nodes[0], blank], axis=0)
            right = jnp.concatenate([blank, nodes[1]], axis=0)
            depth_ref[d // 2] = lax.dot_general(
                jnp.concatenate(facets, axis=0),
                jnp.concatenate([left, right], axis=1),
                (((0,), (0,)), ((), ())),
                preferred_element_type=F32,
            )

    def body(group, carry):
        forces = []
        for d in range(0, GROUP, 2):
            starts, lengths, rows = [], [], []
            for e in range(2):
                i, live = at(group, d + e)
                t = plan_ref[0, i]
                starts.append(start_ref[pl.ds(t, 1), :])
                lengths.append(jnp.where(live, length_ref[pl.ds(t, 1), :], 0))
                rows.append(force_tab[plan_ref[2, i] - base])
            start = jnp.concatenate(starts, axis=1).astype(small)
            length = jnp.concatenate(lengths, axis=1).astype(small)
            inside = ((facet - start) & (BLK - 1)) < length
            pressure = jnp.maximum(depth_ref[d // 2], 0.0)
            high = pressure.astype(BF16)
            low = (pressure - high.astype(F32)).astype(BF16)
            high = jnp.where(inside, high, jnp.zeros((), BF16))
            low = jnp.where(inside, low, jnp.zeros((), BF16))
            both = jnp.where(upper, rows[0], rows[1])
            forces.append(
                jnp.dot(
                    jnp.concatenate([both, both], axis=1),
                    jnp.concatenate([high, low], axis=0),
                    preferred_element_type=F32,
                )
            )
        depths(group + 1)
        for d in range(GROUP):
            i, _ = at(group, d)
            e = d % 2
            slave = plan_ref[1, i]
            part = forces[d // 2][8 * e : 8 * e + 8, e * BLK : (e + 1) * BLK]
            total_ref[slave] = total_ref[slave] + part
        return carry

    depths(0)
    lax.fori_loop(0, (number + GROUP - 1) // GROUP, body, 0)


def own_kernel(plan_ref, recv_ref, *refs, fresh):
    pos_ref = recv_ref if fresh else refs[0]
    refs = refs if fresh else refs[1:]
    start_ref, length_ref, total_ref, slave_tab, master_tab, force_tab, depth_ref = refs
    ones = jnp.ones((3, BLK), F32)
    zero1 = jnp.zeros((1, BLK), F32)
    places = recv_ref.shape[0]

    def entry(p, carry):
        position = pos_ref[p][0:3]
        p_high, p_low = split(position)
        slave_tab[p] = jnp.concatenate(
            [p_high, p_high, p_low, p_low, ones, zero1], axis=0
        ).astype(BF16)
        master_entry(p, position, recv_ref[p][3:6], master_tab, force_tab)
        total_ref[p] = jnp.zeros((ROWS, BLK), F32)
        return carry

    lax.fori_loop(0, places, entry, 0, unroll=8)
    run_tiles(
        plan_ref, 0, plan_ref[3, 0], 0, start_ref, length_ref, slave_tab, master_tab, force_tab,
        total_ref, depth_ref,
    )


def far_kernel(plan_ref, meta_ref, *refs, edges, fresh):
    edge_refs = refs[0:4]
    pos_refs = edge_refs if fresh else refs[4:8]
    refs = refs[4:] if fresh else refs[8:]
    start_ref, length_ref, own_ref, slave_tab, out_ref = refs[0:5]
    master_tab, force_tab, total_ref, depth_ref = refs[5:9]
    places = own_ref.shape[0]
    zero1 = jnp.zeros((1, BLK), F32)
    total_ref[...] = own_ref[...]
    for side in range(4):
        valid = meta_ref[2 + side] > 0
        for e in range(edges):
            normal = jnp.where(valid, edge_refs[side][e], 0.0)[3:6]
            position = jnp.where(valid, pos_refs[side][e], 0.0)[0:3]
            master_entry(side * edges + e, position, normal, master_tab, force_tab)
    run_tiles(
        plan_ref, plan_ref.shape[1] // 2, plan_ref[3, 1], places, start_ref, length_ref, slave_tab, master_tab,
        force_tab, total_ref, depth_ref,
    )

    def finish(p, carry):
        tile = total_ref[p]
        out_ref[p] = (PENALTY / BLK) * jnp.concatenate([tile[0:3] + tile[3:6], zero1], axis=0)
        return carry

    lax.fori_loop(0, places, finish, 0, unroll=8)


def tile_cost(tiles):
    return pl.CostEstimate(
        flops=tiles * BLK * BLK * 64, transcendentals=0, bytes_accessed=tiles * BLK * 8
    )


def own_contact(plan, received, positions, start, length):
    places = received.shape[0]
    fresh = positions is None
    arrays = [received] + ([] if fresh else [positions]) + [start, length]

    def kernel(*refs):
        own_kernel(*refs, fresh=fresh)

    return pl.pallas_call(
        kernel,
        out_shape=[
            jax.ShapeDtypeStruct((places, ROWS, BLK), F32),
            jax.ShapeDtypeStruct((places, 16, BLK), BF16),
        ],
        in_specs=[sspec()] + [vspec()] * len(arrays),
        out_specs=[vspec()] * 2,
        scratch_shapes=[
            VMEM((places, 16, BLK), BF16),
            VMEM((places, 16, BLK), BF16),
            VMEM((GROUP // 2, BLK, 2 * BLK), F32),
        ],
        cost_estimate=tile_cost(start.shape[0] // 2),
        compiler_params=limit(8),
        name="own_contact",
    )(plan, *arrays)


def far_contact(plan, meta, edges, edge_positions, start, length, total, slave_tab):
    places = total.shape[0]
    fresh = edge_positions is None
    edge_count = edges[0].shape[0]
    arrays = list(edges) + ([] if fresh else list(edge_positions))
    arrays += [start, length, total, slave_tab]

    def kernel(*refs):
        far_kernel(*refs, edges=edge_count, fresh=fresh)

    return pl.pallas_call(
        kernel,
        out_shape=jax.ShapeDtypeStruct((places, HALF, BLK), F32),
        in_specs=[sspec()] * 2 + [vspec()] * len(arrays),
        out_specs=vspec(),
        scratch_shapes=[
            VMEM((4 * edge_count, 16, BLK), BF16),
            VMEM((4 * edge_count, 16, BLK), BF16),
            VMEM((places, ROWS, BLK), F32),
            VMEM((GROUP // 2, BLK, 2 * BLK), F32),
        ],
        cost_estimate=tile_cost(start.shape[0] // 2),
        compiler_params=limit(8),
        name="far_contact",
    )(plan, meta, *arrays)


def side_list(list_ref, meta_ref, side):
    axis = side // 2
    low = list_ref[2 * axis : 2 * axis + 1, :]
    high = list_ref[2 * axis + 1 : 2 * axis + 2, :]
    return jnp.where(meta_ref[axis] != side % 2, high, low)


def inverse_kernel(meta_ref, list_ref, out_ref):
    blocks = out_ref.shape[0]
    block_id = lax.broadcasted_iota(jnp.int32, (blocks, BLK), 0)
    lane_id = lax.broadcasted_iota(jnp.int32, (BLK, BLK), 0)
    rank = (lax.broadcasted_iota(jnp.int32, (BLK, BLK), 1) + 1).astype(F32)
    code = jnp.full((blocks, BLK), -1, jnp.int32)
    for side in range(4):
        nodes = side_list(list_ref, meta_ref, side)
        valid = meta_ref[2 + side] > 0
        in_block = jnp.where(
            jnp.logical_and(block_id == nodes // BLK, valid), 1.0, 0.0
        ).astype(BF16)
        at_lane = jnp.where(lane_id == (nodes & (BLK - 1)), rank, 0.0).astype(BF16)
        found = lax.dot_general(
            in_block, at_lane, (((1,), (1,)), ((), ())), preferred_element_type=F32
        ).astype(jnp.int32)
        code = jnp.where(found > 0, found - 1 + side * BLK, code)
    out_ref[...] = code


def inverse(meta, lists, blocks):
    return pl.pallas_call(
        inverse_kernel,
        out_shape=jax.ShapeDtypeStruct((blocks, BLK), jnp.int32),
        in_specs=[sspec(), vspec()],
        out_specs=vspec(),
        compiler_params=limit(2),
        name="inverse",
    )(meta, lists)


def force_kernel(slot_ref, meta_ref, back_ref, first_ref, second_ref, list_ref, force_ref, *side_refs):
    half = first_ref.shape[0]
    blocks = slot_ref.shape[0]
    pad = jnp.zeros((ROWS - HALF, BLK), F32)
    lanes = []
    owners = []
    for side in range(4):
        nodes = jnp.broadcast_to(side_list(list_ref, meta_ref, side), (ROWS, BLK))
        lanes.append(nodes & (BLK - 1))
        owners.append(nodes // BLK)
    sums = [jnp.zeros((ROWS, BLK), F32) for _ in range(4)]
    for k in range(blocks):
        internal = first_ref[k] if k < half else second_ref[k - half]
        tile = jnp.concatenate([back_ref[slot_ref[k]], pad], axis=0) - internal
        force_ref[k] = tile
        for side in range(4):
            sums[side] = jnp.where(
                owners[side] == k, lane_gather(tile, lanes[side]), sums[side]
            )
    for side in range(4):
        side_refs[side][...] = sums[side]


def nodal_force(block_slot, meta, returned, internal, lists):
    blocks = 2 * internal[0].shape[0]
    return pl.pallas_call(
        force_kernel,
        out_shape=[jax.ShapeDtypeStruct((blocks, ROWS, BLK), F32)]
        + [jax.ShapeDtypeStruct((ROWS, BLK), F32)] * 4,
        in_specs=[sspec()] * 2 + [vspec()] * 4,
        out_specs=[vspec()] * 5,
        compiler_params=limit(4),
        name="force",
    )(block_slot, meta, returned, *internal, lists)


def update_kernel(
    slot_ref,
    force_ref,
    near0_ref,
    near1_ref,
    near2_ref,
    near3_ref,
    code_ref,
    mass_ref,
    vel_ref,
    disp_ref,
    pos_ref,
    vel_out,
    disp_out,
    *send_refs,
):
    blocks = force_ref.shape[0]
    near = [r[...] for r in (near0_ref, near1_ref, near2_ref, near3_ref)]
    if send_refs and send_refs[0].shape[0] != blocks:
        send_refs[0][...] = jnp.zeros(send_refs[0].shape, F32)
    zero1 = jnp.zeros((1, BLK), F32)
    for k in range(blocks):
        lanes = slice(k * BLK, (k + 1) * BLK)
        code = jnp.broadcast_to(code_ref[k : k + 1, :], (ROWS, BLK))
        index = code & (BLK - 1)
        extra = jnp.zeros((ROWS, BLK), F32)
        for side in range(4):
            inside = jnp.logical_and(code >= side * BLK, code < (side + 1) * BLK)
            extra = jnp.where(inside, lane_gather(near[side], index), extra)
        assembled = (force_ref[k] + extra)[0:6]
        vel = vel_ref[:, lanes] + TIME_STEP * mass_ref[:, lanes] * assembled
        disp = disp_ref[:, lanes] + TIME_STEP * vel
        vel_out[:, lanes] = vel
        disp_out[:, lanes] = disp
        if send_refs:
            send_refs[0][slot_ref[k]] = jnp.concatenate(
                [pos_ref[:, lanes] + disp[0:3], zero1], axis=0
            )


def update(block_slot, force, near, code, inv_mass, velocity, displacement, ref_pos, places):
    nodes = displacement.shape[1]
    out = [jax.ShapeDtypeStruct((6, nodes), F32)] * 2
    if places:
        out = out + [jax.ShapeDtypeStruct((places, HALF, BLK), F32)]
    return pl.pallas_call(
        update_kernel,
        out_shape=out,
        in_specs=[sspec()] + [vspec()] * 10,
        out_specs=[vspec()] * len(out),
        compiler_params=limit(6),
        name="update",
    )(block_slot, force, *near, code, inv_mass, velocity, displacement, ref_pos)


def pair_lists(sizes):
    rows, columns = sizes
    near = [[(i, i ^ 1) for i in range(size)] for size in sizes]
    other = [(i, (i + 1) % rows if i % 2 else (i - 1) % rows) for i in range(rows)]
    flat = []
    for i in range(rows):
        for j in range(columns):
            k = j + 1 if j % 2 else j - 1
            inside = 0 <= k < columns
            flat.append((i * columns + j, i * columns + k if inside else (i ^ 1) * columns + j))
    return [("gx", near[0]), ("gx", other), ("gy", near[1]), (AXES, flat)]


def swap(values, sizes):
    moved = [
        lax.ppermute(value, axis, pairs)
        for value, (axis, pairs) in reversed(list(zip(values, pair_lists(sizes))))
    ]
    return moved[::-1]


def body(
    displacement,
    velocity,
    ref_pos,
    normals,
    inv_mass,
    connectivity,
    stiffness,
    yield_force,
    shared_nodes,
    block_slot,
    edge_slots,
    tile_pairs,
    tile_count,
    win_start,
    win_len,
):
    sizes = [lax.axis_size(axis) for axis in AXES]
    if any(size % 2 for size in sizes):
        raise ValueError("odd axis")
    places = sizes[0] * sizes[1] * CAP
    blocks = displacement.shape[1] // BLK
    edge_count = edge_slots.shape[0]
    at = [lax.axis_index(axis) for axis in AXES]
    odd = [i % 2 for i in at]
    inner = [((i > 0) & (i < size - 1)).astype(jnp.int32) for i, size in zip(at, sizes)]
    slot = jnp.arange(8, dtype=jnp.int32)
    meta = jnp.ones((8,), jnp.int32)
    for i, value in ((0, 1 - odd[0]), (1, 1 - odd[1]), (3, inner[0]), (5, inner[1])):
        meta = jnp.where(slot == i, value, meta)
    plan = plan_tiles(tile_count, tile_pairs, meta, places, edge_count)
    code = None

    def exchange(blocks_out):
        return lax.all_to_all(blocks_out, AXES, split_axis=0, concat_axis=0, tiled=True)

    def half(disp, part):
        return element_forces(disp, connectivity, stiffness, yield_force, part, 2)

    outgoing = prep(block_slot, displacement, ref_pos, normals, places)
    first = None
    for step in range(STEPS):
        fresh = step == 0
        received = exchange(outgoing)
        internal0 = half(displacement, 0)
        received, internal0, plan = lax.optimization_barrier((received, internal0, plan))
        near = swap([received[edge_slots]] * 4, sizes)
        if fresh:
            first = (received, near)
        total, slave_tab = own_contact(
            plan, first[0], None if fresh else received, win_start, win_len
        )
        box_force = far_contact(
            plan, meta, first[1], None if fresh else near, win_start, win_len, total, slave_tab
        )
        box_force, later = lax.optimization_barrier((box_force, displacement))
        returned = exchange(box_force)
        internal1 = half(later, 1)
        force, *sides = nodal_force(
            block_slot, meta, returned, (internal0, internal1), shared_nodes
        )
        if code is None:
            sides, lists = lax.optimization_barrier((sides, shared_nodes))
            code = inverse(meta, lists, blocks)
        incoming = swap(sides, sizes)
        last = step == STEPS - 1
        out = update(
            block_slot,
            force,
            incoming,
            code,
            inv_mass,
            velocity,
            displacement,
            ref_pos,
            0 if last else places,
        )
        velocity, displacement = out[0:2]
        if not last:
            outgoing = out[2]
    return (displacement, velocity)


def solution(mesh):
    split_last = P(None, AXES)
    placed = (
        split_last,
        split_last,
        split_last,
        split_last,
        split_last,
        split_last,
        P(None, None, AXES),
        P(AXES),
        split_last,
        P(AXES),
        P(AXES),
        split_last,
        P(AXES),
        P(AXES, None),
        P(AXES, None),
    )
    return jax.shard_map(
        body,
        mesh=mesh,
        in_specs=placed,
        out_specs=(split_last, split_last),
        check_vma=False,
    )
```

```python
import jax
import jax.numpy as jnp
from jax import lax
from jax.experimental import pallas as pl
from jax.experimental.pallas import tpu as pltpu
from jax.sharding import PartitionSpec as P

BLK = 128
CAP = 2
STEPS = 2
ROWS = 8
HALF = 4
EBLK = 8
GROUP = 16
FIELD = 10

TIME_STEP = 0.5
PENALTY = 32.0
THICKNESS = 0.2

AXES = ("gx", "gy")
F32 = jnp.float32
BF16 = jnp.bfloat16
VMEM = pltpu.VMEM
SMEM = pltpu.SMEM


def vspec():
    return pl.BlockSpec(memory_space=VMEM)


def sspec():
    return pl.BlockSpec(memory_space=SMEM)


def limit(mebibytes):
    return pltpu.CompilerParams(vmem_limit_bytes=mebibytes << 20)


def left(x):
    return pltpu.with_memory_space_constraint(x, pltpu.HBM)


def lane_gather(data, index):
    return jnp.take_along_axis(data, index, axis=1, mode="promise_in_bounds")


def split(x):
    high = x.astype(BF16).astype(F32)
    return high, x - high


def prep_kernel(slot_ref, disp_ref, pos_ref, nrm_ref, out_ref):
    places = out_ref.shape[0]
    blocks = slot_ref.shape[0]
    if places != blocks:
        out_ref[...] = jnp.zeros(out_ref.shape, F32)
    pad = jnp.zeros((ROWS - 6, BLK), F32)
    for k in range(blocks):
        lanes = slice(k * BLK, (k + 1) * BLK)
        position = pos_ref[:, lanes] + disp_ref[0:3, lanes]
        out_ref[slot_ref[k]] = jnp.concatenate([position, nrm_ref[:, lanes], pad], axis=0)


def prep(block_slot, displacement, ref_pos, normals, places):
    return pl.pallas_call(
        prep_kernel,
        out_shape=jax.ShapeDtypeStruct((places, ROWS, BLK), F32),
        in_specs=[sspec(), vspec(), vspec(), vspec()],
        out_specs=vspec(),
        compiler_params=limit(4),
        name="prep",
    )(left(block_slot), left(displacement), left(ref_pos), left(normals))


def fold_rows(tiles, row):
    low4 = row < 4
    low2 = (row & 2) == 0
    low1 = (row & 1) == 0
    four = []
    for i in range(4):
        a, b = tiles[i], tiles[i + 4]
        four.append(jnp.where(low4, a, b) + pltpu.roll(jnp.where(low4, b, a), 4, 0))
    two = []
    for i in range(2):
        a, b = four[i], four[i + 2]
        two.append(jnp.where(low2, a + pltpu.roll(a, 6, 0), b + pltpu.roll(b, 2, 0)))
    a, b = two
    return jnp.where(low1, a + pltpu.roll(a, 7, 0), b + pltpu.roll(b, 1, 0))


def element_kernel(*refs, origin, places):
    disp_ref, conn_ref, hbm_ref, yield_ref = refs[0:4]
    out_ref = refs[6] if places else refs[4]
    stiff_ref, sems = refs[-2:]
    wide = EBLK * BLK
    turns = out_ref.shape[0] // EBLK
    if places:
        plan_ref = refs[7]
        sort = tile_sorter(*refs[4:6], plan_ref, places)
        share = -(-refs[5].shape[1] // turns)

    def load(r):
        return pltpu.make_async_copy(
            hbm_ref.at[:, :, pl.ds(origin * BLK + r * wide, wide)], stiff_ref.at[r], sems.at[r]
        )

    for r in range(turns):
        load(r).start()
    row = lax.broadcasted_iota(jnp.int32, (ROWS, BLK), 0)
    row48 = lax.broadcasted_iota(jnp.int32, (48, BLK), 0)
    node = lax.broadcasted_iota(jnp.int32, (BLK, BLK), 0).astype(jnp.int16)
    unit = jnp.ones((), BF16)
    zero = jnp.zeros((), BF16)
    row48 = row48.astype(jnp.int16) & 3
    def one_block(r, d):
        k = r * EBLK + d
        lanes = pl.ds(pl.multiple_of((origin + k) * BLK, BLK), BLK)
        local = conn_ref[:, lanes] & (BLK - 1)
        index = jnp.concatenate([local, local], axis=0)
        dofs = []
        for t in range(3):
            first = jnp.broadcast_to(disp_ref[2 * t : 2 * t + 1, lanes], (4, BLK))
            second = jnp.broadcast_to(disp_ref[2 * t + 1 : 2 * t + 2, lanes], (4, BLK))
            dofs.append(lane_gather(jnp.concatenate([first, second], axis=0), index))
        trial = []
        for g in range(3):
            tiles = []
            for i in range(8 * g, 8 * g + 8):
                line = stiff_ref[r, i, :, d * BLK : (d + 1) * BLK].astype(F32)
                tiles.append(line[0:8] * dofs[0] + line[8:16] * dofs[1] + line[16:24] * dofs[2])
            trial.append(fold_rows(tiles, row))
        squared = trial[0] * trial[0] + trial[1] * trial[1] + trial[2] * trial[2]
        squared = squared + pltpu.roll(squared, 4, 0)
        squared = squared + pltpu.roll(squared, 2, 0)
        squared = squared + pltpu.roll(squared, 1, 0)
        level = yield_ref[pl.ds(origin + k, 1), :]
        factor = lax.rsqrt(1.0 + squared / (level * level))
        forces = jnp.concatenate([t * factor for t in trial], axis=0)
        high, low = split(forces)
        stacked = jnp.concatenate([high, low], axis=0).astype(BF16)
        small = local.astype(jnp.int16)
        total = jnp.zeros((48, BLK), F32)
        for a in range(4):
            corner = jnp.where(row48 == a, stacked, zero)
            picker = jnp.where(node == small[a : a + 1, :], unit, zero)
            total = total + lax.dot_general(
                corner, picker, (((1,), (1,)), ((), ())), preferred_element_type=F32
            )
        total = total[0:24] + total[24:48]
        pieces = []
        for t in range(3):
            x = total[8 * t : 8 * t + 8]
            x = x + pltpu.roll(x, 7, 0)
            x = x + pltpu.roll(x, 6, 0)
            pieces += [x[0:1], x[4:5]]
        out_ref[k] = jnp.concatenate(pieces + [jnp.zeros((2, BLK), F32)], axis=0)

    def body(r, own):
        load(r).wait()
        for d in range(EBLK):
            if places:
                for q in range(share * d // EBLK, share * (d + 1) // EBLK):
                    own = sort(r * share + q, own)
            one_block(r, d)
        return own

    own = lax.fori_loop(0, turns, body, jnp.int32(0))
    if places:
        plan_ref[plan_ref.shape[0] - 2] = own
        plan_ref[plan_ref.shape[0] - 1] = refs[4][0] - own


def element_forces(
    displacement, connectivity, stiffness, yield_force, part=0, parts=1, tiles=(), places=0
):
    nodes = displacement.shape[1]
    blocks = nodes // BLK // parts

    def kernel(*refs):
        element_kernel(*refs, origin=part * blocks, places=places)

    out = jax.ShapeDtypeStruct((blocks, ROWS, BLK), F32)
    out_spec = vspec()
    if places:
        out = [out, jax.ShapeDtypeStruct((2 * tiles[1].shape[1] + 8,), jnp.int32)]
        out_spec = [out_spec, sspec()]
    return pl.pallas_call(
        kernel,
        out_shape=out,
        in_specs=[vspec()] * 2
        + [pl.BlockSpec(memory_space=pltpu.HBM)]
        + [vspec()]
        + [sspec()] * len(tiles),
        out_specs=out_spec,
        scratch_shapes=[
            VMEM((blocks // EBLK, 24, 24, EBLK * BLK), BF16),
            pltpu.SemaphoreType.DMA((blocks // EBLK,)),
        ],
        cost_estimate=pl.CostEstimate(
            flops=2 * 576 * nodes, transcendentals=nodes, bytes_accessed=2 * 576 * nodes
        ),
        compiler_params=limit(12),
        name="element",
    )(displacement, connectivity, left(stiffness), yield_force, *tiles)


def packed(tile, slave, master):
    return tile | slave << FIELD | master << (2 * FIELD)


def unpacked(entry):
    mask = (1 << FIELD) - 1
    return entry & mask, (entry >> FIELD) & mask, entry >> (2 * FIELD)


def tile_sorter(count_ref, pairs_ref, plan_ref, places):
    tiles = pairs_ref.shape[1]
    plan_ref[0] = packed(0, 0, 0)
    plan_ref[tiles] = packed(0, 0, places)
    count = count_ref[0]

    def sort(t, own):
        live = t < count
        at = jnp.minimum(t, tiles - 1)
        master = pairs_ref[1, at]
        is_own = master < places
        where = jnp.where(is_own, own, tiles + t - own)
        where = jnp.where(live, where, 2 * tiles)
        plan_ref[where] = packed(at, pairs_ref[0, at], master)
        return own + jnp.where(jnp.logical_and(live, is_own), 1, 0)

    return sort


def master_entry(where, position, normal, master_tab, force_tab):
    zero1 = jnp.zeros((1, BLK), F32)
    zero2 = jnp.zeros((2, BLK), F32)
    n_high, n_low = split(normal)
    product = position * normal
    offset = THICKNESS + (product[0:1] + product[1:2] + product[2:3])
    o_high, o_rest = split(offset)
    o_mid, o_low = split(o_rest)
    negative = jnp.concatenate([-n_high, -n_low], axis=0)
    master_tab[where] = jnp.concatenate(
        [negative, negative, o_high, o_mid, o_low, zero1], axis=0
    ).astype(BF16)
    lines = [n_high, n_low, zero2]
    force_tab[where] = jnp.concatenate(lines + lines, axis=0).astype(BF16)


def run_tiles(
    plan_ref, first, number, base, start_ref, length_ref, slave_tab, master_tab, force_tab,
    total_ref, depth_ref,
):
    facet = lax.broadcasted_iota(jnp.int32, (BLK, 2 * BLK), 0).astype(jnp.int16)
    upper = lax.broadcasted_iota(jnp.int32, (16, BLK), 0) < 8
    blank = jnp.zeros((16, BLK), BF16)
    small = jnp.int16
    last = jnp.maximum(number - 1, 0)

    def at(group, d):
        i = group * GROUP + d
        return plan_ref[first + jnp.minimum(i, last)], i < number

    def depths(group):
        for d in range(0, GROUP, 2):
            facets, nodes = [], []
            for e in range(2):
                entry, _ = at(group, d + e)
                _, slave, master = unpacked(entry)
                facets.append(master_tab[master - base])
                nodes.append(slave_tab[slave])
            left = jnp.concatenate([nodes[0], blank], axis=0)
            right = jnp.concatenate([blank, nodes[1]], axis=0)
            depth_ref[d // 2] = lax.dot_general(
                jnp.concatenate(facets, axis=0),
                jnp.concatenate([left, right], axis=1),
                (((0,), (0,)), ((), ())),
                preferred_element_type=F32,
            )

    def body(group, carry):
        forces = []
        for d in range(0, GROUP, 2):
            starts, lengths, rows = [], [], []
            for e in range(2):
                entry, live = at(group, d + e)
                t, _, master = unpacked(entry)
                starts.append(start_ref[pl.ds(t, 1), :])
                lengths.append(jnp.where(live, length_ref[pl.ds(t, 1), :], 0))
                rows.append(force_tab[master - base])
            start = jnp.concatenate(starts, axis=1).astype(small)
            length = jnp.concatenate(lengths, axis=1).astype(small)
            inside = ((facet - start) & (BLK - 1)) < length
            pressure = jnp.maximum(depth_ref[d // 2], 0.0)
            high = pressure.astype(BF16)
            low = (pressure - high.astype(F32)).astype(BF16)
            high = jnp.where(inside, high, jnp.zeros((), BF16))
            low = jnp.where(inside, low, jnp.zeros((), BF16))
            both = jnp.where(upper, rows[0], rows[1])
            forces.append(
                jnp.dot(
                    jnp.concatenate([both, both], axis=1),
                    jnp.concatenate([high, low], axis=0),
                    preferred_element_type=F32,
                )
            )
        depths(group + 1)
        for d in range(GROUP):
            _, slave, _ = unpacked(at(group, d)[0])
            e = d % 2
            part = forces[d // 2][8 * e : 8 * e + 8, e * BLK : (e + 1) * BLK]
            total_ref[slave] = total_ref[slave] + part
        return carry

    depths(0)
    lax.fori_loop(0, (number + GROUP - 1) // GROUP, body, 0)


def own_kernel(plan_ref, recv_ref, *refs, fresh):
    pos_ref = recv_ref if fresh else refs[0]
    refs = refs if fresh else refs[1:]
    start_ref, length_ref, total_ref, slave_tab, master_tab, force_tab, depth_ref = refs
    ones = jnp.ones((3, BLK), F32)
    zero1 = jnp.zeros((1, BLK), F32)
    places = recv_ref.shape[0]

    def entry(p, carry):
        position = pos_ref[p][0:3]
        p_high, p_low = split(position)
        slave_tab[p] = jnp.concatenate(
            [p_high, p_high, p_low, p_low, ones, zero1], axis=0
        ).astype(BF16)
        master_entry(p, position, recv_ref[p][3:6], master_tab, force_tab)
        total_ref[p] = jnp.zeros((ROWS, BLK), F32)
        return carry

    lax.fori_loop(0, places, entry, 0, unroll=8)
    run_tiles(
        plan_ref, 0, plan_ref[plan_ref.shape[0] - 2], 0, start_ref, length_ref, slave_tab, master_tab, force_tab,
        total_ref, depth_ref,
    )


def far_kernel(plan_ref, meta_ref, *refs, edges, fresh):
    edge_refs = refs[0:4]
    pos_refs = edge_refs if fresh else refs[4:8]
    refs = refs[4:] if fresh else refs[8:]
    start_ref, length_ref, own_ref, slave_tab, out_ref = refs[0:5]
    master_tab, force_tab, total_ref, depth_ref = refs[5:9]
    places = own_ref.shape[0]
    zero1 = jnp.zeros((1, BLK), F32)
    total_ref[...] = own_ref[...]
    for side in range(4):
        valid = meta_ref[2 + side] > 0
        base = (side ^ meta_ref[side // 2]) * edges
        for e in range(edges):
            normal = jnp.where(valid, edge_refs[side][e], 0.0)[3:6]
            position = jnp.where(valid, pos_refs[side][e], 0.0)[0:3]
            master_entry(base + e, position, normal, master_tab, force_tab)
    run_tiles(
        plan_ref, start_ref.shape[0], plan_ref[plan_ref.shape[0] - 1], places, start_ref, length_ref,
        slave_tab, master_tab, force_tab, total_ref, depth_ref,
    )

    def finish(p, carry):
        tile = total_ref[p]
        out_ref[p] = (PENALTY / BLK) * jnp.concatenate([tile[0:3] + tile[3:6], zero1], axis=0)
        return carry

    lax.fori_loop(0, places, finish, 0, unroll=8)


def tile_cost(tiles):
    return pl.CostEstimate(
        flops=tiles * BLK * BLK * 64, transcendentals=0, bytes_accessed=tiles * BLK * 8
    )


def own_contact(plan, received, positions, start, length):
    places = received.shape[0]
    fresh = positions is None
    arrays = [received] + ([] if fresh else [positions]) + [start, length]

    def kernel(*refs):
        own_kernel(*refs, fresh=fresh)

    return pl.pallas_call(
        kernel,
        out_shape=[
            jax.ShapeDtypeStruct((places, ROWS, BLK), F32),
            jax.ShapeDtypeStruct((places, 16, BLK), BF16),
        ],
        in_specs=[sspec()] + [vspec()] * len(arrays),
        out_specs=[vspec()] * 2,
        scratch_shapes=[
            VMEM((places, 16, BLK), BF16),
            VMEM((places, 16, BLK), BF16),
            VMEM((GROUP // 2, BLK, 2 * BLK), F32),
        ],
        cost_estimate=tile_cost(start.shape[0] // 2),
        compiler_params=limit(8),
        name="own_contact",
    )(plan, *arrays)


def far_contact(plan, meta, edges, edge_positions, start, length, total, slave_tab):
    places = total.shape[0]
    fresh = edge_positions is None
    edge_count = edges[0].shape[0]
    arrays = list(edges) + ([] if fresh else list(edge_positions))
    arrays += [start, length, total, slave_tab]

    def kernel(*refs):
        far_kernel(*refs, edges=edge_count, fresh=fresh)

    return pl.pallas_call(
        kernel,
        out_shape=jax.ShapeDtypeStruct((places, HALF, BLK), F32),
        in_specs=[sspec()] * 2 + [vspec()] * len(arrays),
        out_specs=vspec(),
        scratch_shapes=[
            VMEM((4 * edge_count, 16, BLK), BF16),
            VMEM((4 * edge_count, 16, BLK), BF16),
            VMEM((places, ROWS, BLK), F32),
            VMEM((GROUP // 2, BLK, 2 * BLK), F32),
        ],
        cost_estimate=tile_cost(start.shape[0] // 2),
        compiler_params=limit(8),
        name="far_contact",
    )(plan, meta, *arrays)


def side_list(list_ref, meta_ref, side):
    axis = side // 2
    low = list_ref[2 * axis : 2 * axis + 1, :]
    high = list_ref[2 * axis + 1 : 2 * axis + 2, :]
    return jnp.where(meta_ref[axis] != side % 2, high, low)


def inverse_kernel(meta_ref, list_ref, out_ref):
    blocks = out_ref.shape[0]
    block_id = lax.broadcasted_iota(jnp.int32, (blocks, BLK), 0)
    lane_id = lax.broadcasted_iota(jnp.int32, (BLK, BLK), 0)
    rank = (lax.broadcasted_iota(jnp.int32, (BLK, BLK), 1) + 1).astype(F32)
    code = jnp.full((blocks, BLK), -1, jnp.int32)
    for side in range(4):
        nodes = side_list(list_ref, meta_ref, side)
        valid = meta_ref[2 + side] > 0
        in_block = jnp.where(
            jnp.logical_and(block_id == nodes // BLK, valid), 1.0, 0.0
        ).astype(BF16)
        at_lane = jnp.where(lane_id == (nodes & (BLK - 1)), rank, 0.0).astype(BF16)
        found = lax.dot_general(
            in_block, at_lane, (((1,), (1,)), ((), ())), preferred_element_type=F32
        ).astype(jnp.int32)
        code = jnp.where(found > 0, found - 1 + side * BLK, code)
    out_ref[...] = code


def inverse(meta, lists, blocks):
    return pl.pallas_call(
        inverse_kernel,
        out_shape=jax.ShapeDtypeStruct((blocks, BLK), jnp.int32),
        in_specs=[sspec(), vspec()],
        out_specs=vspec(),
        compiler_params=limit(2),
        name="inverse",
    )(meta, lists)


def force_kernel(slot_ref, meta_ref, back_ref, first_ref, second_ref, list_ref, force_ref, *side_refs):
    half = first_ref.shape[0]
    blocks = slot_ref.shape[0]
    pad = jnp.zeros((ROWS - HALF, BLK), F32)
    lanes = []
    owners = []
    for side in range(4):
        nodes = jnp.broadcast_to(side_list(list_ref, meta_ref, side), (ROWS, BLK))
        lanes.append(nodes & (BLK - 1))
        owners.append(nodes // BLK)
    sums = [jnp.zeros((ROWS, BLK), F32) for _ in range(4)]
    for k in range(blocks):
        internal = first_ref[k] if k < half else second_ref[k - half]
        tile = jnp.concatenate([back_ref[slot_ref[k]], pad], axis=0) - internal
        force_ref[k] = tile
    for side in range(4):
        for k in range(blocks):
            sums[side] = jnp.where(
                owners[side] == k, lane_gather(force_ref[k], lanes[side]), sums[side]
            )
    for side in range(4):
        side_refs[side][...] = sums[side]


def nodal_force(block_slot, meta, returned, internal, lists):
    blocks = 2 * internal[0].shape[0]
    return pl.pallas_call(
        force_kernel,
        out_shape=[jax.ShapeDtypeStruct((blocks, ROWS, BLK), F32)]
        + [jax.ShapeDtypeStruct((ROWS, BLK), F32)] * 4,
        in_specs=[sspec()] * 2 + [vspec()] * 4,
        out_specs=[vspec()] * 5,
        compiler_params=limit(4),
        name="force",
    )(block_slot, meta, returned, *internal, lists)


def update_kernel(
    slot_ref,
    force_ref,
    near0_ref,
    near1_ref,
    near2_ref,
    near3_ref,
    code_ref,
    mass_ref,
    vel_ref,
    disp_ref,
    pos_ref,
    vel_out,
    disp_out,
    *send_refs,
):
    blocks = force_ref.shape[0]
    near = [r[...] for r in (near0_ref, near1_ref, near2_ref, near3_ref)]
    if send_refs and send_refs[0].shape[0] != blocks:
        send_refs[0][...] = jnp.zeros(send_refs[0].shape, F32)
    zero1 = jnp.zeros((1, BLK), F32)
    for k in range(blocks):
        lanes = slice(k * BLK, (k + 1) * BLK)
        code = jnp.broadcast_to(code_ref[k : k + 1, :], (ROWS, BLK))
        index = code & (BLK - 1)
        extra = jnp.zeros((ROWS, BLK), F32)
        for side in range(4):
            inside = jnp.logical_and(code >= side * BLK, code < (side + 1) * BLK)
            extra = jnp.where(inside, lane_gather(near[side], index), extra)
        assembled = (force_ref[k] + extra)[0:6]
        vel = vel_ref[:, lanes] + TIME_STEP * mass_ref[:, lanes] * assembled
        disp = disp_ref[:, lanes] + TIME_STEP * vel
        vel_out[:, lanes] = vel
        disp_out[:, lanes] = disp
        if send_refs:
            send_refs[0][slot_ref[k]] = jnp.concatenate(
                [pos_ref[:, lanes] + disp[0:3], zero1], axis=0
            )


def update(block_slot, force, near, code, inv_mass, velocity, displacement, ref_pos, places):
    nodes = displacement.shape[1]
    out = [jax.ShapeDtypeStruct((6, nodes), F32)] * 2
    if places:
        out = out + [jax.ShapeDtypeStruct((places, HALF, BLK), F32)]
    return pl.pallas_call(
        update_kernel,
        out_shape=out,
        in_specs=[sspec()] + [vspec()] * 10,
        out_specs=[vspec()] * len(out),
        compiler_params=limit(6),
        name="update",
    )(block_slot, force, *near, code, inv_mass, velocity, displacement, ref_pos)


def pair_lists(sizes):
    rows, columns = sizes
    near = [[(i, i ^ 1) for i in range(size)] for size in sizes]
    other = [(i, (i + 1) % rows if i % 2 else (i - 1) % rows) for i in range(rows)]
    flat = []
    for i in range(rows):
        for j in range(columns):
            k = j + 1 if j % 2 else j - 1
            inside = 0 <= k < columns
            flat.append((i * columns + j, i * columns + k if inside else (i ^ 1) * columns + j))
    return [("gx", near[0]), ("gx", other), ("gy", near[1]), (AXES, flat)]


def swap(values, sizes):
    moved = [
        lax.ppermute(value, axis, pairs)
        for value, (axis, pairs) in reversed(list(zip(values, pair_lists(sizes))))
    ]
    return moved[::-1]


def body(
    displacement,
    velocity,
    ref_pos,
    normals,
    inv_mass,
    connectivity,
    stiffness,
    yield_force,
    shared_nodes,
    block_slot,
    edge_slots,
    tile_pairs,
    tile_count,
    win_start,
    win_len,
):
    sizes = [lax.axis_size(axis) for axis in AXES]
    if any(size % 2 for size in sizes):
        raise ValueError("odd axis")
    places = sizes[0] * sizes[1] * CAP
    blocks = displacement.shape[1] // BLK
    edge_count = edge_slots.shape[0]
    if max(tile_pairs.shape[1], places + 4 * edge_count) >= 1 << FIELD:
        raise ValueError("field width")
    at = [lax.axis_index(axis) for axis in AXES]
    odd = [i % 2 for i in at]
    inner = [((i > 0) & (i < size - 1)).astype(jnp.int32) for i, size in zip(at, sizes)]
    slot = jnp.arange(8, dtype=jnp.int32)
    meta = jnp.ones((8,), jnp.int32)
    for i, value in ((0, 1 - odd[0]), (1, 1 - odd[1]), (3, inner[0]), (5, inner[1])):
        meta = jnp.where(slot == i, value, meta)
    levels = yield_force.reshape(-1, BLK)
    plan = None
    code = None

    def exchange(blocks_out):
        return lax.all_to_all(blocks_out, AXES, split_axis=0, concat_axis=0, tiled=True)

    def half(disp, part):
        return element_forces(disp, connectivity, stiffness, levels, part, 2)

    outgoing = prep(block_slot, displacement, ref_pos, normals, places)
    first = None
    for step in range(STEPS):
        fresh = step == 0
        received = exchange(outgoing)
        if fresh:
            internal0, plan = element_forces(
                left(displacement),
                left(connectivity),
                stiffness,
                left(levels),
                0,
                2,
                (tile_count, left(tile_pairs)),
                places,
            )
        else:
            internal0 = half(displacement, 0)
        received, internal0, plan = lax.optimization_barrier((received, internal0, plan))
        near = swap([received[edge_slots]] * 4, sizes)
        if fresh:
            first = (received, near)
        total, slave_tab = own_contact(
            plan, first[0], None if fresh else received, win_start, win_len
        )
        box_force = far_contact(
            plan, meta, first[1], None if fresh else near, win_start, win_len, total, slave_tab
        )
        box_force, later = lax.optimization_barrier((box_force, displacement))
        returned = exchange(box_force)
        internal1 = half(later, 1)
        force, *sides = nodal_force(
            block_slot, meta, returned, (internal0, internal1), shared_nodes
        )
        if code is None:
            sides, lists = lax.optimization_barrier((sides, shared_nodes))
            code = inverse(meta, lists, blocks)
        incoming = swap(sides, sizes)
        last = step == STEPS - 1
        out = update(
            block_slot,
            force,
            incoming,
            code,
            inv_mass,
            velocity,
            displacement,
            ref_pos,
            0 if last else places,
        )
        velocity, displacement = out[0:2]
        if not last:
            outgoing = out[2]
    return (displacement, velocity)


def solution(mesh):
    split_last = P(None, AXES)
    placed = (
        split_last,
        split_last,
        split_last,
        split_last,
        split_last,
        split_last,
        P(None, None, AXES),
        P(AXES),
        split_last,
        P(AXES),
        P(AXES),
        split_last,
        P(AXES),
        P(AXES, None),
        P(AXES, None),
    )
    return jax.shard_map(
        body,
        mesh=mesh,
        in_specs=placed,
        out_specs=(split_last, split_last),
        check_vma=False,
    )
```

```python
import jax
import jax.numpy as jnp
from jax import lax
from jax.experimental import pallas as pl
from jax.experimental.pallas import tpu as pltpu
from jax.sharding import PartitionSpec as P

BLK = 128
CAP = 2
STEPS = 2
ROWS = 8
EBLK = 8
GROUP = 16
FIELD = 10

TIME_STEP = 0.5
PENALTY = 32.0
THICKNESS = 0.2

AXES = ("gx", "gy")
F32 = jnp.float32
BF16 = jnp.bfloat16
VMEM = pltpu.VMEM
SMEM = pltpu.SMEM


def vspec():
    return pl.BlockSpec(memory_space=VMEM)


def sspec():
    return pl.BlockSpec(memory_space=SMEM)


def limit(mebibytes):
    return pltpu.CompilerParams(vmem_limit_bytes=mebibytes << 20)


def left(x):
    return pltpu.with_memory_space_constraint(x, pltpu.HBM)


def load_rows(ref, place, first, count):
    rows = [ref[place, :, r * BLK : (r + 1) * BLK] for r in range(first, first + count)]
    return jnp.concatenate(rows, axis=0)


def store_rows(ref, place, rows):
    for r in range(rows.shape[0]):
        ref[place, :, r * BLK : (r + 1) * BLK] = rows[r : r + 1]


def lane_gather(data, index):
    return jnp.take_along_axis(data, index, axis=1, mode="promise_in_bounds")


def split(x):
    high = x.astype(BF16).astype(F32)
    return high, x - high


def prep_kernel(slot_ref, disp_ref, pos_ref, nrm_ref, out_ref):
    places = out_ref.shape[0]
    blocks = slot_ref.shape[0]
    if places != blocks:
        out_ref[...] = jnp.zeros(out_ref.shape, F32)
    for k in range(blocks):
        lanes = slice(k * BLK, (k + 1) * BLK)
        position = pos_ref[:, lanes] + disp_ref[0:3, lanes]
        both = jnp.concatenate([position, nrm_ref[:, lanes]], axis=0)
        store_rows(out_ref, slot_ref[k], both)


def prep(block_slot, displacement, ref_pos, normals, places):
    return pl.pallas_call(
        prep_kernel,
        out_shape=jax.ShapeDtypeStruct((places, 1, 6 * BLK), F32),
        in_specs=[sspec(), vspec(), vspec(), vspec()],
        out_specs=vspec(),
        compiler_params=limit(4),
        name="prep",
    )(left(block_slot), left(displacement), left(ref_pos), left(normals))


def fold_rows(tiles, row):
    low4 = row < 4
    low2 = (row & 2) == 0
    low1 = (row & 1) == 0
    four = []
    for i in range(4):
        a, b = tiles[i], tiles[i + 4]
        four.append(jnp.where(low4, a, b) + pltpu.roll(jnp.where(low4, b, a), 4, 0))
    two = []
    for i in range(2):
        a, b = four[i], four[i + 2]
        two.append(jnp.where(low2, a + pltpu.roll(a, 6, 0), b + pltpu.roll(b, 2, 0)))
    a, b = two
    return jnp.where(low1, a + pltpu.roll(a, 7, 0), b + pltpu.roll(b, 1, 0))


def element_kernel(*refs, origin, places):
    disp_ref, conn_ref, hbm_ref, yield_ref = refs[0:4]
    out_ref = refs[6] if places else refs[4]
    stiff_ref, sems = refs[-2:]
    wide = EBLK * BLK
    turns = out_ref.shape[0] // EBLK
    if places:
        plan_ref = refs[7]
        sort = tile_sorter(*refs[4:6], plan_ref, places)
        share = -(-refs[5].shape[1] // turns)

    def load(r):
        return pltpu.make_async_copy(
            hbm_ref.at[:, :, pl.ds(origin * BLK + r * wide, wide)], stiff_ref.at[r], sems.at[r]
        )

    for r in range(turns):
        load(r).start()
    row = lax.broadcasted_iota(jnp.int32, (ROWS, BLK), 0)
    row48 = lax.broadcasted_iota(jnp.int32, (48, BLK), 0)
    node = lax.broadcasted_iota(jnp.int32, (BLK, BLK), 0).astype(jnp.int16)
    unit = jnp.ones((), BF16)
    zero = jnp.zeros((), BF16)
    row48 = row48.astype(jnp.int16) & 3
    def one_block(r, d):
        k = r * EBLK + d
        lanes = pl.ds(pl.multiple_of((origin + k) * BLK, BLK), BLK)
        local = conn_ref[:, lanes] & (BLK - 1)
        index = jnp.concatenate([local, local], axis=0)
        dofs = []
        for t in range(3):
            first = jnp.broadcast_to(disp_ref[2 * t : 2 * t + 1, lanes], (4, BLK))
            second = jnp.broadcast_to(disp_ref[2 * t + 1 : 2 * t + 2, lanes], (4, BLK))
            dofs.append(lane_gather(jnp.concatenate([first, second], axis=0), index))
        trial = []
        for g in range(3):
            tiles = []
            for i in range(8 * g, 8 * g + 8):
                line = stiff_ref[r, i, :, d * BLK : (d + 1) * BLK].astype(F32)
                tiles.append(line[0:8] * dofs[0] + line[8:16] * dofs[1] + line[16:24] * dofs[2])
            trial.append(fold_rows(tiles, row))
        squared = trial[0] * trial[0] + trial[1] * trial[1] + trial[2] * trial[2]
        squared = squared + pltpu.roll(squared, 4, 0)
        squared = squared + pltpu.roll(squared, 2, 0)
        squared = squared + pltpu.roll(squared, 1, 0)
        level = yield_ref[pl.ds(origin + k, 1), :]
        factor = lax.rsqrt(1.0 + squared / (level * level))
        forces = jnp.concatenate([t * factor for t in trial], axis=0)
        high, low = split(forces)
        stacked = jnp.concatenate([high, low], axis=0).astype(BF16)
        small = local.astype(jnp.int16)
        total = jnp.zeros((48, BLK), F32)
        for a in range(4):
            corner = jnp.where(row48 == a, stacked, zero)
            picker = jnp.where(node == small[a : a + 1, :], unit, zero)
            total = total + lax.dot_general(
                corner, picker, (((1,), (1,)), ((), ())), preferred_element_type=F32
            )
        total = total[0:24] + total[24:48]
        pieces = []
        for t in range(3):
            x = total[8 * t : 8 * t + 8]
            x = x + pltpu.roll(x, 7, 0)
            x = x + pltpu.roll(x, 6, 0)
            pieces += [x[0:1], x[4:5]]
        out_ref[k] = jnp.concatenate(pieces + [jnp.zeros((2, BLK), F32)], axis=0)

    def body(r, own):
        load(r).wait()
        for d in range(EBLK):
            if places:
                for q in range(share * d // EBLK, share * (d + 1) // EBLK):
                    own = sort(r * share + q, own)
            one_block(r, d)
        return own

    own = lax.fori_loop(0, turns, body, jnp.int32(0))
    if places:
        plan_ref[plan_ref.shape[0] - 2] = own
        plan_ref[plan_ref.shape[0] - 1] = refs[4][0] - own


def element_forces(
    displacement, connectivity, stiffness, yield_force, part=0, parts=1, tiles=(), places=0
):
    nodes = displacement.shape[1]
    blocks = nodes // BLK // parts

    def kernel(*refs):
        element_kernel(*refs, origin=part * blocks, places=places)

    out = jax.ShapeDtypeStruct((blocks, ROWS, BLK), F32)
    out_spec = vspec()
    if places:
        out = [out, jax.ShapeDtypeStruct((2 * tiles[1].shape[1] + 8,), jnp.int32)]
        out_spec = [out_spec, sspec()]
    return pl.pallas_call(
        kernel,
        out_shape=out,
        in_specs=[vspec()] * 2
        + [pl.BlockSpec(memory_space=pltpu.HBM)]
        + [vspec()]
        + [sspec()] * len(tiles),
        out_specs=out_spec,
        scratch_shapes=[
            VMEM((blocks // EBLK, 24, 24, EBLK * BLK), BF16),
            pltpu.SemaphoreType.DMA((blocks // EBLK,)),
        ],
        cost_estimate=pl.CostEstimate(
            flops=2 * 576 * nodes, transcendentals=nodes, bytes_accessed=2 * 576 * nodes
        ),
        compiler_params=limit(12),
        name="element",
    )(displacement, connectivity, left(stiffness), yield_force, *tiles)


def packed(tile, slave, master):
    return tile | slave << FIELD | master << (2 * FIELD)


def unpacked(entry):
    mask = (1 << FIELD) - 1
    return entry & mask, (entry >> FIELD) & mask, entry >> (2 * FIELD)


def tile_sorter(count_ref, pairs_ref, plan_ref, places):
    tiles = pairs_ref.shape[1]
    plan_ref[0] = packed(0, 0, 0)
    plan_ref[tiles] = packed(0, 0, places)
    count = count_ref[0]

    def sort(t, own):
        live = t < count
        at = jnp.minimum(t, tiles - 1)
        master = pairs_ref[1, at]
        is_own = master < places
        where = jnp.where(is_own, own, tiles + t - own)
        where = jnp.where(live, where, 2 * tiles)
        plan_ref[where] = packed(at, pairs_ref[0, at], master)
        return own + jnp.where(jnp.logical_and(live, is_own), 1, 0)

    return sort


def master_entry(where, position, normal, master_tab, force_tab):
    zero1 = jnp.zeros((1, BLK), F32)
    zero2 = jnp.zeros((2, BLK), F32)
    n_high, n_low = split(normal)
    product = position * normal
    offset = THICKNESS + (product[0:1] + product[1:2] + product[2:3])
    o_high, o_rest = split(offset)
    o_mid, o_low = split(o_rest)
    negative = jnp.concatenate([-n_high, -n_low], axis=0)
    master_tab[where] = jnp.concatenate(
        [negative, negative, o_high, o_mid, o_low, zero1], axis=0
    ).astype(BF16)
    lines = [n_high, n_low, zero2]
    force_tab[where] = jnp.concatenate(lines + lines, axis=0).astype(BF16)


def run_tiles(
    plan_ref, first, number, base, start_ref, length_ref, slave_tab, master_tab, force_tab,
    total_ref, depth_ref,
):
    facet = lax.broadcasted_iota(jnp.int32, (BLK, 2 * BLK), 0).astype(jnp.int16)
    upper = lax.broadcasted_iota(jnp.int32, (16, BLK), 0) < 8
    blank = jnp.zeros((16, BLK), BF16)
    small = jnp.int16
    last = jnp.maximum(number - 1, 0)

    def at(group, d):
        i = group * GROUP + d
        return plan_ref[first + jnp.minimum(i, last)], i < number

    def depths(group):
        for d in range(0, GROUP, 2):
            facets, nodes = [], []
            for e in range(2):
                entry, _ = at(group, d + e)
                _, slave, master = unpacked(entry)
                facets.append(master_tab[master - base])
                nodes.append(slave_tab[slave])
            left = jnp.concatenate([nodes[0], blank], axis=0)
            right = jnp.concatenate([blank, nodes[1]], axis=0)
            depth_ref[d // 2] = lax.dot_general(
                jnp.concatenate(facets, axis=0),
                jnp.concatenate([left, right], axis=1),
                (((0,), (0,)), ((), ())),
                preferred_element_type=F32,
            )

    def body(group, carry):
        forces = []
        for d in range(0, GROUP, 2):
            starts, lengths, rows = [], [], []
            for e in range(2):
                entry, live = at(group, d + e)
                t, _, master = unpacked(entry)
                starts.append(start_ref[pl.ds(t, 1), :])
                lengths.append(jnp.where(live, length_ref[pl.ds(t, 1), :], 0))
                rows.append(force_tab[master - base])
            start = jnp.concatenate(starts, axis=1).astype(small)
            length = jnp.concatenate(lengths, axis=1).astype(small)
            inside = ((facet - start) & (BLK - 1)) < length
            pressure = jnp.maximum(depth_ref[d // 2], 0.0)
            high = pressure.astype(BF16)
            low = (pressure - high.astype(F32)).astype(BF16)
            high = jnp.where(inside, high, jnp.zeros((), BF16))
            low = jnp.where(inside, low, jnp.zeros((), BF16))
            both = jnp.where(upper, rows[0], rows[1])
            forces.append(
                jnp.dot(
                    jnp.concatenate([both, both], axis=1),
                    jnp.concatenate([high, low], axis=0),
                    preferred_element_type=F32,
                )
            )
        depths(group + 1)
        for d in range(GROUP):
            _, slave, _ = unpacked(at(group, d)[0])
            e = d % 2
            part = forces[d // 2][8 * e : 8 * e + 8, e * BLK : (e + 1) * BLK]
            total_ref[slave] = total_ref[slave] + part
        return carry

    depths(0)
    lax.fori_loop(0, (number + GROUP - 1) // GROUP, body, 0)


def own_kernel(plan_ref, recv_ref, *refs, fresh):
    pos_ref = recv_ref if fresh else refs[0]
    refs = refs if fresh else refs[1:]
    start_ref, length_ref, total_ref, slave_tab, master_tab, force_tab, depth_ref = refs
    ones = jnp.ones((3, BLK), F32)
    zero1 = jnp.zeros((1, BLK), F32)
    places = recv_ref.shape[0]

    def entry(p, carry):
        position = load_rows(pos_ref, p, 0, 3)
        p_high, p_low = split(position)
        slave_tab[p] = jnp.concatenate(
            [p_high, p_high, p_low, p_low, ones, zero1], axis=0
        ).astype(BF16)
        master_entry(p, position, load_rows(recv_ref, p, 3, 3), master_tab, force_tab)
        total_ref[p] = jnp.zeros((ROWS, BLK), F32)
        return carry

    lax.fori_loop(0, places, entry, 0, unroll=8)
    run_tiles(
        plan_ref, 0, plan_ref[plan_ref.shape[0] - 2], 0, start_ref, length_ref, slave_tab, master_tab, force_tab,
        total_ref, depth_ref,
    )


def far_kernel(plan_ref, meta_ref, *refs, edges, fresh):
    edge_refs = refs[0:4]
    pos_refs = edge_refs if fresh else refs[4:8]
    refs = refs[4:] if fresh else refs[8:]
    start_ref, length_ref, own_ref, slave_tab, out_ref = refs[0:5]
    master_tab, force_tab, total_ref, depth_ref = refs[5:9]
    places = own_ref.shape[0]
    total_ref[...] = own_ref[...]
    for side in range(4):
        valid = meta_ref[2 + side] > 0
        base = (side ^ meta_ref[side // 2]) * edges
        for e in range(edges):
            normal = jnp.where(valid, load_rows(edge_refs[side], e, 3, 3), 0.0)
            position = jnp.where(valid, load_rows(pos_refs[side], e, 0, 3), 0.0)
            master_entry(base + e, position, normal, master_tab, force_tab)
    run_tiles(
        plan_ref, start_ref.shape[0], plan_ref[plan_ref.shape[0] - 1], places, start_ref, length_ref,
        slave_tab, master_tab, force_tab, total_ref, depth_ref,
    )

    def finish(p, carry):
        tile = total_ref[p]
        store_rows(out_ref, p, (PENALTY / BLK) * (tile[0:3] + tile[3:6]))
        return carry

    lax.fori_loop(0, places, finish, 0, unroll=8)


def edge_kernel(slot_ref, recv_ref, out_ref):
    for e in range(slot_ref.shape[0]):
        out_ref[e] = recv_ref[slot_ref[e]]


def edge_rows(edge_slots, received):
    return pl.pallas_call(
        edge_kernel,
        out_shape=jax.ShapeDtypeStruct((edge_slots.shape[0],) + received.shape[1:], F32),
        in_specs=[sspec(), vspec()],
        out_specs=vspec(),
        compiler_params=limit(1),
        name="edges",
    )(edge_slots, received)


def tile_cost(tiles):
    return pl.CostEstimate(
        flops=tiles * BLK * BLK * 64, transcendentals=0, bytes_accessed=tiles * BLK * 8
    )


def own_contact(plan, received, positions, start, length):
    places = received.shape[0]
    fresh = positions is None
    arrays = [received] + ([] if fresh else [positions]) + [start, length]

    def kernel(*refs):
        own_kernel(*refs, fresh=fresh)

    return pl.pallas_call(
        kernel,
        out_shape=[
            jax.ShapeDtypeStruct((places, ROWS, BLK), F32),
            jax.ShapeDtypeStruct((places, 16, BLK), BF16),
        ],
        in_specs=[sspec()] + [vspec()] * len(arrays),
        out_specs=[vspec()] * 2,
        scratch_shapes=[
            VMEM((places, 16, BLK), BF16),
            VMEM((places, 16, BLK), BF16),
            VMEM((GROUP // 2, BLK, 2 * BLK), F32),
        ],
        cost_estimate=tile_cost(start.shape[0] // 2),
        compiler_params=limit(8),
        name="own_contact",
    )(plan, *arrays)


def far_contact(plan, meta, edges, edge_positions, start, length, total, slave_tab):
    places = total.shape[0]
    fresh = edge_positions is None
    edge_count = edges[0].shape[0]
    arrays = list(edges) + ([] if fresh else list(edge_positions))
    arrays += [start, length, total, slave_tab]

    def kernel(*refs):
        far_kernel(*refs, edges=edge_count, fresh=fresh)

    return pl.pallas_call(
        kernel,
        out_shape=jax.ShapeDtypeStruct((places, 1, 3 * BLK), F32),
        in_specs=[sspec()] * 2 + [vspec()] * len(arrays),
        out_specs=vspec(),
        scratch_shapes=[
            VMEM((4 * edge_count, 16, BLK), BF16),
            VMEM((4 * edge_count, 16, BLK), BF16),
            VMEM((places, ROWS, BLK), F32),
            VMEM((GROUP // 2, BLK, 2 * BLK), F32),
        ],
        cost_estimate=tile_cost(start.shape[0] // 2),
        compiler_params=limit(8),
        name="far_contact",
    )(plan, meta, *arrays)


def side_list(list_ref, meta_ref, side):
    axis = side // 2
    low = list_ref[2 * axis : 2 * axis + 1, :]
    high = list_ref[2 * axis + 1 : 2 * axis + 2, :]
    return jnp.where(meta_ref[axis] != side % 2, high, low)


def inverse_kernel(meta_ref, list_ref, out_ref):
    blocks = out_ref.shape[0]
    block_id = lax.broadcasted_iota(jnp.int32, (blocks, BLK), 0)
    lane_id = lax.broadcasted_iota(jnp.int32, (BLK, BLK), 0)
    rank = (lax.broadcasted_iota(jnp.int32, (BLK, BLK), 1) + 1).astype(F32)
    code = jnp.full((blocks, BLK), -1, jnp.int32)
    for side in range(4):
        nodes = side_list(list_ref, meta_ref, side)
        valid = meta_ref[2 + side] > 0
        in_block = jnp.where(
            jnp.logical_and(block_id == nodes // BLK, valid), 1.0, 0.0
        ).astype(BF16)
        at_lane = jnp.where(lane_id == (nodes & (BLK - 1)), rank, 0.0).astype(BF16)
        found = lax.dot_general(
            in_block, at_lane, (((1,), (1,)), ((), ())), preferred_element_type=F32
        ).astype(jnp.int32)
        code = jnp.where(found > 0, found - 1 + side * BLK, code)
    out_ref[...] = code


def inverse(meta, lists, blocks):
    return pl.pallas_call(
        inverse_kernel,
        out_shape=jax.ShapeDtypeStruct((blocks, BLK), jnp.int32),
        in_specs=[sspec(), vspec()],
        out_specs=vspec(),
        compiler_params=limit(2),
        name="inverse",
    )(meta, lists)


def force_kernel(slot_ref, meta_ref, back_ref, first_ref, second_ref, list_ref, force_ref, *side_refs):
    half = first_ref.shape[0]
    blocks = slot_ref.shape[0]
    pad = jnp.zeros((ROWS - 3, BLK), F32)
    lanes = []
    owners = []
    for side in range(4):
        nodes = jnp.broadcast_to(side_list(list_ref, meta_ref, side), (ROWS, BLK))
        lanes.append(nodes & (BLK - 1))
        owners.append(nodes // BLK)
    sums = [jnp.zeros((ROWS, BLK), F32) for _ in range(4)]
    for k in range(blocks):
        internal = first_ref[k] if k < half else second_ref[k - half]
        tile = jnp.concatenate([load_rows(back_ref, slot_ref[k], 0, 3), pad], axis=0) - internal
        force_ref[k] = tile
    for side in range(4):
        for k in range(blocks):
            sums[side] = jnp.where(
                owners[side] == k, lane_gather(force_ref[k], lanes[side]), sums[side]
            )
    for side in range(4):
        side_refs[side][...] = sums[side]


def nodal_force(block_slot, meta, returned, internal, lists):
    blocks = 2 * internal[0].shape[0]
    return pl.pallas_call(
        force_kernel,
        out_shape=[jax.ShapeDtypeStruct((blocks, ROWS, BLK), F32)]
        + [jax.ShapeDtypeStruct((ROWS, BLK), F32)] * 4,
        in_specs=[sspec()] * 2 + [vspec()] * 4,
        out_specs=[vspec()] * 5,
        compiler_params=limit(4),
        name="force",
    )(block_slot, meta, returned, *internal, lists)


def update_kernel(
    slot_ref,
    force_ref,
    near0_ref,
    near1_ref,
    near2_ref,
    near3_ref,
    code_ref,
    mass_ref,
    vel_ref,
    disp_ref,
    pos_ref,
    vel_out,
    disp_out,
    *send_refs,
):
    blocks = force_ref.shape[0]
    near = [r[...] for r in (near0_ref, near1_ref, near2_ref, near3_ref)]
    if send_refs and send_refs[0].shape[0] != blocks:
        send_refs[0][...] = jnp.zeros(send_refs[0].shape, F32)
    for k in range(blocks):
        lanes = slice(k * BLK, (k + 1) * BLK)
        code = jnp.broadcast_to(code_ref[k : k + 1, :], (ROWS, BLK))
        index = code & (BLK - 1)
        extra = jnp.zeros((ROWS, BLK), F32)
        for side in range(4):
            inside = jnp.logical_and(code >= side * BLK, code < (side + 1) * BLK)
            extra = jnp.where(inside, lane_gather(near[side], index), extra)
        assembled = (force_ref[k] + extra)[0:6]
        vel = vel_ref[:, lanes] + TIME_STEP * mass_ref[:, lanes] * assembled
        disp = disp_ref[:, lanes] + TIME_STEP * vel
        vel_out[:, lanes] = vel
        disp_out[:, lanes] = disp
        if send_refs:
            store_rows(send_refs[0], slot_ref[k], pos_ref[:, lanes] + disp[0:3])


def update(block_slot, force, near, code, inv_mass, velocity, displacement, ref_pos, places):
    nodes = displacement.shape[1]
    out = [jax.ShapeDtypeStruct((6, nodes), F32)] * 2
    if places:
        out = out + [jax.ShapeDtypeStruct((places, 1, 3 * BLK), F32)]
    return pl.pallas_call(
        update_kernel,
        out_shape=out,
        in_specs=[sspec()] + [vspec()] * 10,
        out_specs=[vspec()] * len(out),
        compiler_params=limit(6),
        name="update",
    )(block_slot, force, *near, code, inv_mass, velocity, displacement, ref_pos)


def pair_lists(sizes):
    rows, columns = sizes
    near = [[(i, i ^ 1) for i in range(size)] for size in sizes]
    other = [(i, (i + 1) % rows if i % 2 else (i - 1) % rows) for i in range(rows)]
    flat = []
    for i in range(rows):
        for j in range(columns):
            k = j + 1 if j % 2 else j - 1
            inside = 0 <= k < columns
            flat.append((i * columns + j, i * columns + k if inside else (i ^ 1) * columns + j))
    return [("gx", near[0]), ("gx", other), ("gy", near[1]), (AXES, flat)]


def swap(values, sizes):
    moved = [
        lax.ppermute(value, axis, pairs)
        for value, (axis, pairs) in reversed(list(zip(values, pair_lists(sizes))))
    ]
    return moved[::-1]


def body(
    displacement,
    velocity,
    ref_pos,
    normals,
    inv_mass,
    connectivity,
    stiffness,
    yield_force,
    shared_nodes,
    block_slot,
    edge_slots,
    tile_pairs,
    tile_count,
    win_start,
    win_len,
):
    sizes = [lax.axis_size(axis) for axis in AXES]
    if any(size % 2 for size in sizes):
        raise ValueError("odd axis")
    places = sizes[0] * sizes[1] * CAP
    blocks = displacement.shape[1] // BLK
    edge_count = edge_slots.shape[0]
    if max(tile_pairs.shape[1], places + 4 * edge_count) >= 1 << FIELD:
        raise ValueError("field width")
    at = [lax.axis_index(axis) for axis in AXES]
    odd = [i % 2 for i in at]
    inner = [((i > 0) & (i < size - 1)).astype(jnp.int32) for i, size in zip(at, sizes)]
    slot = jnp.arange(8, dtype=jnp.int32)
    meta = jnp.ones((8,), jnp.int32)
    for i, value in ((0, 1 - odd[0]), (1, 1 - odd[1]), (3, inner[0]), (5, inner[1])):
        meta = jnp.where(slot == i, value, meta)
    levels = yield_force.reshape(-1, BLK)
    plan = None
    code = None

    def exchange(blocks_out):
        return lax.all_to_all(blocks_out, AXES, split_axis=0, concat_axis=0, tiled=True)

    def half(disp, part):
        return element_forces(disp, connectivity, stiffness, levels, part, 2)

    outgoing = prep(block_slot, displacement, ref_pos, normals, places)
    first = None
    for step in range(STEPS):
        fresh = step == 0
        received = exchange(outgoing)
        if fresh:
            internal0, plan = element_forces(
                left(displacement),
                left(connectivity),
                stiffness,
                left(levels),
                0,
                2,
                (tile_count, left(tile_pairs)),
                places,
            )
        else:
            internal0 = half(displacement, 0)
        received, internal0, plan = lax.optimization_barrier((received, internal0, plan))
        near = swap([edge_rows(edge_slots, received)] * 4, sizes)
        if fresh:
            first = (received, near)
        total, slave_tab = own_contact(
            plan, first[0], None if fresh else received, win_start, win_len
        )
        box_force = far_contact(
            plan, meta, first[1], None if fresh else near, win_start, win_len, total, slave_tab
        )
        box_force, later = lax.optimization_barrier((box_force, displacement))
        returned = exchange(box_force)
        internal1 = half(later, 1)
        force, *sides = nodal_force(
            block_slot, meta, returned, (internal0, internal1), shared_nodes
        )
        if code is None:
            sides, lists = lax.optimization_barrier((sides, shared_nodes))
            code = inverse(meta, lists, blocks)
        incoming = swap(sides, sizes)
        last = step == STEPS - 1
        out = update(
            block_slot,
            force,
            incoming,
            code,
            inv_mass,
            velocity,
            displacement,
            ref_pos,
            0 if last else places,
        )
        velocity, displacement = out[0:2]
        if not last:
            outgoing = out[2]
    return (displacement, velocity)


def solution(mesh):
    split_last = P(None, AXES)
    placed = (
        split_last,
        split_last,
        split_last,
        split_last,
        split_last,
        split_last,
        P(None, None, AXES),
        P(AXES),
        split_last,
        P(AXES),
        P(AXES),
        split_last,
        P(AXES),
        P(AXES, None),
        P(AXES, None),
    )
    return jax.shard_map(
        body,
        mesh=mesh,
        in_specs=placed,
        out_specs=(split_last, split_last),
        check_vma=False,
    )
```

```python
import jax
import jax.numpy as jnp
from jax import lax
from jax.experimental import pallas as pl
from jax.experimental.pallas import tpu as pltpu
from jax.sharding import PartitionSpec as P

BLK = 128
CAP = 2
STEPS = 2
ROWS = 8
EBLK = 8
GROUP = 16
FIELD = 10
TAIL = 16
PART = 16

TIME_STEP = 0.5
PENALTY = 32.0
THICKNESS = 0.2

AXES = ("gx", "gy")
F32 = jnp.float32
BF16 = jnp.bfloat16
VMEM = pltpu.VMEM
SMEM = pltpu.SMEM


def vspec():
    return pl.BlockSpec(memory_space=VMEM)


def sspec():
    return pl.BlockSpec(memory_space=SMEM)


def limit(mebibytes):
    return pltpu.CompilerParams(vmem_limit_bytes=mebibytes << 20)


def left(x):
    return pltpu.with_memory_space_constraint(x, pltpu.HBM)


def load_rows(ref, place, first, count):
    rows = [ref[place, :, r * BLK : (r + 1) * BLK] for r in range(first, first + count)]
    return jnp.concatenate(rows, axis=0)


def store_rows(ref, place, rows):
    for r in range(rows.shape[0]):
        ref[place, :, r * BLK : (r + 1) * BLK] = rows[r : r + 1]


def lane_gather(data, index):
    return jnp.take_along_axis(data, index, axis=1, mode="promise_in_bounds")


def split(x):
    high = x.astype(BF16).astype(F32)
    return high, x - high


def prep_kernel(slot_ref, disp_ref, pos_ref, nrm_ref, out_ref):
    places = out_ref.shape[0]
    blocks = slot_ref.shape[0]
    if places != blocks:
        out_ref[...] = jnp.zeros(out_ref.shape, F32)
    for k in range(blocks):
        lanes = slice(k * BLK, (k + 1) * BLK)
        position = pos_ref[:, lanes] + disp_ref[0:3, lanes]
        both = jnp.concatenate([position, nrm_ref[:, lanes]], axis=0)
        store_rows(out_ref, slot_ref[k], both)


def prep(block_slot, displacement, ref_pos, normals, places):
    return pl.pallas_call(
        prep_kernel,
        out_shape=jax.ShapeDtypeStruct((places, 1, 6 * BLK), F32),
        in_specs=[sspec(), vspec(), vspec(), vspec()],
        out_specs=vspec(),
        compiler_params=limit(4),
        name="prep",
    )(left(block_slot), left(displacement), left(ref_pos), left(normals))


def fold_rows(tiles, row):
    low4 = row < 4
    low2 = (row & 2) == 0
    low1 = (row & 1) == 0
    four = []
    for i in range(4):
        a, b = tiles[i], tiles[i + 4]
        four.append(jnp.where(low4, a, b) + pltpu.roll(jnp.where(low4, b, a), 4, 0))
    two = []
    for i in range(2):
        a, b = four[i], four[i + 2]
        two.append(jnp.where(low2, a + pltpu.roll(a, 6, 0), b + pltpu.roll(b, 2, 0)))
    a, b = two
    return jnp.where(low1, a + pltpu.roll(a, 7, 0), b + pltpu.roll(b, 1, 0))


def element_kernel(*refs, origin, places):
    disp_ref, conn_ref, hbm_ref, yield_ref = refs[0:4]
    out_ref = refs[7] if places else refs[4]
    stiff_ref, sems = refs[-2:]
    wide = EBLK * BLK
    turns = out_ref.shape[0] // EBLK
    if places:
        plan_ref = refs[8]
        sort = tile_sorter(*refs[4:6], plan_ref, places)
        for i in range(refs[6].shape[0]):
            plan_ref[plan_ref.shape[0] - TAIL + i] = refs[6][i]
        share = -(-refs[5].shape[1] // turns)

    def load(r):
        return pltpu.make_async_copy(
            hbm_ref.at[:, :, pl.ds(origin * BLK + r * wide, wide)], stiff_ref.at[r], sems.at[r]
        )

    for r in range(turns):
        load(r).start()
    row = lax.broadcasted_iota(jnp.int32, (ROWS, BLK), 0)
    row48 = lax.broadcasted_iota(jnp.int32, (48, BLK), 0)
    node = lax.broadcasted_iota(jnp.int32, (BLK, BLK), 0).astype(jnp.int16)
    unit = jnp.ones((), BF16)
    zero = jnp.zeros((), BF16)
    row48 = row48.astype(jnp.int16) & 3
    def one_block(r, d):
        k = r * EBLK + d
        lanes = pl.ds(pl.multiple_of((origin + k) * BLK, BLK), BLK)
        local = conn_ref[:, lanes] & (BLK - 1)
        index = jnp.concatenate([local, local], axis=0)
        dofs = []
        for t in range(3):
            first = jnp.broadcast_to(disp_ref[2 * t : 2 * t + 1, lanes], (4, BLK))
            second = jnp.broadcast_to(disp_ref[2 * t + 1 : 2 * t + 2, lanes], (4, BLK))
            dofs.append(lane_gather(jnp.concatenate([first, second], axis=0), index))
        trial = []
        for g in range(3):
            tiles = []
            for i in range(8 * g, 8 * g + 8):
                line = stiff_ref[r, i, :, d * BLK : (d + 1) * BLK].astype(F32)
                tiles.append(line[0:8] * dofs[0] + line[8:16] * dofs[1] + line[16:24] * dofs[2])
            trial.append(fold_rows(tiles, row))
        squared = trial[0] * trial[0] + trial[1] * trial[1] + trial[2] * trial[2]
        squared = squared + pltpu.roll(squared, 4, 0)
        squared = squared + pltpu.roll(squared, 2, 0)
        squared = squared + pltpu.roll(squared, 1, 0)
        level = yield_ref[pl.ds(origin + k, 1), :]
        factor = lax.rsqrt(1.0 + squared / (level * level))
        forces = jnp.concatenate([t * factor for t in trial], axis=0)
        high, low = split(forces)
        stacked = jnp.concatenate([high, low], axis=0).astype(BF16)
        small = local.astype(jnp.int16)
        total = jnp.zeros((48, BLK), F32)
        for a in range(4):
            corner = jnp.where(row48 == a, stacked, zero)
            picker = jnp.where(node == small[a : a + 1, :], unit, zero)
            total = total + lax.dot_general(
                corner, picker, (((1,), (1,)), ((), ())), preferred_element_type=F32
            )
        total = total[0:24] + total[24:48]
        pieces = []
        for t in range(3):
            x = total[8 * t : 8 * t + 8]
            x = x + pltpu.roll(x, 7, 0)
            x = x + pltpu.roll(x, 6, 0)
            pieces += [x[0:1], x[4:5]]
        out_ref[k] = jnp.concatenate(pieces + [jnp.zeros((2, BLK), F32)], axis=0)

    def body(r, own):
        load(r).wait()
        for d in range(EBLK):
            if places:
                for q in range(share * d // EBLK, share * (d + 1) // EBLK):
                    own = sort(r * share + q, own)
            one_block(r, d)
        return own

    own = lax.fori_loop(0, turns, body, jnp.int32(0))
    if places:
        plan_ref[plan_ref.shape[0] - TAIL - 2] = own
        plan_ref[plan_ref.shape[0] - TAIL - 1] = refs[4][0] - own


def element_forces(
    displacement, connectivity, stiffness, yield_force, part=0, parts=1, tiles=(), places=0
):
    nodes = displacement.shape[1]
    blocks = nodes // BLK // parts

    def kernel(*refs):
        element_kernel(*refs, origin=part * blocks, places=places)

    out = jax.ShapeDtypeStruct((blocks, ROWS, BLK), F32)
    out_spec = vspec()
    if places:
        out = [out, jax.ShapeDtypeStruct((2 * tiles[1].shape[1] + 2 * TAIL,), jnp.int32)]
        out_spec = [out_spec, sspec()]
    return pl.pallas_call(
        kernel,
        out_shape=out,
        in_specs=[vspec()] * 2
        + [pl.BlockSpec(memory_space=pltpu.HBM)]
        + [vspec()]
        + [sspec()] * len(tiles),
        out_specs=out_spec,
        scratch_shapes=[
            VMEM((blocks // EBLK, 24, 24, EBLK * BLK), BF16),
            pltpu.SemaphoreType.DMA((blocks // EBLK,)),
        ],
        cost_estimate=pl.CostEstimate(
            flops=2 * 576 * nodes, transcendentals=nodes, bytes_accessed=2 * 576 * nodes
        ),
        compiler_params=limit(12),
        name="element",
    )(displacement, connectivity, left(stiffness), yield_force, *tiles)


def packed(tile, slave, master):
    return tile | slave << FIELD | master << (2 * FIELD)


def unpacked(entry):
    mask = (1 << FIELD) - 1
    return entry & mask, (entry >> FIELD) & mask, entry >> (2 * FIELD)


def tile_sorter(count_ref, pairs_ref, plan_ref, places):
    tiles = pairs_ref.shape[1]
    plan_ref[0] = packed(0, 0, 0)
    plan_ref[tiles] = packed(0, 0, places)
    count = count_ref[0]

    def sort(t, own):
        live = t < count
        at = jnp.minimum(t, tiles - 1)
        master = pairs_ref[1, at]
        is_own = master < places
        where = jnp.where(is_own, own, tiles + t - own)
        where = jnp.where(live, where, 2 * tiles)
        plan_ref[where] = packed(at, pairs_ref[0, at], master)
        return own + jnp.where(jnp.logical_and(live, is_own), 1, 0)

    return sort


def master_entry(where, position, normal, master_tab, force_tab):
    zero1 = jnp.zeros((1, BLK), F32)
    zero2 = jnp.zeros((2, BLK), F32)
    n_high, n_low = split(normal)
    product = position * normal
    offset = THICKNESS + (product[0:1] + product[1:2] + product[2:3])
    o_high, o_rest = split(offset)
    o_mid, o_low = split(o_rest)
    negative = jnp.concatenate([-n_high, -n_low], axis=0)
    master_tab[where] = jnp.concatenate(
        [negative, negative, o_high, o_mid, o_low, zero1], axis=0
    ).astype(BF16)
    lines = [n_high, n_low, zero2]
    force_tab[where] = jnp.concatenate(lines + lines, axis=0).astype(BF16)


def run_tiles(
    plan_ref, first, number, facet_entry, start_ref, length_ref, slave_tab, master_tab, force_tab,
    total_ref, depth_ref,
):
    facet = lax.broadcasted_iota(jnp.int32, (BLK, 2 * BLK), 0).astype(jnp.int16)
    upper = lax.broadcasted_iota(jnp.int32, (16, BLK), 0) < 8
    blank = jnp.zeros((16, BLK), BF16)
    small = jnp.int16
    last = jnp.maximum(number - 1, 0)

    def at(group, d):
        i = group * GROUP + d
        return plan_ref[first + jnp.minimum(i, last)], i < number

    def depths(group):
        for d in range(0, GROUP, 2):
            facets, nodes = [], []
            for e in range(2):
                entry, _ = at(group, d + e)
                _, slave, master = unpacked(entry)
                facets.append(master_tab[facet_entry(master)[0]])
                nodes.append(slave_tab[slave])
            left = jnp.concatenate([nodes[0], blank], axis=0)
            right = jnp.concatenate([blank, nodes[1]], axis=0)
            depth_ref[d // 2] = lax.dot_general(
                jnp.concatenate(facets, axis=0),
                jnp.concatenate([left, right], axis=1),
                (((0,), (0,)), ((), ())),
                preferred_element_type=F32,
            )

    def body(group, carry):
        forces = []
        for d in range(0, GROUP, 2):
            starts, lengths, rows = [], [], []
            for e in range(2):
                entry, live = at(group, d + e)
                t, _, master = unpacked(entry)
                where, known = facet_entry(master)
                live = jnp.logical_and(live, known)
                starts.append(start_ref[pl.ds(t, 1), :])
                lengths.append(jnp.where(live, length_ref[pl.ds(t, 1), :], 0))
                rows.append(force_tab[where])
            start = jnp.concatenate(starts, axis=1).astype(small)
            length = jnp.concatenate(lengths, axis=1).astype(small)
            inside = ((facet - start) & (BLK - 1)) < length
            pressure = jnp.maximum(depth_ref[d // 2], 0.0)
            high = pressure.astype(BF16)
            low = (pressure - high.astype(F32)).astype(BF16)
            high = jnp.where(inside, high, jnp.zeros((), BF16))
            low = jnp.where(inside, low, jnp.zeros((), BF16))
            both = jnp.where(upper, rows[0], rows[1])
            forces.append(
                jnp.dot(
                    jnp.concatenate([both, both], axis=1),
                    jnp.concatenate([high, low], axis=0),
                    preferred_element_type=F32,
                )
            )
        depths(group + 1)
        for d in range(GROUP):
            _, slave, _ = unpacked(at(group, d)[0])
            e = d % 2
            part = forces[d // 2][8 * e : 8 * e + 8, e * BLK : (e + 1) * BLK]
            total_ref[slave] = total_ref[slave] + part
        return carry

    depths(0)
    lax.fori_loop(0, (number + GROUP - 1) // GROUP, body, 0)


def own_kernel(table_ref, recv_ref, *refs, fresh):
    pos_ref = recv_ref if fresh else refs[0]
    refs = refs if fresh else refs[1:]
    start_ref, length_ref, total_ref, slave_tab, master_tab, force_tab, depth_ref = refs[:7]
    plan_ref, sem = refs[7:]
    load = pltpu.make_async_copy(table_ref, plan_ref, sem)
    load.start()
    ones = jnp.ones((3, BLK), F32)
    zero1 = jnp.zeros((1, BLK), F32)
    places = recv_ref.shape[0]

    def entry(p, carry):
        position = load_rows(pos_ref, p, 0, 3)
        p_high, p_low = split(position)
        slave_tab[p] = jnp.concatenate(
            [p_high, p_high, p_low, p_low, ones, zero1], axis=0
        ).astype(BF16)
        master_entry(p, position, load_rows(recv_ref, p, 3, 3), master_tab, force_tab)
        total_ref[p] = jnp.zeros((ROWS, BLK), F32)
        return carry

    lax.fori_loop(0, places, entry, 0, unroll=8)
    load.wait()
    run_tiles(
        plan_ref, 0, plan_ref[plan_ref.shape[0] - TAIL - 2], lambda m: (m, True), start_ref, length_ref, slave_tab, master_tab, force_tab,
        total_ref, depth_ref,
    )


def far_kernel(table_ref, *refs, edges, fresh):
    edge_refs = refs[0:4]
    pos_refs = edge_refs if fresh else refs[4:8]
    refs = refs[4:] if fresh else refs[8:]
    start_ref, length_ref, own_ref, slave_tab, out_ref = refs[0:5]
    master_tab, force_tab, total_ref, depth_ref, plan_ref, sem = refs[5:11]
    load = pltpu.make_async_copy(table_ref, plan_ref, sem)
    load.start()
    tail = plan_ref.shape[0] - TAIL
    places = own_ref.shape[0]
    total_ref[...] = own_ref[...]
    for side in range(4):
        for e in range(edges):
            normal = load_rows(edge_refs[side], e, 3, 3)
            position = load_rows(pos_refs[side], e, 0, 3)
            master_entry(side * edges + e, position, normal, master_tab, force_tab)
    load.wait()
    log = edges.bit_length() - 1
    power = edges == 1 << log

    def facet_entry(master):
        entry = master - places
        side = entry >> log if power else entry // edges
        pairing = side ^ jnp.where(side < 2, plan_ref[tail], plan_ref[tail + 1])
        return entry + edges * (pairing - side), plan_ref[tail + 2 + pairing] > 0

    run_tiles(
        plan_ref, start_ref.shape[0], plan_ref[tail - 1], facet_entry, start_ref, length_ref,
        slave_tab, master_tab, force_tab, total_ref, depth_ref,
    )

    def finish(p, carry):
        tile = total_ref[p]
        store_rows(out_ref, p, (PENALTY / BLK) * (tile[0:3] + tile[3:6]))
        return carry

    lax.fori_loop(0, places, finish, 0, unroll=8)


def edge_kernel(slot_ref, recv_ref, out_ref):
    for e in range(slot_ref.shape[0]):
        out_ref[e] = recv_ref[slot_ref[e]]


def edge_rows(edge_slots, received):
    return pl.pallas_call(
        edge_kernel,
        out_shape=jax.ShapeDtypeStruct((edge_slots.shape[0],) + received.shape[1:], F32),
        in_specs=[sspec(), vspec()],
        out_specs=vspec(),
        compiler_params=limit(1),
        name="edges",
    )(edge_slots, received)


def tile_cost(tiles):
    return pl.CostEstimate(
        flops=tiles * BLK * BLK * 64, transcendentals=0, bytes_accessed=tiles * BLK * 8
    )


def own_contact(plan, received, positions, start, length):
    places = received.shape[0]
    fresh = positions is None
    arrays = [received] + ([] if fresh else [positions]) + [start, length]

    def kernel(*refs):
        own_kernel(*refs, fresh=fresh)

    return pl.pallas_call(
        kernel,
        out_shape=[
            jax.ShapeDtypeStruct((places, ROWS, BLK), F32),
            jax.ShapeDtypeStruct((places, 16, BLK), BF16),
        ],
        in_specs=[pl.BlockSpec(memory_space=pl.ANY)] + [vspec()] * len(arrays),
        out_specs=[vspec()] * 2,
        scratch_shapes=[
            VMEM((places, 16, BLK), BF16),
            VMEM((places, 16, BLK), BF16),
            VMEM((GROUP // 2, BLK, 2 * BLK), F32),
            SMEM(plan.shape, jnp.int32),
            pltpu.SemaphoreType.DMA(()),
        ],
        cost_estimate=tile_cost(start.shape[0] // 2),
        compiler_params=limit(8),
        name="own_contact",
    )(plan, *arrays)


def far_contact(plan, edges, edge_positions, start, length, total, slave_tab):
    places = total.shape[0]
    fresh = edge_positions is None
    edge_count = edges[0].shape[0]
    arrays = list(edges) + ([] if fresh else list(edge_positions))
    arrays += [start, length, total, slave_tab]

    def kernel(*refs):
        far_kernel(*refs, edges=edge_count, fresh=fresh)

    return pl.pallas_call(
        kernel,
        out_shape=jax.ShapeDtypeStruct((places, 1, 3 * BLK), F32),
        in_specs=[pl.BlockSpec(memory_space=pl.ANY)] + [vspec()] * len(arrays),
        out_specs=vspec(),
        scratch_shapes=[
            VMEM((4 * edge_count, 16, BLK), BF16),
            VMEM((4 * edge_count, 16, BLK), BF16),
            VMEM((places, ROWS, BLK), F32),
            VMEM((GROUP // 2, BLK, 2 * BLK), F32),
            SMEM(plan.shape, jnp.int32),
            pltpu.SemaphoreType.DMA(()),
        ],
        cost_estimate=tile_cost(start.shape[0] // 2),
        compiler_params=limit(8),
        name="far_contact",
    )(plan, *arrays)


def side_list(list_ref, meta_ref, side):
    axis = side // 2
    low = list_ref[2 * axis : 2 * axis + 1, :]
    high = list_ref[2 * axis + 1 : 2 * axis + 2, :]
    return jnp.where(meta_ref[axis] != side % 2, high, low)


def inverse_kernel(meta_ref, list_ref, out_ref):
    blocks = out_ref.shape[0]
    block_id = lax.broadcasted_iota(jnp.int32, (blocks, BLK), 0)
    lane_id = lax.broadcasted_iota(jnp.int32, (BLK, BLK), 0)
    rank = (lax.broadcasted_iota(jnp.int32, (BLK, BLK), 1) + 1).astype(F32)
    code = jnp.full((blocks, BLK), -1, jnp.int32)
    for side in range(4):
        nodes = side_list(list_ref, meta_ref, side)
        valid = meta_ref[2 + side] > 0
        in_block = jnp.where(
            jnp.logical_and(block_id == nodes // BLK, valid), 1.0, 0.0
        ).astype(BF16)
        at_lane = jnp.where(lane_id == (nodes & (BLK - 1)), rank, 0.0).astype(BF16)
        found = lax.dot_general(
            in_block, at_lane, (((1,), (1,)), ((), ())), preferred_element_type=F32
        ).astype(jnp.int32)
        code = jnp.where(found > 0, found - 1 + side * BLK, code)
    out_ref[...] = code


def inverse(meta, lists, blocks):
    return pl.pallas_call(
        inverse_kernel,
        out_shape=jax.ShapeDtypeStruct((blocks, BLK), jnp.int32),
        in_specs=[sspec(), vspec()],
        out_specs=vspec(),
        compiler_params=limit(2),
        name="inverse",
    )(meta, lists)


def force_kernel(slot_ref, meta_ref, back_ref, first_ref, second_ref, list_ref, force_ref, *side_refs):
    half = first_ref.shape[0]
    blocks = slot_ref.shape[0]
    pad = jnp.zeros((ROWS - 3, BLK), F32)
    lanes = []
    owners = []
    for side in range(4):
        nodes = jnp.broadcast_to(side_list(list_ref, meta_ref, side), (ROWS, BLK))
        lanes.append(nodes & (BLK - 1))
        owners.append(nodes // BLK)
    sums = [jnp.zeros((ROWS, BLK), F32) for _ in range(4)]
    for k in range(blocks):
        internal = first_ref[k] if k < half else second_ref[k - half]
        tile = jnp.concatenate([load_rows(back_ref, slot_ref[k], 0, 3), pad], axis=0) - internal
        force_ref[k] = tile
    for side in range(4):
        for k in range(blocks):
            sums[side] = jnp.where(
                owners[side] == k, lane_gather(force_ref[k], lanes[side]), sums[side]
            )
    for side in range(4):
        side_refs[side][...] = sums[side]


def nodal_force(block_slot, meta, returned, internal, lists):
    blocks = 2 * internal[0].shape[0]
    return pl.pallas_call(
        force_kernel,
        out_shape=[jax.ShapeDtypeStruct((blocks, ROWS, BLK), F32)]
        + [jax.ShapeDtypeStruct((ROWS, BLK), F32)] * 4,
        in_specs=[sspec()] * 2 + [vspec()] * 4,
        out_specs=[vspec()] * 5,
        compiler_params=limit(4),
        name="force",
    )(block_slot, meta, returned, *internal, lists)


def update_kernel(*refs, send):
    if send:
        table_ref = refs[0]
        slot_ref, sem = refs[-2:]
        refs = refs[1:-2]
        load = pltpu.make_async_copy(table_ref, slot_ref, sem)
        load.start()
    force_ref = refs[0]
    near = [r[...] for r in refs[1:5]]
    code_ref, mass_ref, vel_ref, disp_ref = refs[5:9]
    if send:
        pos_ref, vel_out, disp_out, send_ref = refs[9:]
    else:
        vel_hbm, disp_hbm, vel_out, disp_out, sems = refs[9:]
    blocks = force_ref.shape[0]
    if send and send_ref.shape[0] != blocks:
        send_ref[...] = jnp.zeros(send_ref.shape, F32)
    copies = []
    for k in range(blocks):
        lanes = slice(k * BLK, (k + 1) * BLK)
        code = jnp.broadcast_to(code_ref[k : k + 1, :], (ROWS, BLK))
        index = code & (BLK - 1)
        extra = jnp.zeros((ROWS, BLK), F32)
        for side in range(4):
            inside = jnp.logical_and(code >= side * BLK, code < (side + 1) * BLK)
            extra = jnp.where(inside, lane_gather(near[side], index), extra)
        assembled = (force_ref[k] + extra)[0:6]
        vel = vel_ref[:, lanes] + TIME_STEP * mass_ref[:, lanes] * assembled
        disp = disp_ref[:, lanes] + TIME_STEP * vel
        vel_out[:, lanes] = vel
        disp_out[:, lanes] = disp
        if not send and (k + 1) % PART == 0:
            span = slice((k + 1 - PART) * BLK, (k + 1) * BLK)
            for i, (held, out) in enumerate(((vel_out, vel_hbm), (disp_out, disp_hbm))):
                copies.append(
                    pltpu.make_async_copy(
                        held.at[:, span], out.at[:, span], sems.at[i, k // PART]
                    )
                )
                copies[-1].start()
    for copy in copies:
        copy.wait()
    if send:
        load.wait()
        for k in range(blocks):
            lanes = slice(k * BLK, (k + 1) * BLK)
            store_rows(send_ref, slot_ref[k], pos_ref[:, lanes] + disp_out[0:3, lanes])


def update(block_slot, force, near, code, inv_mass, velocity, displacement, ref_pos, places):
    nodes = displacement.shape[1]
    out = [jax.ShapeDtypeStruct((6, nodes), F32)] * 2
    arrays = [force, *near, code, inv_mass, velocity, displacement]
    specs = [vspec()] * len(arrays)
    out_specs = [vspec()] * 2
    scratch = []
    if places:
        arrays = [block_slot] + arrays + [ref_pos]
        specs = [pl.BlockSpec(memory_space=pl.ANY)] + specs + [vspec()]
        scratch = [SMEM(block_slot.shape, jnp.int32), pltpu.SemaphoreType.DMA(())]
        out = out + [jax.ShapeDtypeStruct((places, 1, 3 * BLK), F32)]
        out_specs = [vspec()] * 3
    else:
        out_specs = [pl.BlockSpec(memory_space=pl.ANY)] * 2
        scratch = [VMEM((6, nodes), F32)] * 2
        scratch += [pltpu.SemaphoreType.DMA((2, nodes // BLK // PART))]

    def kernel(*refs):
        update_kernel(*refs, send=places > 0)

    return pl.pallas_call(
        kernel,
        out_shape=out,
        in_specs=specs,
        out_specs=out_specs,
        scratch_shapes=scratch,
        compiler_params=limit(6),
        name="update",
    )(*arrays)


def pair_lists(sizes):
    rows, columns = sizes
    near = [[(i, i ^ 1) for i in range(size)] for size in sizes]
    other = [(i, (i + 1) % rows if i % 2 else (i - 1) % rows) for i in range(rows)]
    flat = []
    for i in range(rows):
        for j in range(columns):
            k = j + 1 if j % 2 else j - 1
            inside = 0 <= k < columns
            flat.append((i * columns + j, i * columns + k if inside else (i ^ 1) * columns + j))
    return [("gx", near[0]), ("gx", other), ("gy", near[1]), (AXES, flat)]


def swap(values, sizes):
    moved = [
        lax.ppermute(value, axis, pairs)
        for value, (axis, pairs) in reversed(list(zip(values, pair_lists(sizes))))
    ]
    return moved[::-1]


def body(
    displacement,
    velocity,
    ref_pos,
    normals,
    inv_mass,
    connectivity,
    stiffness,
    yield_force,
    shared_nodes,
    block_slot,
    edge_slots,
    tile_pairs,
    tile_count,
    win_start,
    win_len,
):
    sizes = [lax.axis_size(axis) for axis in AXES]
    if any(size % 2 for size in sizes):
        raise ValueError("odd axis")
    places = sizes[0] * sizes[1] * CAP
    blocks = displacement.shape[1] // BLK
    edge_count = edge_slots.shape[0]
    if max(tile_pairs.shape[1], places + 4 * edge_count) >= 1 << FIELD:
        raise ValueError("field width")
    at = [lax.axis_index(axis) for axis in AXES]
    odd = [i % 2 for i in at]
    inner = [((i > 0) & (i < size - 1)).astype(jnp.int32) for i, size in zip(at, sizes)]
    slot = jnp.arange(8, dtype=jnp.int32)
    meta = jnp.ones((8,), jnp.int32)
    for i, value in ((0, 1 - odd[0]), (1, 1 - odd[1]), (3, inner[0]), (5, inner[1])):
        meta = jnp.where(slot == i, value, meta)
    levels = yield_force.reshape(-1, BLK)
    plan = None
    code = None

    def exchange(blocks_out):
        return lax.all_to_all(blocks_out, AXES, split_axis=0, concat_axis=0, tiled=True)

    def half(disp, part):
        return element_forces(disp, connectivity, stiffness, levels, part, 2)

    outgoing = prep(block_slot, displacement, ref_pos, normals, places)
    first = None
    for step in range(STEPS):
        fresh = step == 0
        received = exchange(outgoing)
        if fresh:
            internal0, plan = element_forces(
                left(displacement),
                left(connectivity),
                stiffness,
                left(levels),
                0,
                2,
                (tile_count, left(tile_pairs), meta),
                places,
            )
        else:
            internal0 = half(displacement, 0)
        received, internal0, plan = lax.optimization_barrier((received, internal0, plan))
        near = swap([edge_rows(edge_slots, received)] * 4, sizes)
        if fresh:
            first = (received, near)
        total, slave_tab = own_contact(
            plan, first[0], None if fresh else received, win_start, win_len
        )
        box_force = far_contact(
            plan, first[1], None if fresh else near, win_start, win_len, total, slave_tab
        )
        box_force, later = lax.optimization_barrier((box_force, displacement))
        returned = exchange(box_force)
        internal1 = half(later, 1)
        force, *sides = nodal_force(
            block_slot, meta, returned, (internal0, internal1), shared_nodes
        )
        if code is None:
            sides, lists = lax.optimization_barrier((sides, shared_nodes))
            code = inverse(meta, lists, blocks)
        incoming = swap(sides, sizes)
        last = step == STEPS - 1
        out = update(
            block_slot,
            force,
            incoming,
            code,
            inv_mass,
            velocity,
            displacement,
            ref_pos,
            0 if last else places,
        )
        velocity, displacement = out[0:2]
        if not last:
            outgoing = out[2]
    return (displacement, velocity)


def solution(mesh):
    split_last = P(None, AXES)
    placed = (
        split_last,
        split_last,
        split_last,
        split_last,
        split_last,
        split_last,
        P(None, None, AXES),
        P(AXES),
        split_last,
        P(AXES),
        P(AXES),
        split_last,
        P(AXES),
        P(AXES, None),
        P(AXES, None),
    )
    return jax.shard_map(
        body,
        mesh=mesh,
        in_specs=placed,
        out_specs=(split_last, split_last),
        check_vma=False,
    )
```

```python
import jax
import jax.numpy as jnp
from jax import lax
from jax.experimental import pallas as pl
from jax.experimental.pallas import tpu as pltpu
from jax.sharding import PartitionSpec as P

BLK = 128
CAP = 2
STEPS = 2
ROWS = 8
EBLK = 16
GROUP = 16
FIELD = 10
TAIL = 16
PART = 16

TIME_STEP = 0.5
PENALTY = 32.0
THICKNESS = 0.2

AXES = ("gx", "gy")
F32 = jnp.float32
BF16 = jnp.bfloat16
VMEM = pltpu.VMEM
SMEM = pltpu.SMEM


def vspec():
    return pl.BlockSpec(memory_space=VMEM)


def sspec():
    return pl.BlockSpec(memory_space=SMEM)


def limit(mebibytes):
    return pltpu.CompilerParams(vmem_limit_bytes=mebibytes << 20)


def left(x):
    return pltpu.with_memory_space_constraint(x, pltpu.HBM)


def load_rows(ref, place, first, count):
    rows = [ref[place, :, r * BLK : (r + 1) * BLK] for r in range(first, first + count)]
    return jnp.concatenate(rows, axis=0)


def store_rows(ref, place, rows):
    for r in range(rows.shape[0]):
        ref[place, :, r * BLK : (r + 1) * BLK] = rows[r : r + 1]


def lane_gather(data, index):
    return jnp.take_along_axis(data, index, axis=1, mode="promise_in_bounds")


def split(x):
    high = x.astype(BF16).astype(F32)
    return high, x - high


def prep_kernel(slot_ref, disp_ref, pos_ref, nrm_ref, out_ref):
    places = out_ref.shape[0]
    blocks = slot_ref.shape[0]
    if places != blocks:
        out_ref[...] = jnp.zeros(out_ref.shape, F32)
    for k in range(blocks):
        lanes = slice(k * BLK, (k + 1) * BLK)
        position = pos_ref[:, lanes] + disp_ref[0:3, lanes]
        both = jnp.concatenate([position, nrm_ref[:, lanes]], axis=0)
        store_rows(out_ref, slot_ref[k], both)


def prep(block_slot, displacement, ref_pos, normals, places):
    return pl.pallas_call(
        prep_kernel,
        out_shape=jax.ShapeDtypeStruct((places, 1, 6 * BLK), F32),
        in_specs=[sspec(), vspec(), vspec(), vspec()],
        out_specs=vspec(),
        compiler_params=limit(4),
        name="prep",
    )(left(block_slot), left(displacement), left(ref_pos), left(normals))


def fold_rows(tiles, row):
    low4 = row < 4
    low2 = (row & 2) == 0
    low1 = (row & 1) == 0
    four = []
    for i in range(4):
        a, b = tiles[i], tiles[i + 4]
        four.append(jnp.where(low4, a, b) + pltpu.roll(jnp.where(low4, b, a), 4, 0))
    two = []
    for i in range(2):
        a, b = four[i], four[i + 2]
        two.append(jnp.where(low2, a + pltpu.roll(a, 6, 0), b + pltpu.roll(b, 2, 0)))
    a, b = two
    return jnp.where(low1, a + pltpu.roll(a, 7, 0), b + pltpu.roll(b, 1, 0))


def element_kernel(*refs, origin, places):
    disp_ref, conn_ref, hbm_ref, yield_ref = refs[0:4]
    out_ref = refs[7] if places else refs[4]
    stiff_ref, sems = refs[-2:]
    wide = EBLK * BLK
    turns = out_ref.shape[0] // EBLK
    if places:
        plan_ref = refs[8]
        sort = tile_sorter(*refs[4:6], plan_ref, places)
        for i in range(refs[6].shape[0]):
            plan_ref[plan_ref.shape[0] - TAIL + i] = refs[6][i]
        share = -(-refs[5].shape[1] // turns)

    def load(r):
        return pltpu.make_async_copy(
            hbm_ref.at[:, :, pl.ds(origin * BLK + r * wide, wide)], stiff_ref.at[r], sems.at[r]
        )

    for r in range(turns):
        load(r).start()
    row = lax.broadcasted_iota(jnp.int32, (ROWS, BLK), 0)
    row48 = lax.broadcasted_iota(jnp.int32, (48, BLK), 0)
    node = lax.broadcasted_iota(jnp.int32, (BLK, BLK), 0).astype(jnp.int16)
    unit = jnp.ones((), BF16)
    zero = jnp.zeros((), BF16)
    row48 = row48.astype(jnp.int16) & 3
    def one_block(r, d):
        k = r * EBLK + d
        lanes = pl.ds(pl.multiple_of((origin + k) * BLK, BLK), BLK)
        local = conn_ref[:, lanes] & (BLK - 1)
        index = jnp.concatenate([local, local], axis=0)
        dofs = []
        for t in range(3):
            first = jnp.broadcast_to(disp_ref[2 * t : 2 * t + 1, lanes], (4, BLK))
            second = jnp.broadcast_to(disp_ref[2 * t + 1 : 2 * t + 2, lanes], (4, BLK))
            dofs.append(lane_gather(jnp.concatenate([first, second], axis=0), index))
        trial = []
        for g in range(3):
            tiles = []
            for i in range(8 * g, 8 * g + 8):
                line = stiff_ref[r, i, :, d * BLK : (d + 1) * BLK].astype(F32)
                tiles.append(line[0:8] * dofs[0] + line[8:16] * dofs[1] + line[16:24] * dofs[2])
            trial.append(fold_rows(tiles, row))
        squared = trial[0] * trial[0] + trial[1] * trial[1] + trial[2] * trial[2]
        squared = squared + pltpu.roll(squared, 4, 0)
        squared = squared + pltpu.roll(squared, 2, 0)
        squared = squared + pltpu.roll(squared, 1, 0)
        level = yield_ref[pl.ds(origin + k, 1), :]
        factor = lax.rsqrt(1.0 + squared / (level * level))
        forces = jnp.concatenate([t * factor for t in trial], axis=0)
        high, low = split(forces)
        stacked = jnp.concatenate([high, low], axis=0).astype(BF16)
        small = local.astype(jnp.int16)
        total = jnp.zeros((48, BLK), F32)
        for a in range(4):
            corner = jnp.where(row48 == a, stacked, zero)
            picker = jnp.where(node == small[a : a + 1, :], unit, zero)
            total = total + lax.dot_general(
                corner, picker, (((1,), (1,)), ((), ())), preferred_element_type=F32
            )
        total = total[0:24] + total[24:48]
        pieces = []
        for t in range(3):
            x = total[8 * t : 8 * t + 8]
            x = x + pltpu.roll(x, 7, 0)
            x = x + pltpu.roll(x, 6, 0)
            pieces += [x[0:1], x[4:5]]
        out_ref[k] = jnp.concatenate(pieces + [jnp.zeros((2, BLK), F32)], axis=0)

    def body(r, own):
        load(r).wait()
        for d in range(EBLK):
            if places:
                for q in range(share * d // EBLK, share * (d + 1) // EBLK):
                    own = sort(r * share + q, own)
            one_block(r, d)
        return own

    own = lax.fori_loop(0, turns, body, jnp.int32(0))
    if places:
        plan_ref[plan_ref.shape[0] - TAIL - 2] = own
        plan_ref[plan_ref.shape[0] - TAIL - 1] = refs[4][0] - own


def element_forces(
    displacement, connectivity, stiffness, yield_force, part=0, parts=1, tiles=(), places=0
):
    nodes = displacement.shape[1]
    blocks = nodes // BLK // parts

    def kernel(*refs):
        element_kernel(*refs, origin=part * blocks, places=places)

    out = jax.ShapeDtypeStruct((blocks, ROWS, BLK), F32)
    out_spec = vspec()
    if places:
        out = [out, jax.ShapeDtypeStruct((2 * tiles[1].shape[1] + 2 * TAIL,), jnp.int32)]
        out_spec = [out_spec, sspec()]
    return pl.pallas_call(
        kernel,
        out_shape=out,
        in_specs=[vspec()] * 2
        + [pl.BlockSpec(memory_space=pltpu.HBM)]
        + [vspec()]
        + [sspec()] * len(tiles),
        out_specs=out_spec,
        scratch_shapes=[
            VMEM((blocks // EBLK, 24, 24, EBLK * BLK), BF16),
            pltpu.SemaphoreType.DMA((blocks // EBLK,)),
        ],
        cost_estimate=pl.CostEstimate(
            flops=2 * 576 * nodes, transcendentals=nodes, bytes_accessed=2 * 576 * nodes
        ),
        compiler_params=limit(12),
        name="element",
    )(displacement, connectivity, left(stiffness), yield_force, *tiles)


def packed(tile, slave, master):
    return tile | slave << FIELD | master << (2 * FIELD)


def unpacked(entry):
    mask = (1 << FIELD) - 1
    return entry & mask, (entry >> FIELD) & mask, entry >> (2 * FIELD)


def tile_sorter(count_ref, pairs_ref, plan_ref, places):
    tiles = pairs_ref.shape[1]
    plan_ref[0] = packed(0, 0, 0)
    plan_ref[tiles] = packed(0, 0, places)
    count = count_ref[0]

    def sort(t, own):
        live = t < count
        at = jnp.minimum(t, tiles - 1)
        master = pairs_ref[1, at]
        is_own = master < places
        where = jnp.where(is_own, own, tiles + t - own)
        where = jnp.where(live, where, 2 * tiles)
        plan_ref[where] = packed(at, pairs_ref[0, at], master)
        return own + jnp.where(jnp.logical_and(live, is_own), 1, 0)

    return sort


def master_entry(where, position, normal, master_tab, force_tab):
    zero1 = jnp.zeros((1, BLK), F32)
    zero2 = jnp.zeros((2, BLK), F32)
    n_high, n_low = split(normal)
    product = position * normal
    offset = THICKNESS + (product[0:1] + product[1:2] + product[2:3])
    o_high, o_rest = split(offset)
    o_mid, o_low = split(o_rest)
    negative = jnp.concatenate([-n_high, -n_low], axis=0)
    master_tab[where] = jnp.concatenate(
        [negative, negative, o_high, o_mid, o_low, zero1], axis=0
    ).astype(BF16)
    lines = [n_high, n_low, zero2]
    force_tab[where] = jnp.concatenate(lines + lines, axis=0).astype(BF16)


def run_tiles(
    plan_ref, first, number, facet_entry, start_ref, length_ref, slave_tab, master_tab, force_tab,
    total_ref, depth_ref,
):
    facet = lax.broadcasted_iota(jnp.int32, (BLK, 2 * BLK), 0).astype(jnp.int16)
    upper = lax.broadcasted_iota(jnp.int32, (16, BLK), 0) < 8
    blank = jnp.zeros((16, BLK), BF16)
    small = jnp.int16
    last = jnp.maximum(number - 1, 0)

    def at(group, d):
        i = group * GROUP + d
        return plan_ref[first + jnp.minimum(i, last)], i < number

    def depths(group):
        for d in range(0, GROUP, 2):
            facets, nodes = [], []
            for e in range(2):
                entry, _ = at(group, d + e)
                _, slave, master = unpacked(entry)
                facets.append(master_tab[facet_entry(master)[0]])
                nodes.append(slave_tab[slave])
            left = jnp.concatenate([nodes[0], blank], axis=0)
            right = jnp.concatenate([blank, nodes[1]], axis=0)
            depth_ref[d // 2] = lax.dot_general(
                jnp.concatenate(facets, axis=0),
                jnp.concatenate([left, right], axis=1),
                (((0,), (0,)), ((), ())),
                preferred_element_type=F32,
            )

    def body(group, carry):
        forces = []
        for d in range(0, GROUP, 2):
            starts, lengths, rows = [], [], []
            for e in range(2):
                entry, live = at(group, d + e)
                t, _, master = unpacked(entry)
                where, known = facet_entry(master)
                live = jnp.logical_and(live, known)
                starts.append(start_ref[pl.ds(t, 1), :])
                lengths.append(jnp.where(live, length_ref[pl.ds(t, 1), :], 0))
                rows.append(force_tab[where])
            start = jnp.concatenate(starts, axis=1).astype(small)
            length = jnp.concatenate(lengths, axis=1).astype(small)
            inside = ((facet - start) & (BLK - 1)) < length
            pressure = jnp.maximum(depth_ref[d // 2], 0.0)
            high = pressure.astype(BF16)
            low = (pressure - high.astype(F32)).astype(BF16)
            high = jnp.where(inside, high, jnp.zeros((), BF16))
            low = jnp.where(inside, low, jnp.zeros((), BF16))
            both = jnp.where(upper, rows[0], rows[1])
            forces.append(
                jnp.dot(
                    jnp.concatenate([both, both], axis=1),
                    jnp.concatenate([high, low], axis=0),
                    preferred_element_type=F32,
                )
            )
        depths(group + 1)
        for d in range(GROUP):
            _, slave, _ = unpacked(at(group, d)[0])
            e = d % 2
            part = forces[d // 2][8 * e : 8 * e + 8, e * BLK : (e + 1) * BLK]
            total_ref[slave] = total_ref[slave] + part
        return carry

    depths(0)
    lax.fori_loop(0, (number + GROUP - 1) // GROUP, body, 0)


def own_kernel(table_ref, recv_ref, *refs, fresh):
    pos_ref = recv_ref if fresh else refs[0]
    refs = refs if fresh else refs[1:]
    start_ref, length_ref, total_ref, slave_tab, master_tab, force_tab, depth_ref = refs[:7]
    plan_ref, sem = refs[7:]
    load = pltpu.make_async_copy(table_ref, plan_ref, sem)
    load.start()
    ones = jnp.ones((3, BLK), F32)
    zero1 = jnp.zeros((1, BLK), F32)
    places = recv_ref.shape[0]

    def entry(p, carry):
        position = load_rows(pos_ref, p, 0, 3)
        p_high, p_low = split(position)
        slave_tab[p] = jnp.concatenate(
            [p_high, p_high, p_low, p_low, ones, zero1], axis=0
        ).astype(BF16)
        master_entry(p, position, load_rows(recv_ref, p, 3, 3), master_tab, force_tab)
        total_ref[p] = jnp.zeros((ROWS, BLK), F32)
        return carry

    lax.fori_loop(0, places, entry, 0, unroll=8)
    load.wait()
    run_tiles(
        plan_ref, 0, plan_ref[plan_ref.shape[0] - TAIL - 2], lambda m: (m, True), start_ref, length_ref, slave_tab, master_tab, force_tab,
        total_ref, depth_ref,
    )


def far_kernel(table_ref, *refs, edges, fresh):
    edge_refs = refs[0:4]
    pos_refs = edge_refs if fresh else refs[4:8]
    refs = refs[4:] if fresh else refs[8:]
    start_ref, length_ref, own_ref, slave_tab, out_ref = refs[0:5]
    master_tab, force_tab, total_ref, depth_ref, plan_ref, sem = refs[5:11]
    load = pltpu.make_async_copy(table_ref, plan_ref, sem)
    load.start()
    tail = plan_ref.shape[0] - TAIL
    places = own_ref.shape[0]
    total_ref[...] = own_ref[...]
    for side in range(4):
        for e in range(edges):
            normal = load_rows(edge_refs[side], e, 3, 3)
            position = load_rows(pos_refs[side], e, 0, 3)
            master_entry(side * edges + e, position, normal, master_tab, force_tab)
    load.wait()
    log = edges.bit_length() - 1
    power = edges == 1 << log

    def facet_entry(master):
        entry = master - places
        side = entry >> log if power else entry // edges
        pairing = side ^ jnp.where(side < 2, plan_ref[tail], plan_ref[tail + 1])
        return entry + edges * (pairing - side), plan_ref[tail + 2 + pairing] > 0

    run_tiles(
        plan_ref, start_ref.shape[0], plan_ref[tail - 1], facet_entry, start_ref, length_ref,
        slave_tab, master_tab, force_tab, total_ref, depth_ref,
    )

    def finish(p, carry):
        tile = total_ref[p]
        store_rows(out_ref, p, (PENALTY / BLK) * (tile[0:3] + tile[3:6]))
        return carry

    lax.fori_loop(0, places, finish, 0, unroll=8)


def edge_kernel(slot_ref, recv_ref, out_ref):
    for e in range(slot_ref.shape[0]):
        out_ref[e] = recv_ref[slot_ref[e]]


def edge_rows(edge_slots, received):
    return pl.pallas_call(
        edge_kernel,
        out_shape=jax.ShapeDtypeStruct((edge_slots.shape[0],) + received.shape[1:], F32),
        in_specs=[sspec(), vspec()],
        out_specs=vspec(),
        compiler_params=limit(1),
        name="edges",
    )(edge_slots, received)


def tile_cost(tiles):
    return pl.CostEstimate(
        flops=tiles * BLK * BLK * 64, transcendentals=0, bytes_accessed=tiles * BLK * 8
    )


def own_contact(plan, received, positions, start, length):
    places = received.shape[0]
    fresh = positions is None
    arrays = [received] + ([] if fresh else [positions]) + [start, length]

    def kernel(*refs):
        own_kernel(*refs, fresh=fresh)

    return pl.pallas_call(
        kernel,
        out_shape=[
            jax.ShapeDtypeStruct((places, ROWS, BLK), F32),
            jax.ShapeDtypeStruct((places, 16, BLK), BF16),
        ],
        in_specs=[pl.BlockSpec(memory_space=pl.ANY)] + [vspec()] * len(arrays),
        out_specs=[vspec()] * 2,
        scratch_shapes=[
            VMEM((places, 16, BLK), BF16),
            VMEM((places, 16, BLK), BF16),
            VMEM((GROUP // 2, BLK, 2 * BLK), F32),
            SMEM(plan.shape, jnp.int32),
            pltpu.SemaphoreType.DMA(()),
        ],
        cost_estimate=tile_cost(start.shape[0] // 2),
        compiler_params=limit(8),
        name="own_contact",
    )(plan, *arrays)


def far_contact(plan, edges, edge_positions, start, length, total, slave_tab):
    places = total.shape[0]
    fresh = edge_positions is None
    edge_count = edges[0].shape[0]
    arrays = list(edges) + ([] if fresh else list(edge_positions))
    arrays += [start, length, total, slave_tab]

    def kernel(*refs):
        far_kernel(*refs, edges=edge_count, fresh=fresh)

    return pl.pallas_call(
        kernel,
        out_shape=jax.ShapeDtypeStruct((places, 1, 3 * BLK), F32),
        in_specs=[pl.BlockSpec(memory_space=pl.ANY)] + [vspec()] * len(arrays),
        out_specs=vspec(),
        scratch_shapes=[
            VMEM((4 * edge_count, 16, BLK), BF16),
            VMEM((4 * edge_count, 16, BLK), BF16),
            VMEM((places, ROWS, BLK), F32),
            VMEM((GROUP // 2, BLK, 2 * BLK), F32),
            SMEM(plan.shape, jnp.int32),
            pltpu.SemaphoreType.DMA(()),
        ],
        cost_estimate=tile_cost(start.shape[0] // 2),
        compiler_params=limit(8),
        name="far_contact",
    )(plan, *arrays)


def side_list(list_ref, meta_ref, side):
    axis = side // 2
    low = list_ref[2 * axis : 2 * axis + 1, :]
    high = list_ref[2 * axis + 1 : 2 * axis + 2, :]
    return jnp.where(meta_ref[axis] != side % 2, high, low)


def inverse_kernel(meta_ref, list_ref, out_ref):
    blocks = out_ref.shape[0]
    block_id = lax.broadcasted_iota(jnp.int32, (blocks, BLK), 0)
    lane_id = lax.broadcasted_iota(jnp.int32, (BLK, BLK), 0)
    rank = (lax.broadcasted_iota(jnp.int32, (BLK, BLK), 1) + 1).astype(F32)
    code = jnp.full((blocks, BLK), -1, jnp.int32)
    for side in range(4):
        nodes = side_list(list_ref, meta_ref, side)
        valid = meta_ref[2 + side] > 0
        in_block = jnp.where(
            jnp.logical_and(block_id == nodes // BLK, valid), 1.0, 0.0
        ).astype(BF16)
        at_lane = jnp.where(lane_id == (nodes & (BLK - 1)), rank, 0.0).astype(BF16)
        found = lax.dot_general(
            in_block, at_lane, (((1,), (1,)), ((), ())), preferred_element_type=F32
        ).astype(jnp.int32)
        code = jnp.where(found > 0, found - 1 + side * BLK, code)
    out_ref[...] = code


def inverse(meta, lists, blocks):
    return pl.pallas_call(
        inverse_kernel,
        out_shape=jax.ShapeDtypeStruct((blocks, BLK), jnp.int32),
        in_specs=[sspec(), vspec()],
        out_specs=vspec(),
        compiler_params=limit(2),
        name="inverse",
    )(meta, lists)


def force_kernel(slot_ref, meta_ref, back_ref, first_ref, second_ref, list_ref, force_ref, *side_refs):
    half = first_ref.shape[0]
    blocks = slot_ref.shape[0]
    pad = jnp.zeros((ROWS - 3, BLK), F32)
    lanes = []
    owners = []
    for side in range(4):
        nodes = jnp.broadcast_to(side_list(list_ref, meta_ref, side), (ROWS, BLK))
        lanes.append(nodes & (BLK - 1))
        owners.append(nodes // BLK)
    sums = [jnp.zeros((ROWS, BLK), F32) for _ in range(4)]
    for k in range(blocks):
        internal = first_ref[k] if k < half else second_ref[k - half]
        tile = jnp.concatenate([load_rows(back_ref, slot_ref[k], 0, 3), pad], axis=0) - internal
        force_ref[k] = tile
    for side in range(4):
        for k in range(blocks):
            sums[side] = jnp.where(
                owners[side] == k, lane_gather(force_ref[k], lanes[side]), sums[side]
            )
    for side in range(4):
        side_refs[side][...] = sums[side]


def nodal_force(block_slot, meta, returned, internal, lists):
    blocks = 2 * internal[0].shape[0]
    return pl.pallas_call(
        force_kernel,
        out_shape=[jax.ShapeDtypeStruct((blocks, ROWS, BLK), F32)]
        + [jax.ShapeDtypeStruct((ROWS, BLK), F32)] * 4,
        in_specs=[sspec()] * 2 + [vspec()] * 4,
        out_specs=[vspec()] * 5,
        compiler_params=limit(4),
        name="force",
    )(block_slot, meta, returned, *internal, lists)


def update_kernel(*refs, send):
    if send:
        table_ref = refs[0]
        slot_ref, sem = refs[-2:]
        refs = refs[1:-2]
        load = pltpu.make_async_copy(table_ref, slot_ref, sem)
        load.start()
    force_ref = refs[0]
    near = [r[...] for r in refs[1:5]]
    code_ref, mass_ref, vel_ref, disp_ref = refs[5:9]
    if send:
        pos_ref, vel_out, disp_out, send_ref = refs[9:]
    else:
        vel_hbm, disp_hbm, vel_out, disp_out, sems = refs[9:]
    blocks = force_ref.shape[0]
    if send and send_ref.shape[0] != blocks:
        send_ref[...] = jnp.zeros(send_ref.shape, F32)
    copies = []
    for k in range(blocks):
        lanes = slice(k * BLK, (k + 1) * BLK)
        code = jnp.broadcast_to(code_ref[k : k + 1, :], (ROWS, BLK))
        index = code & (BLK - 1)
        extra = jnp.zeros((ROWS, BLK), F32)
        for side in range(4):
            inside = jnp.logical_and(code >= side * BLK, code < (side + 1) * BLK)
            extra = jnp.where(inside, lane_gather(near[side], index), extra)
        assembled = (force_ref[k] + extra)[0:6]
        vel = vel_ref[:, lanes] + TIME_STEP * mass_ref[:, lanes] * assembled
        disp = disp_ref[:, lanes] + TIME_STEP * vel
        vel_out[:, lanes] = vel
        disp_out[:, lanes] = disp
        if not send and (k + 1) % PART == 0:
            span = slice((k + 1 - PART) * BLK, (k + 1) * BLK)
            for i, (held, out) in enumerate(((vel_out, vel_hbm), (disp_out, disp_hbm))):
                copies.append(
                    pltpu.make_async_copy(
                        held.at[:, span], out.at[:, span], sems.at[i, k // PART]
                    )
                )
                copies[-1].start()
    for copy in copies:
        copy.wait()
    if send:
        load.wait()
        for k in range(blocks):
            lanes = slice(k * BLK, (k + 1) * BLK)
            store_rows(send_ref, slot_ref[k], pos_ref[:, lanes] + disp_out[0:3, lanes])


def update(block_slot, force, near, code, inv_mass, velocity, displacement, ref_pos, places):
    nodes = displacement.shape[1]
    out = [jax.ShapeDtypeStruct((6, nodes), F32)] * 2
    arrays = [force, *near, code, inv_mass, velocity, displacement]
    specs = [vspec()] * len(arrays)
    out_specs = [vspec()] * 2
    scratch = []
    if places:
        arrays = [block_slot] + arrays + [ref_pos]
        specs = [pl.BlockSpec(memory_space=pl.ANY)] + specs + [vspec()]
        scratch = [SMEM(block_slot.shape, jnp.int32), pltpu.SemaphoreType.DMA(())]
        out = out + [jax.ShapeDtypeStruct((places, 1, 3 * BLK), F32)]
        out_specs = [vspec()] * 3
    else:
        out_specs = [pl.BlockSpec(memory_space=pl.ANY)] * 2
        scratch = [VMEM((6, nodes), F32)] * 2
        scratch += [pltpu.SemaphoreType.DMA((2, nodes // BLK // PART))]

    def kernel(*refs):
        update_kernel(*refs, send=places > 0)

    return pl.pallas_call(
        kernel,
        out_shape=out,
        in_specs=specs,
        out_specs=out_specs,
        scratch_shapes=scratch,
        compiler_params=limit(6),
        name="update",
    )(*arrays)


def pair_lists(sizes):
    rows, columns = sizes
    near = [[(i, i ^ 1) for i in range(size)] for size in sizes]
    other = [(i, (i + 1) % rows if i % 2 else (i - 1) % rows) for i in range(rows)]
    flat = []
    for i in range(rows):
        for j in range(columns):
            k = j + 1 if j % 2 else j - 1
            inside = 0 <= k < columns
            flat.append((i * columns + j, i * columns + k if inside else (i ^ 1) * columns + j))
    return [("gx", near[0]), ("gx", other), ("gy", near[1]), (AXES, flat)]


def swap(values, sizes):
    moved = [
        lax.ppermute(value, axis, pairs)
        for value, (axis, pairs) in reversed(list(zip(values, pair_lists(sizes))))
    ]
    return moved[::-1]


def body(
    displacement,
    velocity,
    ref_pos,
    normals,
    inv_mass,
    connectivity,
    stiffness,
    yield_force,
    shared_nodes,
    block_slot,
    edge_slots,
    tile_pairs,
    tile_count,
    win_start,
    win_len,
):
    sizes = [lax.axis_size(axis) for axis in AXES]
    if any(size % 2 for size in sizes):
        raise ValueError("odd axis")
    places = sizes[0] * sizes[1] * CAP
    blocks = displacement.shape[1] // BLK
    edge_count = edge_slots.shape[0]
    if max(tile_pairs.shape[1], places + 4 * edge_count) >= 1 << FIELD:
        raise ValueError("field width")
    at = [lax.axis_index(axis) for axis in AXES]
    odd = [i % 2 for i in at]
    inner = [((i > 0) & (i < size - 1)).astype(jnp.int32) for i, size in zip(at, sizes)]
    slot = jnp.arange(8, dtype=jnp.int32)
    meta = jnp.ones((8,), jnp.int32)
    for i, value in ((0, 1 - odd[0]), (1, 1 - odd[1]), (3, inner[0]), (5, inner[1])):
        meta = jnp.where(slot == i, value, meta)
    levels = yield_force.reshape(-1, BLK)
    plan = None
    code = None

    def exchange(blocks_out):
        return lax.all_to_all(blocks_out, AXES, split_axis=0, concat_axis=0, tiled=True)

    def half(disp, part):
        return element_forces(disp, connectivity, stiffness, levels, part, 2)

    outgoing = prep(block_slot, displacement, ref_pos, normals, places)
    first = None
    for step in range(STEPS):
        fresh = step == 0
        received = exchange(outgoing)
        if fresh:
            internal0, plan = element_forces(
                left(displacement),
                left(connectivity),
                stiffness,
                left(levels),
                0,
                2,
                (tile_count, left(tile_pairs), meta),
                places,
            )
        else:
            internal0 = half(displacement, 0)
        received, internal0, plan = lax.optimization_barrier((received, internal0, plan))
        near = swap([edge_rows(edge_slots, received)] * 4, sizes)
        if fresh:
            first = (received, near)
        total, slave_tab = own_contact(
            plan, first[0], None if fresh else received, win_start, win_len
        )
        box_force = far_contact(
            plan, first[1], None if fresh else near, win_start, win_len, total, slave_tab
        )
        box_force, later = lax.optimization_barrier((box_force, displacement))
        returned = exchange(box_force)
        internal1 = half(later, 1)
        force, *sides = nodal_force(
            block_slot, meta, returned, (internal0, internal1), shared_nodes
        )
        if code is None:
            sides, lists = lax.optimization_barrier((sides, shared_nodes))
            code = inverse(meta, lists, blocks)
        incoming = swap(sides, sizes)
        last = step == STEPS - 1
        out = update(
            block_slot,
            force,
            incoming,
            code,
            inv_mass,
            velocity,
            displacement,
            ref_pos,
            0 if last else places,
        )
        velocity, displacement = out[0:2]
        if not last:
            outgoing = out[2]
    return (displacement, velocity)


def solution(mesh):
    split_last = P(None, AXES)
    placed = (
        split_last,
        split_last,
        split_last,
        split_last,
        split_last,
        split_last,
        P(None, None, AXES),
        P(AXES),
        split_last,
        P(AXES),
        P(AXES),
        split_last,
        P(AXES),
        P(AXES, None),
        P(AXES, None),
    )
    return jax.shard_map(
        body,
        mesh=mesh,
        in_specs=placed,
        out_specs=(split_last, split_last),
        check_vma=False,
    )
```

```python
import jax
import jax.numpy as jnp
from jax import lax
from jax.experimental import pallas as pl
from jax.experimental.pallas import tpu as pltpu
from jax.sharding import PartitionSpec as P

BLK = 128
CAP = 2
STEPS = 2
ROWS = 8
EBLK = 16
GROUP = 16
FIELD = 10
TAIL = 16
PART = 16

TIME_STEP = 0.5
PENALTY = 32.0
THICKNESS = 0.2

AXES = ("gx", "gy")
F32 = jnp.float32
BF16 = jnp.bfloat16
VMEM = pltpu.VMEM
SMEM = pltpu.SMEM


def vspec():
    return pl.BlockSpec(memory_space=VMEM)


def sspec():
    return pl.BlockSpec(memory_space=SMEM)


def limit(mebibytes):
    return pltpu.CompilerParams(vmem_limit_bytes=mebibytes << 20)


def left(x):
    return pltpu.with_memory_space_constraint(x, pltpu.HBM)


def load_rows(ref, place, first, count):
    rows = [ref[place, :, r * BLK : (r + 1) * BLK] for r in range(first, first + count)]
    return jnp.concatenate(rows, axis=0)


def store_rows(ref, place, rows):
    for r in range(rows.shape[0]):
        ref[place, :, r * BLK : (r + 1) * BLK] = rows[r : r + 1]


def lane_gather(data, index):
    return jnp.take_along_axis(data, index, axis=1, mode="promise_in_bounds")


def split(x):
    high = x.astype(BF16).astype(F32)
    return high, x - high


def prep_kernel(slot_ref, disp_ref, pos_ref, nrm_ref, out_ref):
    places = out_ref.shape[0]
    blocks = slot_ref.shape[0]
    if places != blocks:
        out_ref[...] = jnp.zeros(out_ref.shape, F32)
    for k in range(blocks):
        lanes = slice(k * BLK, (k + 1) * BLK)
        position = pos_ref[:, lanes] + disp_ref[0:3, lanes]
        both = jnp.concatenate([position, nrm_ref[:, lanes]], axis=0)
        store_rows(out_ref, slot_ref[k], both)


def prep(block_slot, displacement, ref_pos, normals, places):
    return pl.pallas_call(
        prep_kernel,
        out_shape=jax.ShapeDtypeStruct((places, 1, 6 * BLK), F32),
        in_specs=[sspec(), vspec(), vspec(), vspec()],
        out_specs=vspec(),
        compiler_params=limit(4),
        name="prep",
    )(left(block_slot), left(displacement), left(ref_pos), left(normals))


def fold_rows(tiles, row):
    low4 = row < 4
    low2 = (row & 2) == 0
    low1 = (row & 1) == 0
    four = []
    for i in range(4):
        a, b = tiles[i], tiles[i + 4]
        four.append(jnp.where(low4, a, b) + pltpu.roll(jnp.where(low4, b, a), 4, 0))
    two = []
    for i in range(2):
        a, b = four[i], four[i + 2]
        two.append(jnp.where(low2, a + pltpu.roll(a, 6, 0), b + pltpu.roll(b, 2, 0)))
    a, b = two
    return jnp.where(low1, a + pltpu.roll(a, 7, 0), b + pltpu.roll(b, 1, 0))


def element_kernel(*refs, origin, places):
    disp_ref, conn_ref, hbm_ref, yield_ref = refs[0:4]
    out_ref = refs[7] if places else refs[4]
    stiff_ref, sems = refs[-2:]
    wide = EBLK * BLK
    turns = out_ref.shape[0] // EBLK
    if places:
        plan_ref = refs[8]
        sort = tile_sorter(*refs[4:6], plan_ref, places)
        for i in range(refs[6].shape[0]):
            plan_ref[plan_ref.shape[0] - TAIL + i] = refs[6][i]
        share = -(-refs[5].shape[1] // turns)

    def load(r):
        return pltpu.make_async_copy(
            hbm_ref.at[:, :, pl.ds(origin * BLK + r * wide, wide)], stiff_ref.at[r], sems.at[r]
        )

    for r in range(turns):
        load(r).start()
    row = lax.broadcasted_iota(jnp.int32, (ROWS, BLK), 0)
    row48 = lax.broadcasted_iota(jnp.int32, (48, BLK), 0)
    node = lax.broadcasted_iota(jnp.int32, (BLK, BLK), 0).astype(jnp.int16)
    unit = jnp.ones((), BF16)
    zero = jnp.zeros((), BF16)
    row48 = row48.astype(jnp.int16) & 3
    def one_block(r, d):
        k = r * EBLK + d
        lanes = pl.ds(pl.multiple_of((origin + k) * BLK, BLK), BLK)
        local = conn_ref[:, lanes] & (BLK - 1)
        index = jnp.concatenate([local, local], axis=0)
        dofs = []
        for t in range(3):
            first = jnp.broadcast_to(disp_ref[2 * t : 2 * t + 1, lanes], (4, BLK))
            second = jnp.broadcast_to(disp_ref[2 * t + 1 : 2 * t + 2, lanes], (4, BLK))
            dofs.append(lane_gather(jnp.concatenate([first, second], axis=0), index))
        trial = []
        for g in range(3):
            tiles = []
            for i in range(8 * g, 8 * g + 8):
                line = stiff_ref[r, i, :, d * BLK : (d + 1) * BLK].astype(F32)
                tiles.append(line[0:8] * dofs[0] + line[8:16] * dofs[1] + line[16:24] * dofs[2])
            trial.append(fold_rows(tiles, row))
        squared = trial[0] * trial[0] + trial[1] * trial[1] + trial[2] * trial[2]
        squared = squared + pltpu.roll(squared, 4, 0)
        squared = squared + pltpu.roll(squared, 2, 0)
        squared = squared + pltpu.roll(squared, 1, 0)
        level = yield_ref[pl.ds(origin + k, 1), :]
        factor = lax.rsqrt(1.0 + squared / (level * level))
        forces = jnp.concatenate([t * factor for t in trial], axis=0)
        high, low = split(forces)
        stacked = jnp.concatenate([high, low], axis=0).astype(BF16)
        small = local.astype(jnp.int16)
        total = jnp.zeros((48, BLK), F32)
        for a in range(4):
            corner = jnp.where(row48 == a, stacked, zero)
            picker = jnp.where(node == small[a : a + 1, :], unit, zero)
            total = total + lax.dot_general(
                corner, picker, (((1,), (1,)), ((), ())), preferred_element_type=F32
            )
        total = total[0:24] + total[24:48]
        pieces = []
        for t in range(3):
            x = total[8 * t : 8 * t + 8]
            x = x + pltpu.roll(x, 7, 0)
            x = x + pltpu.roll(x, 6, 0)
            pieces += [x[0:1], x[4:5]]
        out_ref[k] = jnp.concatenate(pieces + [jnp.zeros((2, BLK), F32)], axis=0)

    def body(r, own):
        load(r).wait()
        for d in range(EBLK):
            if places:
                for q in range(share * d // EBLK, share * (d + 1) // EBLK):
                    own = sort(r * share + q, own)
            one_block(r, d)
        return own

    own = lax.fori_loop(0, turns, body, jnp.int32(0))
    if places:
        plan_ref[plan_ref.shape[0] - TAIL - 2] = own
        plan_ref[plan_ref.shape[0] - TAIL - 1] = refs[4][0] - own


def element_forces(
    displacement, connectivity, stiffness, yield_force, part=0, parts=1, tiles=(), places=0
):
    nodes = displacement.shape[1]
    blocks = nodes // BLK // parts

    def kernel(*refs):
        element_kernel(*refs, origin=part * blocks, places=places)

    out = jax.ShapeDtypeStruct((blocks, ROWS, BLK), F32)
    out_spec = vspec()
    if places:
        out = [out, jax.ShapeDtypeStruct((2 * tiles[1].shape[1] + 2 * TAIL,), jnp.int32)]
        out_spec = [out_spec, sspec()]
    return pl.pallas_call(
        kernel,
        out_shape=out,
        in_specs=[vspec()] * 2
        + [pl.BlockSpec(memory_space=pltpu.HBM)]
        + [vspec()]
        + [sspec()] * len(tiles),
        out_specs=out_spec,
        scratch_shapes=[
            VMEM((blocks // EBLK, 24, 24, EBLK * BLK), BF16),
            pltpu.SemaphoreType.DMA((blocks // EBLK,)),
        ],
        cost_estimate=pl.CostEstimate(
            flops=2 * 576 * nodes, transcendentals=nodes, bytes_accessed=2 * 576 * nodes
        ),
        compiler_params=limit(12),
        name="element",
    )(displacement, connectivity, left(stiffness), yield_force, *tiles)


def packed(tile, slave, master):
    return tile | slave << FIELD | master << (2 * FIELD)


def unpacked(entry):
    mask = (1 << FIELD) - 1
    return entry & mask, (entry >> FIELD) & mask, entry >> (2 * FIELD)


def tile_sorter(count_ref, pairs_ref, plan_ref, places):
    tiles = pairs_ref.shape[1]
    plan_ref[0] = packed(0, 0, 0)
    plan_ref[tiles] = packed(0, 0, places)
    count = count_ref[0]

    def sort(t, own):
        live = t < count
        at = jnp.minimum(t, tiles - 1)
        master = pairs_ref[1, at]
        is_own = master < places
        where = jnp.where(is_own, own, tiles + t - own)
        where = jnp.where(live, where, 2 * tiles)
        plan_ref[where] = packed(at, pairs_ref[0, at], master)
        return own + jnp.where(jnp.logical_and(live, is_own), 1, 0)

    return sort


def master_entry(where, position, normal, master_tab, force_tab):
    zero1 = jnp.zeros((1, BLK), F32)
    zero2 = jnp.zeros((2, BLK), F32)
    n_high, n_low = split(normal)
    product = position * normal
    offset = THICKNESS + (product[0:1] + product[1:2] + product[2:3])
    o_high, o_rest = split(offset)
    o_mid, o_low = split(o_rest)
    negative = jnp.concatenate([-n_high, -n_low], axis=0)
    master_tab[where] = jnp.concatenate(
        [negative, negative, o_high, o_mid, o_low, zero1], axis=0
    ).astype(BF16)
    lines = [n_high, n_low, zero2]
    force_tab[where] = jnp.concatenate(lines + lines, axis=0).astype(BF16)


def run_tiles(
    plan_ref, first, number, facet_entry, start_ref, length_ref, slave_tab, master_tab, force_tab,
    total_ref, depth_ref,
):
    facet = lax.broadcasted_iota(jnp.int32, (BLK, 2 * BLK), 0).astype(jnp.int16)
    upper = lax.broadcasted_iota(jnp.int32, (16, BLK), 0) < 8
    blank = jnp.zeros((16, BLK), BF16)
    small = jnp.int16
    last = jnp.maximum(number - 1, 0)

    def at(group, d):
        i = group * GROUP + d
        return plan_ref[first + jnp.minimum(i, last)], i < number

    def depths(group):
        for d in range(0, GROUP, 2):
            facets, nodes = [], []
            for e in range(2):
                entry, _ = at(group, d + e)
                _, slave, master = unpacked(entry)
                facets.append(master_tab[facet_entry(master)[0]])
                nodes.append(slave_tab[slave])
            left = jnp.concatenate([nodes[0], blank], axis=0)
            right = jnp.concatenate([blank, nodes[1]], axis=0)
            depth_ref[d // 2] = lax.dot_general(
                jnp.concatenate(facets, axis=0),
                jnp.concatenate([left, right], axis=1),
                (((0,), (0,)), ((), ())),
                preferred_element_type=F32,
            )

    def body(group, carry):
        forces = []
        for d in range(0, GROUP, 2):
            starts, lengths, rows = [], [], []
            for e in range(2):
                entry, live = at(group, d + e)
                t, _, master = unpacked(entry)
                where, known = facet_entry(master)
                live = jnp.logical_and(live, known)
                starts.append(start_ref[pl.ds(t, 1), :])
                lengths.append(jnp.where(live, length_ref[pl.ds(t, 1), :], 0))
                rows.append(force_tab[where])
            start = jnp.concatenate(starts, axis=1).astype(small)
            length = jnp.concatenate(lengths, axis=1).astype(small)
            inside = ((facet - start) & (BLK - 1)) < length
            pressure = jnp.maximum(depth_ref[d // 2], 0.0)
            high = pressure.astype(BF16)
            low = (pressure - high.astype(F32)).astype(BF16)
            high = jnp.where(inside, high, jnp.zeros((), BF16))
            low = jnp.where(inside, low, jnp.zeros((), BF16))
            both = jnp.where(upper, rows[0], rows[1])
            forces.append(
                jnp.dot(
                    jnp.concatenate([both, both], axis=1),
                    jnp.concatenate([high, low], axis=0),
                    preferred_element_type=F32,
                )
            )
        depths(group + 1)
        for d in range(GROUP):
            _, slave, _ = unpacked(at(group, d)[0])
            e = d % 2
            part = forces[d // 2][8 * e : 8 * e + 8, e * BLK : (e + 1) * BLK]
            total_ref[slave] = total_ref[slave] + part
        return carry

    depths(0)
    lax.fori_loop(0, (number + GROUP - 1) // GROUP, body, 0)


def own_kernel(table_ref, recv_ref, *refs, fresh):
    pos_ref = recv_ref if fresh else refs[0]
    refs = refs if fresh else refs[1:]
    start_ref, length_ref, total_ref, slave_tab, master_tab, force_tab, depth_ref = refs[:7]
    plan_ref, sem = refs[7:]
    load = pltpu.make_async_copy(table_ref, plan_ref, sem)
    load.start()
    ones = jnp.ones((3, BLK), F32)
    zero1 = jnp.zeros((1, BLK), F32)
    places = recv_ref.shape[0]

    def entry(p, carry):
        position = load_rows(pos_ref, p, 0, 3)
        p_high, p_low = split(position)
        slave_tab[p] = jnp.concatenate(
            [p_high, p_high, p_low, p_low, ones, zero1], axis=0
        ).astype(BF16)
        master_entry(p, position, load_rows(recv_ref, p, 3, 3), master_tab, force_tab)
        total_ref[p] = jnp.zeros((ROWS, BLK), F32)
        return carry

    lax.fori_loop(0, places, entry, 0, unroll=8)
    load.wait()
    run_tiles(
        plan_ref, 0, plan_ref[plan_ref.shape[0] - TAIL - 2], lambda m: (m, True), start_ref, length_ref, slave_tab, master_tab, force_tab,
        total_ref, depth_ref,
    )


def far_kernel(table_ref, *refs, edges, fresh):
    edge_refs = refs[0:4]
    pos_refs = edge_refs if fresh else refs[4:8]
    refs = refs[4:] if fresh else refs[8:]
    start_ref, length_ref, own_ref, slave_tab, out_ref = refs[0:5]
    master_tab, force_tab, total_ref, depth_ref, plan_ref, sem = refs[5:11]
    load = pltpu.make_async_copy(table_ref, plan_ref, sem)
    load.start()
    tail = plan_ref.shape[0] - TAIL
    places = own_ref.shape[0]
    total_ref[...] = own_ref[...]
    for side in range(4):
        for e in range(edges):
            normal = load_rows(edge_refs[side], e, 3, 3)
            position = load_rows(pos_refs[side], e, 0, 3)
            master_entry(side * edges + e, position, normal, master_tab, force_tab)
    load.wait()
    log = edges.bit_length() - 1
    power = edges == 1 << log

    def facet_entry(master):
        entry = master - places
        side = entry >> log if power else entry // edges
        pairing = side ^ jnp.where(side < 2, plan_ref[tail], plan_ref[tail + 1])
        return entry + edges * (pairing - side), plan_ref[tail + 2 + pairing] > 0

    run_tiles(
        plan_ref, start_ref.shape[0], plan_ref[tail - 1], facet_entry, start_ref, length_ref,
        slave_tab, master_tab, force_tab, total_ref, depth_ref,
    )

    def finish(p, carry):
        tile = total_ref[p]
        store_rows(out_ref, p, (PENALTY / BLK) * (tile[0:3] + tile[3:6]))
        return carry

    lax.fori_loop(0, places, finish, 0, unroll=8)


def edge_kernel(slot_ref, recv_ref, out_ref):
    for e in range(slot_ref.shape[0]):
        out_ref[e] = recv_ref[slot_ref[e]]


def edge_rows(edge_slots, received):
    return pl.pallas_call(
        edge_kernel,
        out_shape=jax.ShapeDtypeStruct((edge_slots.shape[0],) + received.shape[1:], F32),
        in_specs=[sspec(), vspec()],
        out_specs=vspec(),
        compiler_params=limit(1),
        name="edges",
    )(edge_slots, received)


def tile_cost(tiles):
    return pl.CostEstimate(
        flops=tiles * BLK * BLK * 64, transcendentals=0, bytes_accessed=tiles * BLK * 8
    )


def own_contact(plan, received, positions, start, length):
    places = received.shape[0]
    fresh = positions is None
    arrays = [received] + ([] if fresh else [positions]) + [start, length]

    def kernel(*refs):
        own_kernel(*refs, fresh=fresh)

    return pl.pallas_call(
        kernel,
        out_shape=[
            jax.ShapeDtypeStruct((places, ROWS, BLK), F32),
            jax.ShapeDtypeStruct((places, 16, BLK), BF16),
        ],
        in_specs=[pl.BlockSpec(memory_space=pl.ANY)] + [vspec()] * len(arrays),
        out_specs=[vspec()] * 2,
        scratch_shapes=[
            VMEM((places, 16, BLK), BF16),
            VMEM((places, 16, BLK), BF16),
            VMEM((GROUP // 2, BLK, 2 * BLK), F32),
            SMEM(plan.shape, jnp.int32),
            pltpu.SemaphoreType.DMA(()),
        ],
        cost_estimate=tile_cost(start.shape[0] // 2),
        compiler_params=limit(8),
        name="own_contact",
    )(plan, *arrays)


def far_contact(plan, edges, edge_positions, start, length, total, slave_tab):
    places = total.shape[0]
    fresh = edge_positions is None
    edge_count = edges[0].shape[0]
    arrays = list(edges) + ([] if fresh else list(edge_positions))
    arrays += [start, length, total, slave_tab]

    def kernel(*refs):
        far_kernel(*refs, edges=edge_count, fresh=fresh)

    return pl.pallas_call(
        kernel,
        out_shape=jax.ShapeDtypeStruct((places, 1, 3 * BLK), F32),
        in_specs=[pl.BlockSpec(memory_space=pl.ANY)] + [vspec()] * len(arrays),
        out_specs=vspec(),
        scratch_shapes=[
            VMEM((4 * edge_count, 16, BLK), BF16),
            VMEM((4 * edge_count, 16, BLK), BF16),
            VMEM((places, ROWS, BLK), F32),
            VMEM((GROUP // 2, BLK, 2 * BLK), F32),
            SMEM(plan.shape, jnp.int32),
            pltpu.SemaphoreType.DMA(()),
        ],
        cost_estimate=tile_cost(start.shape[0] // 2),
        compiler_params=limit(8),
        name="far_contact",
    )(plan, *arrays)


def side_list(list_ref, meta_ref, side):
    axis = side // 2
    low = list_ref[2 * axis : 2 * axis + 1, :]
    high = list_ref[2 * axis + 1 : 2 * axis + 2, :]
    return jnp.where(meta_ref[axis] != side % 2, high, low)


def inverse_kernel(meta_ref, list_ref, out_ref):
    blocks = out_ref.shape[0]
    block_id = lax.broadcasted_iota(jnp.int32, (blocks, BLK), 0)
    lane_id = lax.broadcasted_iota(jnp.int32, (BLK, BLK), 0)
    rank = (lax.broadcasted_iota(jnp.int32, (BLK, BLK), 1) + 1).astype(F32)
    code = jnp.full((blocks, BLK), -1, jnp.int32)
    for side in range(4):
        nodes = side_list(list_ref, meta_ref, side)
        valid = meta_ref[2 + side] > 0
        in_block = jnp.where(
            jnp.logical_and(block_id == nodes // BLK, valid), 1.0, 0.0
        ).astype(BF16)
        at_lane = jnp.where(lane_id == (nodes & (BLK - 1)), rank, 0.0).astype(BF16)
        found = lax.dot_general(
            in_block, at_lane, (((1,), (1,)), ((), ())), preferred_element_type=F32
        ).astype(jnp.int32)
        code = jnp.where(found > 0, found - 1 + side * BLK, code)
    out_ref[...] = code


def inverse(meta, lists, blocks):
    return pl.pallas_call(
        inverse_kernel,
        out_shape=jax.ShapeDtypeStruct((blocks, BLK), jnp.int32),
        in_specs=[sspec(), vspec()],
        out_specs=vspec(),
        compiler_params=limit(2),
        name="inverse",
    )(meta, lists)


def force_kernel(slot_ref, meta_ref, back_ref, first_ref, second_ref, list_ref, force_ref, *side_refs):
    half = first_ref.shape[0]
    blocks = slot_ref.shape[0]
    pad = jnp.zeros((ROWS - 3, BLK), F32)
    lanes = []
    owners = []
    for side in range(4):
        nodes = jnp.broadcast_to(side_list(list_ref, meta_ref, side), (ROWS, BLK))
        lanes.append(nodes & (BLK - 1))
        owners.append(nodes // BLK)
    sums = [jnp.zeros((ROWS, BLK), F32) for _ in range(4)]
    for k in range(blocks):
        internal = first_ref[k] if k < half else second_ref[k - half]
        tile = jnp.concatenate([load_rows(back_ref, slot_ref[k], 0, 3), pad], axis=0) - internal
        force_ref[k] = tile
    for side in range(4):
        for k in range(blocks):
            sums[side] = jnp.where(
                owners[side] == k, lane_gather(force_ref[k], lanes[side]), sums[side]
            )
    for side in range(4):
        side_refs[side][...] = sums[side]


def nodal_force(block_slot, meta, returned, internal, lists):
    blocks = 2 * internal[0].shape[0]
    return pl.pallas_call(
        force_kernel,
        out_shape=[jax.ShapeDtypeStruct((blocks, ROWS, BLK), F32)]
        + [jax.ShapeDtypeStruct((ROWS, BLK), F32)] * 4,
        in_specs=[sspec()] * 2 + [vspec()] * 4,
        out_specs=[vspec()] * 5,
        compiler_params=limit(4),
        name="force",
    )(block_slot, meta, returned, *internal, lists)


def update_kernel(*refs, send):
    if send:
        table_ref = refs[0]
        slot_ref, sem = refs[-2:]
        refs = refs[1:-2]
        load = pltpu.make_async_copy(table_ref, slot_ref, sem)
        load.start()
    force_ref = refs[0]
    near = [r[...] for r in refs[1:5]]
    code_ref, mass_ref, vel_ref, disp_ref = refs[5:9]
    if send:
        pos_ref, vel_out, disp_out, send_ref = refs[9:]
    else:
        vel_hbm, disp_hbm, vel_out, disp_out, sems = refs[9:]
    blocks = force_ref.shape[0]
    if send and send_ref.shape[0] != blocks:
        send_ref[...] = jnp.zeros(send_ref.shape, F32)
    copies = []
    for k in range(blocks):
        lanes = slice(k * BLK, (k + 1) * BLK)
        code = jnp.broadcast_to(code_ref[k : k + 1, :], (ROWS, BLK))
        index = code & (BLK - 1)
        extra = jnp.zeros((ROWS, BLK), F32)
        for side in range(4):
            inside = jnp.logical_and(code >= side * BLK, code < (side + 1) * BLK)
            extra = jnp.where(inside, lane_gather(near[side], index), extra)
        assembled = (force_ref[k] + extra)[0:6]
        vel = vel_ref[:, lanes] + TIME_STEP * mass_ref[:, lanes] * assembled
        disp = disp_ref[:, lanes] + TIME_STEP * vel
        vel_out[:, lanes] = vel
        disp_out[:, lanes] = disp
        if not send and (k + 1) % PART == 0:
            span = slice((k + 1 - PART) * BLK, (k + 1) * BLK)
            for i, (held, out) in enumerate(((vel_out, vel_hbm), (disp_out, disp_hbm))):
                copies.append(
                    pltpu.make_async_copy(
                        held.at[:, span], out.at[:, span], sems.at[i, k // PART]
                    )
                )
                copies[-1].start()
    for copy in copies:
        copy.wait()
    if send:
        load.wait()
        for k in range(blocks):
            lanes = slice(k * BLK, (k + 1) * BLK)
            store_rows(send_ref, slot_ref[k], pos_ref[:, lanes] + disp_out[0:3, lanes])


def update(block_slot, force, near, code, inv_mass, velocity, displacement, ref_pos, places):
    nodes = displacement.shape[1]
    out = [jax.ShapeDtypeStruct((6, nodes), F32)] * 2
    arrays = [force, *near, code, inv_mass, velocity, displacement]
    specs = [vspec()] * len(arrays)
    out_specs = [vspec()] * 2
    scratch = []
    if places:
        arrays = [block_slot] + arrays + [ref_pos]
        specs = [pl.BlockSpec(memory_space=pl.ANY)] + specs + [vspec()]
        scratch = [SMEM(block_slot.shape, jnp.int32), pltpu.SemaphoreType.DMA(())]
        out = out + [jax.ShapeDtypeStruct((places, 1, 3 * BLK), F32)]
        out_specs = [vspec()] * 3
    else:
        out_specs = [pl.BlockSpec(memory_space=pl.ANY)] * 2
        scratch = [VMEM((6, nodes), F32)] * 2
        scratch += [pltpu.SemaphoreType.DMA((2, nodes // BLK // PART))]

    def kernel(*refs):
        update_kernel(*refs, send=places > 0)

    return pl.pallas_call(
        kernel,
        out_shape=out,
        in_specs=specs,
        out_specs=out_specs,
        scratch_shapes=scratch,
        compiler_params=limit(6),
        name="update",
    )(*arrays)


def pair_lists(sizes):
    rows, columns = sizes
    near = [[(i, i ^ 1) for i in range(size)] for size in sizes]
    other = [(i, (i + 1) % rows if i % 2 else (i - 1) % rows) for i in range(rows)]
    flat = []
    for i in range(rows):
        for j in range(columns):
            k = j + 1 if j % 2 else j - 1
            inside = 0 <= k < columns
            flat.append((i * columns + j, i * columns + k if inside else (i ^ 1) * columns + j))
    return [("gx", near[0]), ("gx", other), ("gy", near[1]), (AXES, flat)]


def swap(values, sizes):
    moved = [
        lax.ppermute(value, axis, pairs)
        for value, (axis, pairs) in zip(values, pair_lists(sizes))
    ]
    return moved


def body(
    displacement,
    velocity,
    ref_pos,
    normals,
    inv_mass,
    connectivity,
    stiffness,
    yield_force,
    shared_nodes,
    block_slot,
    edge_slots,
    tile_pairs,
    tile_count,
    win_start,
    win_len,
):
    sizes = [lax.axis_size(axis) for axis in AXES]
    if any(size % 2 for size in sizes):
        raise ValueError("odd axis")
    places = sizes[0] * sizes[1] * CAP
    blocks = displacement.shape[1] // BLK
    edge_count = edge_slots.shape[0]
    if max(tile_pairs.shape[1], places + 4 * edge_count) >= 1 << FIELD:
        raise ValueError("field width")
    at = [lax.axis_index(axis) for axis in AXES]
    odd = [i % 2 for i in at]
    inner = [((i > 0) & (i < size - 1)).astype(jnp.int32) for i, size in zip(at, sizes)]
    slot = jnp.arange(8, dtype=jnp.int32)
    meta = jnp.ones((8,), jnp.int32)
    for i, value in ((0, 1 - odd[0]), (1, 1 - odd[1]), (3, inner[0]), (5, inner[1])):
        meta = jnp.where(slot == i, value, meta)
    levels = yield_force.reshape(-1, BLK)
    plan = None
    code = None

    def exchange(blocks_out):
        return lax.all_to_all(blocks_out, AXES, split_axis=0, concat_axis=0, tiled=True)

    def half(disp, part):
        return element_forces(disp, connectivity, stiffness, levels, part, 2)

    outgoing = prep(block_slot, displacement, ref_pos, normals, places)
    first = None
    for step in range(STEPS):
        fresh = step == 0
        received = exchange(outgoing)
        if fresh:
            internal0, plan = element_forces(
                left(displacement),
                left(connectivity),
                stiffness,
                left(levels),
                0,
                2,
                (tile_count, left(tile_pairs), meta),
                places,
            )
        else:
            internal0 = half(displacement, 0)
        received, internal0, plan = lax.optimization_barrier((received, internal0, plan))
        near = swap([edge_rows(edge_slots, received)] * 4, sizes)
        if fresh:
            first = (received, near)
        total, slave_tab = own_contact(
            plan, first[0], None if fresh else received, win_start, win_len
        )
        box_force = far_contact(
            plan, first[1], None if fresh else near, win_start, win_len, total, slave_tab
        )
        box_force, later = lax.optimization_barrier((box_force, displacement))
        returned = exchange(box_force)
        internal1 = half(later, 1)
        force, *sides = nodal_force(
            block_slot, meta, returned, (internal0, internal1), shared_nodes
        )
        if code is None:
            sides, lists = lax.optimization_barrier((sides, shared_nodes))
            code = inverse(meta, lists, blocks)
        incoming = swap(sides, sizes)
        last = step == STEPS - 1
        out = update(
            block_slot,
            force,
            incoming,
            code,
            inv_mass,
            velocity,
            displacement,
            ref_pos,
            0 if last else places,
        )
        velocity, displacement = out[0:2]
        if not last:
            outgoing = out[2]
    return (displacement, velocity)


def solution(mesh):
    split_last = P(None, AXES)
    placed = (
        split_last,
        split_last,
        split_last,
        split_last,
        split_last,
        split_last,
        P(None, None, AXES),
        P(AXES),
        split_last,
        P(AXES),
        P(AXES),
        split_last,
        P(AXES),
        P(AXES, None),
        P(AXES, None),
    )
    return jax.shard_map(
        body,
        mesh=mesh,
        in_specs=placed,
        out_specs=(split_last, split_last),
        check_vma=False,
    )
```
